32 devices in a mesh: sky: 8 (over z, core), tm: 4 (over y, x).
Axes of the slice: x: 2, y: 2, z: 4, core: 2. Of those that a mesh axis runs over, the one named last changes fastest.
Arguments:
- residual: float32 [8, 4, 8, 512], P('sky', 'tm'), may hold values from -22 to 22
- counts: int32 [8, 4, 8], P('sky', 'tm'), may hold values from 128 to 512, as said below
- source_index: int32 [8, 4, 8, 512], P('sky', 'tm'), may hold values from 0 to 255
- source_partials: bfloat16 [5, 8, 4, 8, 512], P(None, 'sky', 'tm'), may hold values from -6 to 6
- segment_index: int32 [8, 4, 8, 512], P('sky', 'tm'), may hold values from 0 to 127
- attitude_partials: bfloat16 [4, 8, 4, 8, 512], P(None, 'sky', 'tm'), may hold values from -6 to 6
- unit_index: int32 [8, 4, 8, 512], P('sky', 'tm'), may hold values from 0 to 61
- knot_base: int32 [8, 4, 8, 512], P('sky', 'tm'), may hold values from 0 to 112
- calib_partials: bfloat16 [16, 8, 4, 8, 512], P(None, 'sky', 'tm'), may hold values from -6 to 6
Outputs:
- corrected: float32 [8, 4, 8, 512], P('sky', 'tm')
- source_params: float32 [5, 8192], P(None, ('sky', 'tm'))
- attitude_params: float32 [4, 4096], P(None, ('sky', 'tm'))
The draws below stay inside these ranges and needn't reach their ends.
Inputs may be any that keep to these rules, and one draw needn't show every extreme that they name: `counts`: at most 512 live slots from one zone and row toward one time owner; some zone fills all 512 in every draw; live slots come first.
All inputs are finite; a program needn't handle non-finite values.
Results may differ from the reference program's by a relative error of at most 0.0007.
Values sent between devices are 32-bit elements; how exact they have to be, the bound alone decides.
A program may use at most 64 MiB of HBM per device.

```python
import jax
import jax.numpy as jnp
from jax import lax

CAP = 512
SRC_DEV = 256
SEG_DEV = 128
KNOT_DEV = 113
UNITS = 62
SPLINE = 16
SRC_PARAMS = 5
ATT_PARAMS = 4
ITERS = 2
SOURCES = 8192
SEGMENTS = 4096
N_SKY = 8
N_TM = 4


def draw_counts(key, part):
    dense_key, full_key, noise_key = jax.random.split(key, 3)
    density = jax.random.randint(dense_key, (N_SKY,), 1, 5)
    crowded = jax.random.randint(full_key, (), 0, N_SKY)
    density = jnp.where(jnp.arange(N_SKY) == crowded, 4, density)
    quarter = CAP // 4
    jitter = jax.random.randint(noise_key, (N_SKY, N_TM, N_SKY), 0, quarter + 1)
    return jnp.minimum(density[:, None, None] * quarter + jitter, CAP).astype(jnp.int32)


def draw_residual(key, part):
    value_key = jax.random.fold_in(key, 0)
    layout = (N_SKY, N_TM, N_SKY, CAP)
    zone_ramp = 1.0 + 2.0 * jnp.arange(N_SKY, dtype=jnp.float32) / max(N_SKY - 1, 1)
    values = jax.random.truncated_normal(value_key, -4.0, 4.0, layout, jnp.float32)
    return values * zone_ramp[:, None, None, None]


def set_ends(result, own_key, low, largest):
    longest = result.shape.index(max(result.shape))
    spots = []
    for shift in (0, 1):
        where = [jax.random.randint(jax.random.fold_in(own_key, axis), (), 0, length) for axis, length in enumerate(result.shape)]
        where[longest] = (where[longest] + shift) % result.shape[longest]
        spots.append(tuple(where))
    return result.at[spots[0]].set(low).at[spots[1]].set(largest)


def block_levels(rng, extent, pieces, least, largest):
    level = 1.0
    for dim, shards_of in pieces:
        heights = jax.random.uniform(jax.random.fold_in(jax.random.fold_in(rng, 6), dim), (shards_of,), jnp.float32, least / len(pieces), largest / len(pieces))
        level = level * jnp.repeat(jnp.exp(heights), extent[dim] // shards_of).reshape((-1,) + (1,) * (len(extent) - 1 - dim))
    return level


def bell_draw(own_key, shape, width, most, cuts=(), held_as=jnp.bfloat16):
    array = width * jax.random.normal(own_key, shape, jnp.float32)
    if cuts:
        array = array * block_levels(own_key, shape, cuts, -0.22, 0.18)
    return jnp.clip(array, -most, most).astype(held_as)


def setup_inputs(seed: int = 0) -> dict:
    streams_of = jax.random.split(jax.random.key(seed), 10)
    return {
        "residual": draw_residual(jax.random.fold_in(streams_of[9], 71), 0),
        "counts": draw_counts(jax.random.fold_in(streams_of[9], 71), 0),
        "source_index": set_ends(jax.random.randint(streams_of[2], (N_SKY, N_TM, N_SKY, CAP), 0, SRC_DEV), jax.random.fold_in(streams_of[2], 1), 0, SRC_DEV - 1).astype(jnp.int32),
        "source_partials": bell_draw(streams_of[3], (SRC_PARAMS, N_SKY, N_TM, N_SKY, CAP), 1.0, 6.0, ((1, 8), (2, 4))),
        "segment_index": set_ends(jax.random.randint(streams_of[4], (N_SKY, N_TM, N_SKY, CAP), 0, SEG_DEV), jax.random.fold_in(streams_of[4], 1), 0, SEG_DEV - 1).astype(jnp.int32),
        "attitude_partials": bell_draw(streams_of[5], (ATT_PARAMS, N_SKY, N_TM, N_SKY, CAP), 1.0, 6.0, ((1, 8), (2, 4))),
        "unit_index": set_ends(jax.random.randint(streams_of[6], (N_SKY, N_TM, N_SKY, CAP), 0, UNITS), jax.random.fold_in(streams_of[6], 1), 0, UNITS - 1).astype(jnp.int32),
        "knot_base": set_ends(jax.random.randint(streams_of[7], (N_SKY, N_TM, N_SKY, CAP), 0, KNOT_DEV), jax.random.fold_in(streams_of[7], 1), 0, KNOT_DEV - 1).astype(jnp.int32),
        "calib_partials": bell_draw(streams_of[8], (SPLINE, N_SKY, N_TM, N_SKY, CAP), 1.0, 6.0, ((1, 8), (2, 4))),
    }


clip_factor = 1.5
ridge = 1.0

def block_solve(values, partials, weights, labels, groups, count):
    outer = weights[:, None, None] * partials[:, :, None] * partials[:, None, :]
    matrix = jax.ops.segment_sum(outer, labels, num_segments=groups) + ridge * jnp.eye(count, dtype=jnp.float32)[None]
    right = jax.ops.segment_sum(weights[:, None] * partials * values[:, None], labels, num_segments=groups)
    return jnp.linalg.solve(matrix, right[:, :, None])[:, :, 0]

def reference(residual, counts, source_index, source_partials, segment_index, attitude_partials, unit_index, knot_base, calib_partials):
    knots_all = KNOT_DEV * N_TM + SPLINE - 1
    per_zone = N_TM * N_SKY * CAP
    slot_ids = jnp.arange(CAP, dtype=jnp.int32)
    live_mask = (slot_ids[None, None, None, :] < counts[:, :, :, None]).astype(jnp.float32)
    row_ids = jnp.arange(N_TM, dtype=jnp.int32)[:, None, None]
    offsets = jnp.arange(SPLINE, dtype=jnp.int32)
    current = residual * live_mask
    live_turned = jnp.transpose(live_mask, (2, 1, 0, 3))
    src_moved = jnp.moveaxis(source_partials, 0, 1)
    att_moved = jnp.moveaxis(attitude_partials, 0, 1)
    cal_moved = jnp.moveaxis(calib_partials, 0, 1)
    src_total = jnp.zeros((N_SKY, N_TM * SRC_DEV, SRC_PARAMS), jnp.float32)
    att_total = jnp.zeros((N_SKY, N_TM * SEG_DEV, ATT_PARAMS), jnp.float32)
    for iteration in range(ITERS):
        bound = clip_factor * (jnp.sum(jnp.abs(current) * live_mask) / jnp.sum(live_mask))

        def source_zone(operands):
            values, live_zone, partials, labels = operands
            flat_live = live_zone.reshape(per_zone)
            flat_values = values.reshape(per_zone)
            flat_parts = partials.reshape(SRC_PARAMS, per_zone).T.astype(jnp.float32)
            flat_labels = (row_ids * SRC_DEV + labels).reshape(per_zone)
            weights = flat_live * bound / jnp.maximum(jnp.abs(flat_values), bound)
            update = block_solve(flat_values, flat_parts, weights, flat_labels, N_TM * SRC_DEV, SRC_PARAMS)
            fitted = jnp.sum(flat_parts * update[flat_labels], axis=1)
            return ((flat_values - flat_live * fitted).reshape(N_TM, N_SKY, CAP), update)
        current, src_update = lax.map(source_zone, (current, live_mask, src_moved, source_index))
        src_total = src_total + src_update
        turned = jnp.transpose(current, (2, 1, 0, 3))

        def time_zone(operands):
            values, live_zone, att_part, seg_labels, cal_part, unit_labels, base_labels = operands
            flat_live = live_zone.reshape(per_zone)
            flat_values = values.reshape(per_zone)
            weights = flat_live * bound / jnp.maximum(jnp.abs(flat_values), bound)
            att_flat = att_part.reshape(ATT_PARAMS, per_zone).T.astype(jnp.float32)
            seg_flat = (row_ids * SEG_DEV + seg_labels).reshape(per_zone)
            att_update = block_solve(flat_values, att_flat, weights, seg_flat, N_TM * SEG_DEV, ATT_PARAMS)
            flat_values = flat_values - flat_live * jnp.sum(att_flat * att_update[seg_flat], axis=1)
            first_knot = unit_labels.reshape(per_zone) * knots_all + (row_ids * KNOT_DEV + base_labels).reshape(per_zone)
            knot_ids = (first_knot[:, None] + offsets[None, :]).astype(jnp.int32)
            cal_flat = cal_part.reshape(SPLINE, per_zone).T.astype(jnp.float32)
            gsum = jax.ops.segment_sum((cal_flat * (weights * flat_values)[:, None]).reshape(-1), knot_ids.reshape(-1), num_segments=UNITS * knots_all)
            hsum = jax.ops.segment_sum((weights[:, None] * cal_flat * cal_flat).reshape(-1), knot_ids.reshape(-1), num_segments=UNITS * knots_all)
            coefficients = gsum / (hsum + ridge)
            fitted = jnp.sum(cal_flat * coefficients[knot_ids], axis=1)
            return ((flat_values - flat_live * fitted).reshape(N_TM, N_SKY, CAP), att_update)
        turned, att_update = lax.map(time_zone, (turned, live_turned, att_moved, segment_index, cal_moved, unit_index, knot_base))
        att_total = att_total + att_update
        current = jnp.transpose(turned, (2, 1, 0, 3))
    source_params = src_total.reshape(SOURCES, SRC_PARAMS).T
    attitude_params = att_total.reshape(SEGMENTS, ATT_PARAMS).T
    return (current, source_params, attitude_params)
```

```python
import functools

import jax
import jax.numpy as jnp
from jax import lax
from jax.experimental import pallas as pl
from jax.experimental.pallas import tpu as pltpu
from jax.sharding import PartitionSpec as P

SRC_DEV = 256
SEG_DEV = 128
KNOT_DEV = 113
UNITS = 62
SPLINE = 16
SRC_PARAMS = 5
ATT_PARAMS = 4
ITERS = 2

clip_factor = 1.5
ridge = 1.0

LANES = 128
F32 = jnp.float32
BF16 = jnp.bfloat16
MESH = pl.DeviceIdType.MESH
UNIT_ROWS = -(-UNITS // 64) * 64
EXTENT = -(-(KNOT_DEV + SPLINE - 1) // LANES) * LANES
RIM = SPLINE


def lower_pairs(order):
    return [(row_at, col_at) for row_at in range(order) for col_at in range(row_at + 1)]


def rows_of(order):
    return -(-(order + len(lower_pairs(order))) // 8) * 8


def split_rows(value):
    high = value.astype(BF16).astype(F32)
    return jnp.concatenate([high, value - high], axis=0).astype(BF16)


def dot_nt(left, right):
    return lax.dot_general(left, right, (((1,), (1,)), ((), ())), preferred_element_type=F32)


def dot_nn(left, right):
    return lax.dot_general(left, right, (((1,), (0,)), ((), ())), preferred_element_type=F32)


def in_groups(count, size, body, carry):
    if count <= 16:
        for start in range(0, count, size):
            carry = body(list(range(start, min(start + size, count))), carry)
        return carry
    size = size if count % size == 0 else 1

    def group(number, carry):
        return body([number * size + at for at in range(size)], carry)

    return lax.fori_loop(0, count // size, group, carry)


def add_all(values):
    values = list(values)
    while len(values) > 1:
        values = [
            values[at] + values[at + 1] if at + 1 < len(values) else values[at]
            for at in range(0, len(values), 2)
        ]
    return values[0]


def each(count, body, carry):
    if count <= 16:
        for number in range(count):
            carry = body(number, carry)
        return carry
    return lax.fori_loop(0, count, body, carry)


def block_solve(sums, order):
    pairs = lower_pairs(order)
    matrix = {}
    for number, (row_at, col_at) in enumerate(pairs):
        at = order + number
        matrix[row_at, col_at] = sums[at : at + 1] + (ridge if row_at == col_at else 0.0)
    right = [sums[at : at + 1] for at in range(order)]
    inverse = []
    for pivot in range(order):
        inverse.append(1.0 / matrix[pivot, pivot])
        for row_at in range(pivot + 1, order):
            ratio = matrix[row_at, pivot] * inverse[pivot]
            for col_at in range(pivot + 1, row_at + 1):
                matrix[row_at, col_at] = matrix[row_at, col_at] - ratio * matrix[col_at, pivot]
            right[row_at] = right[row_at] - ratio * right[pivot]
    solved = [None] * order
    for row_at in reversed(range(order)):
        running = right[row_at]
        for inner_at in range(row_at + 1, order):
            running = running - matrix[inner_at, row_at] * solved[inner_at]
        solved[row_at] = running * inverse[row_at]
    return jnp.concatenate(solved, axis=0)


def store_products(partials_ref, prods, order):
    values = [partials_ref[at].astype(F32) for at in range(order)]
    listed = values + [values[row_at] * values[col_at] for row_at, col_at in lower_pairs(order)]
    while len(listed) < prods.shape[1]:
        listed.append(jnp.zeros_like(values[0]))
    for at, value in enumerate(listed):
        prods[:, at, :] = value


def kernel(
    n_sky,
    n_tm,
    res_hbm,
    cnt_hbm,
    src_hbm,
    sp_hbm,
    seg_hbm,
    ap_hbm,
    unit_hbm,
    base_hbm,
    cp_hbm,
    out_ref,
    srcp_ref,
    attp_ref,
    res_ref,
    cnt_ref,
    src_ref,
    sp_ref,
    seg_ref,
    ap_ref,
    unit_ref,
    base_ref,
    cp_ref,
    in_sems,
    src_hot,
    seg_hot,
    src_side,
    seg_side,
    unit_hot,
    placed,
    sq_high,
    sq_low,
    rim_part,
    rim_square,
    src_prods,
    att_prods,
    cal_rows,
    r_src,
    r_time,
    v_time,
    live_time,
    fit_time,
    stat_send,
    stat_recv,
    abs_send,
    abs_recv,
    fwd_send,
    fwd_recv,
    back_send,
    back_recv,
    rim_send,
    rim_recv,
    stat_sems,
    abs_sems,
    fwd_ssem,
    fwd_rsem,
    back_ssem,
    back_rsem,
    rim_ssem,
    rim_rsem,
):
    zones, cap = res_ref.shape
    tiles = cap // LANES
    devices = n_sky * n_tm
    sky = lax.axis_index("sky")
    tm = lax.axis_index("tm")
    me = sky * n_tm + tm

    def wrapped(value, size):
        return jnp.where(value >= size, value - size, value)

    lower = sky < n_sky // 2

    def far_first(number):
        down = n_sky - 1 - number
        down = jnp.where(down <= sky, down - 1, down)
        up = jnp.where(number >= sky, number + 1, number)
        peer = jnp.where(lower, down, up)
        if isinstance(number, int):
            return sky if number == n_sky - 1 else peer
        return jnp.where(number == n_sky - 1, sky, peer)

    def every_other(body):
        if devices <= 64:
            if n_tm & (n_tm - 1):
                tms = [wrapped(tm + at, n_tm) for at in range(n_tm)]
            else:
                tms = [tm ^ at for at in range(n_tm)]
            for number in range(n_sky):
                other = far_first(number)
                for at in reversed(range(n_tm)):
                    if number < n_sky - 1 or at:
                        body(other, tms[at])
            return

        @pl.loop(1, devices)
        def _(step):
            flat = lax.rem(me + step, devices)
            body(flat // n_tm, lax.rem(flat, n_tm))

    arriving = [
        pltpu.make_async_copy(source, target, in_sems.at[number])
        for number, (source, target) in enumerate(
            (
                (res_hbm, res_ref),
                (cnt_hbm, cnt_ref),
                (src_hbm, src_ref),
                (sp_hbm, sp_ref),
                (seg_hbm, seg_ref),
                (ap_hbm, ap_ref),
                (unit_hbm, unit_ref),
                (base_hbm, base_ref),
                (cp_hbm, cp_ref),
            )
        )
    ]
    for copy in arriving:
        copy.start()

    barrier = pltpu.get_barrier_semaphore()

    def greet(to_sky, to_tm):
        pl.semaphore_signal(
            barrier, inc=1, device_id={"sky": to_sky, "tm": to_tm}, device_id_type=MESH
        )

    every_other(greet)

    lane_row = lax.broadcasted_iota(jnp.int32, (1, cap), 1)

    def fold(row):
        total = row[:, :LANES]
        for at in range(1, tiles):
            total = total + row[:, at * LANES : (at + 1) * LANES]
        return total

    def widen(row):
        return jnp.concatenate([row] * tiles, axis=1) if tiles > 1 else row

    def live_of(zone):
        return (lane_row < cnt_ref[zone]).astype(F32)

    for copy in arriving[:2]:
        copy.wait()

    def first_stats(zone, carry):
        sums, lives = carry
        live = live_of(zone)
        row = res_ref[pl.ds(zone, 1), :] * live
        r_src[zone] = row
        stat_send[zone, :, 2 * LANES :] = jnp.full((1, LANES), cnt_ref[zone], jnp.int32).astype(F32)
        return sums + fold(jnp.abs(row)), lives + fold(live)

    zero_row = jnp.zeros((1, LANES), F32)
    sums, lives = each(zones, first_stats, (zero_row, zero_row))

    def put_stats(zone, carry):
        stat_send[zone, :, :LANES] = sums
        stat_send[zone, :, LANES : 2 * LANES] = lives
        return carry

    each(zones, put_stats, 0)
    stat_recv[me] = stat_send[sky]
    pl.semaphore_wait(barrier, devices - 1)

    def send_stats(to_sky, to_tm):
        pltpu.make_async_remote_copy(
            src_ref=stat_send.at[to_sky],
            dst_ref=stat_recv.at[me],
            send_sem=stat_sems.at[0],
            recv_sem=stat_sems.at[1],
            device_id={"sky": to_sky, "tm": to_tm},
            device_id_type=MESH,
        ).start()

    every_other(send_stats)

    for copy in arriving[2:]:
        copy.wait()

    store_products(sp_ref, src_prods, SRC_PARAMS)
    store_products(ap_ref, att_prods, ATT_PARAMS)
    for at in range(SPLINE):
        cal_rows[:, at, :] = cp_ref[at].astype(F32)

    def hot_rows(rows, labels):
        number = lax.broadcasted_iota(jnp.int32, (rows, cap), 0)
        return jnp.where(number == labels, 1.0, 0.0).astype(BF16)

    def tables(zone, carry):
        for labels_ref, hot_ref, side_ref in ((src_ref, src_hot, src_side), (seg_ref, seg_hot, seg_side)):
            labels = labels_ref[pl.ds(zone, 1), :]
            groups = hot_ref.shape[1]
            above = labels >= groups
            hot_ref[zone] = hot_rows(groups, jnp.where(above, labels - groups, labels))
            side_ref[zone] = jnp.where(above, 1.0, 0.0)
        hot = hot_rows(UNIT_ROWS, unit_ref[pl.ds(zone, 1), :])
        unit_hot[zone] = jnp.concatenate([hot, hot], axis=0)
        base = jnp.broadcast_to(base_ref[pl.ds(zone, 1), :], (8, cap))
        turned = []
        for part in range(SPLINE // 8):
            rows = cal_rows[zone, part * 8 : part * 8 + 8, :]
            for bit in (1, 2, 4):
                rows = jnp.where((base & bit) != 0, pltpu.roll(rows, bit, 0), rows)
            turned.append(rows)
        reach = lax.shift_right_arithmetic(
            lax.broadcasted_iota(jnp.int32, (8, cap), 0) - base, jnp.int32(3)
        )
        pieces = []
        for group in range(EXTENT // 8):
            piece = jnp.zeros((8, cap), F32)
            for part, rows in enumerate(turned):
                piece = jnp.where(reach == part - group, rows, piece)
            pieces.append(piece)
        spread = jnp.concatenate(pieces, axis=0)
        placed[zone] = spread.astype(BF16)
        square = spread * spread
        rim_part[zone] = jnp.concatenate([spread[:RIM], spread[EXTENT - RIM :]], axis=0)
        rim_square[zone] = jnp.concatenate([square[:RIM], square[EXTENT - RIM :]], axis=0)
        high = square.astype(BF16)
        sq_high[zone] = high
        sq_low[zone] = (square - high.astype(F32)).astype(BF16)
        return carry

    each(zones, tables, 0)

    whole_stat = stat_recv.at[pl.ds(0, devices - 1)]
    pltpu.make_async_copy(whole_stat, whole_stat, stat_sems.at[1]).wait()
    stats = jnp.sum(stat_recv[...], axis=0)
    live_total = jnp.sum(stats[:, LANES : 2 * LANES], axis=1, keepdims=True)
    abs_total = jnp.sum(stats[:, :LANES], axis=1, keepdims=True)

    def time_live(zone, carry):
        counts = stat_recv[zone * n_tm + tm][:, 2 * LANES :]
        live_time[zone] = (lane_row.astype(F32) < widen(counts)).astype(F32)
        return carry

    each(zones, time_live, 0)

    src_total = jnp.zeros((SRC_PARAMS, SRC_DEV), F32)
    att_total = jnp.zeros((ATT_PARAMS, SEG_DEV), F32)

    def group_sums(zone, prods, hot, side, order, weights, row):
        number = lax.broadcasted_iota(jnp.int32, (8, cap), 0)
        scaled = jnp.concatenate(
            [
                prods[zone, :8, :] * jnp.where(number < order, weights * row, weights),
                prods[zone, 8:, :] * weights,
            ],
            axis=0,
        )
        tall = split_rows(scaled)
        above = tall * side[zone].astype(BF16)
        return dot_nt(jnp.concatenate([tall - above, above], axis=0), hot[zone])

    def group_totals(both, order):
        rows = both.shape[0] // 4
        both = jnp.concatenate([both[: 2 * rows], both[2 * rows :]], axis=1)
        return both[:rows] + both[rows:]

    def padded_steps(step, order):
        groups = step.shape[1]
        tall = split_rows(jnp.concatenate([step, jnp.zeros((8 - order, groups), F32)], axis=0))
        return jnp.concatenate([tall[:, : groups // 2], tall[:, groups // 2 :]], axis=0)

    def fitted(zones_at, steps, prods, hot, side):
        picked = [dot_nn(steps, hot[zone]) for zone in zones_at]
        fits = []
        for zone, values in zip(zones_at, picked):
            values = jnp.where(side[zone] > 0.5, values[16:24] + values[24:], values[:8] + values[8:16])
            fits.append(jnp.sum(values * prods[zone, :8, :], axis=0, keepdims=True))
        return fits

    def zone_copy(send, recv, ssem, rsem, peer):
        return pltpu.make_async_remote_copy(
            src_ref=send.at[peer],
            dst_ref=recv.at[sky],
            send_sem=ssem,
            recv_sem=rsem,
            device_id={"sky": peer, "tm": tm},
            device_id_type=MESH,
        )

    wide = 2 * UNIT_ROWS

    def unit_weights(zone, row):
        high = row.astype(BF16).astype(F32)
        tall = jnp.concatenate(
            [
                jnp.broadcast_to(high, (UNIT_ROWS, cap)),
                jnp.broadcast_to(row - high, (UNIT_ROWS, cap)),
            ],
            axis=0,
        ).astype(BF16)
        return unit_hot[zone] * tall

    for it in range(ITERS):
        bound = clip_factor * (abs_total / live_total)

        def src_sums(numbers, total):
            rows = [r_src[zone] for zone in numbers]
            weights = [
                live_of(zone) * bound / jnp.maximum(jnp.abs(row), bound)
                for zone, row in zip(numbers, rows)
            ]
            return total + add_all(
                group_sums(zone, src_prods, src_hot, src_side, SRC_PARAMS, weight, row)
                for zone, weight, row in zip(numbers, weights, rows)
            )

        both = in_groups(
            zones, 8, src_sums, jnp.zeros((4 * rows_of(SRC_PARAMS), SRC_DEV // 2), F32)
        )
        step_x = block_solve(group_totals(both, SRC_PARAMS), SRC_PARAMS)
        src_total = src_total + step_x
        steps_x = padded_steps(step_x, SRC_PARAMS)

        def src_out(numbers, carry):
            zones_at = [far_first(number) for number in numbers]
            fits = fitted(zones_at, steps_x, src_prods, src_hot, src_side)
            for zone, fit in zip(zones_at, fits):
                fwd_send[it, zone] = r_src[zone] - live_of(zone) * fit

            for number, zone in zip(numbers, zones_at):

                def send():
                    zone_copy(
                        fwd_send.at[it], fwd_recv.at[it], fwd_ssem.at[it], fwd_rsem.at[it, sky], zone
                    ).start()

                if isinstance(number, int):
                    if number < n_sky - 1:
                        send()
                else:
                    pl.when(number < n_sky - 1)(send)
            return carry

        in_groups(zones, 4, src_out, 0)
        fwd_recv[it, sky] = fwd_send[it, sky]

        def att_sums(numbers, total):
            zones_at = [far_first(n_sky - 1 - number) for number in numbers]
            for number, zone in zip(numbers, zones_at):

                def arrive():
                    zone_copy(
                        fwd_send.at[it], fwd_recv.at[it], fwd_ssem.at[it], fwd_rsem.at[it, zone], zone
                    ).wait_recv()

                if isinstance(number, int):
                    if number > 0:
                        arrive()
                else:
                    pl.when(number > 0)(arrive)
            rows = [fwd_recv[it, zone] for zone in zones_at]
            weights = [
                live_time[zone] * bound / jnp.maximum(jnp.abs(row), bound)
                for zone, row in zip(zones_at, rows)
            ]
            for zone, weight in zip(zones_at, weights):
                v_time[zone] = weight
            att_part, h_part = total
            att_part = att_part + add_all(
                group_sums(zone, att_prods, seg_hot, seg_side, ATT_PARAMS, weight, row)
                for zone, weight, row in zip(zones_at, weights, rows)
            )
            h_part = h_part + add_all(
                dot_nt(split_rows(rim_square[zone] * weight), unit_hot[zone, :UNIT_ROWS, :])
                for zone, weight in zip(zones_at, weights)
            )
            return att_part, h_part

        rim_blank = jnp.zeros((4 * RIM, UNIT_ROWS), F32)
        both, h_rims = in_groups(
            zones,
            2,
            att_sums,
            (jnp.zeros((4 * rows_of(ATT_PARAMS), SEG_DEV // 2), F32), rim_blank),
        )
        step_y = block_solve(group_totals(both, ATT_PARAMS), ATT_PARAMS)
        att_total = att_total + step_y
        steps_y = padded_steps(step_y, ATT_PARAMS)

        def rim_sums(numbers, total):
            fits = fitted(numbers, steps_y, att_prods, seg_hot, seg_side)
            rows = [
                fwd_recv[it, zone] - live_time[zone] * fit for zone, fit in zip(numbers, fits)
            ]
            for zone, row in zip(numbers, rows):
                r_time[zone] = row
            return total + add_all(
                dot_nt(split_rows(rim_part[zone] * (v_time[zone] * row)), unit_hot[zone, :UNIT_ROWS, :])
                for zone, row in zip(numbers, rows)
            )

        g_rims = in_groups(zones, 8, rim_sums, rim_blank)
        g_rims = g_rims[: 2 * RIM] + g_rims[2 * RIM :]
        h_rims = h_rims[: 2 * RIM] + h_rims[2 * RIM :]

        def joined(g_part, h_part):
            g_part = g_part + pltpu.roll(g_part, UNIT_ROWS, 1)
            left_half = lax.broadcasted_iota(jnp.int32, g_part.shape, 1) < UNIT_ROWS
            return jnp.where(left_half, g_part, h_part)

        def coefs_of(knots):
            ratio = knots / (pltpu.roll(knots, UNIT_ROWS, 1) + ridge)
            left_half = lax.broadcasted_iota(jnp.int32, knots.shape, 1) < UNIT_ROWS
            ratio = jnp.where(left_half, ratio, 0.0)
            high = ratio.astype(BF16).astype(F32)
            return (high + pltpu.roll(ratio - high, UNIT_ROWS, 1)).astype(BF16)

        for way, rows in ((0, slice(RIM, 2 * RIM)), (1, slice(0, RIM))):
            rim_send[it, way, 0, :, :UNIT_ROWS] = g_rims[rows]
            rim_send[it, way, 1, :, :UNIT_ROWS] = h_rims[rows]
        rims = []
        for way, by in ((0, 1), (1, n_tm - 1)):
            copy = pltpu.make_async_remote_copy(
                src_ref=rim_send.at[it, way],
                dst_ref=rim_recv.at[it, way],
                send_sem=rim_ssem.at[it, way],
                recv_sem=rim_rsem.at[it, way],
                device_id={"sky": sky, "tm": lax.rem(tm + by, n_tm)},
                device_id_type=MESH,
            )
            copy.start()
            rims.append(copy)

        inner = slice(RIM, EXTENT - RIM)

        def inner_sums(numbers, total):
            g_part, h_part = total
            for zone in numbers:
                weight = v_time[zone]
                tall = unit_weights(zone, weight)
                h_part = h_part + dot_nt(sq_high[zone, inner, :], tall) + dot_nt(sq_low[zone, inner, :], tall)
                g_part = g_part + dot_nt(placed[zone, inner, :], unit_weights(zone, weight * r_time[zone]))
            return g_part, h_part

        middle = jnp.zeros((EXTENT - 2 * RIM, wide), F32)
        middle, h_total = in_groups(zones, 8, inner_sums, (middle, middle))
        h_total = h_total + pltpu.roll(h_total, UNIT_ROWS, 1)
        inner_coefs = coefs_of(joined(middle, h_total))

        def inner_fit(zone, carry):
            picked = dot_nn(inner_coefs, unit_hot[zone])
            fit = picked * placed[zone, inner, :].astype(F32)
            fit_time[zone] = jnp.sum(fit.reshape(-1, 8, cap), axis=0)
            return carry

        each(zones, inner_fit, 0)

        for copy in rims:
            copy.wait_recv()
        lead = KNOT_DEV - (EXTENT - RIM)
        shared = SPLINE - 1
        from_last = jnp.where(tm > 0, rim_recv[it, 0], 0.0)[:, lead : lead + shared, :UNIT_ROWS]
        from_next = jnp.where(tm < n_tm - 1, rim_recv[it, 1], 0.0)[:, :shared, :UNIT_ROWS]

        def added(rims, at):
            blank = lambda rows: [jnp.zeros((rows, UNIT_ROWS), F32)] if rows else []
            return rims + jnp.concatenate(
                [from_last[at]]
                + blank(RIM - shared + lead)
                + [from_next[at]]
                + blank(RIM - lead - shared),
                axis=0,
            )

        rim_coefs = split_rows(added(g_rims, 0) / (added(h_rims, 1) + ridge))

        last = it == ITERS - 1

        def cal_out(numbers, total):
            picked = [dot_nn(rim_coefs, unit_hot[zone, :UNIT_ROWS, :]) for zone in numbers]
            rows = []
            for zone, values in zip(numbers, picked):
                fit = (values[: 2 * RIM] + values[2 * RIM :]) * rim_part[zone]
                fit = jnp.sum(fit.reshape(-1, 8, cap), axis=0) + fit_time[zone]
                fit = jnp.sum(fit, axis=0, keepdims=True)
                rows.append(r_time[zone] - live_time[zone] * fit)
            for zone, row in zip(numbers, rows):
                back_send[it, zone] = row
            return total + add_all(fold(jnp.abs(row)) for row in rows)

        abs_sum = in_groups(zones, 8, cal_out, zero_row)

        if not last:
            abs_send[it] = abs_sum
            abs_recv[it, me] = abs_sum

            def send_abs(to_sky, to_tm):
                pltpu.make_async_remote_copy(
                    src_ref=abs_send.at[it],
                    dst_ref=abs_recv.at[it, me],
                    send_sem=abs_sems.at[it, 0],
                    recv_sem=abs_sems.at[it, 1],
                    device_id={"sky": to_sky, "tm": to_tm},
                    device_id_type=MESH,
                ).start()

            every_other(send_abs)

        def back_out(number, carry):
            zone_copy(
                back_send.at[it], back_recv.at[it], back_ssem.at[it], back_rsem.at[it], far_first(number)
            ).start()
            return carry

        each(n_sky - 1, back_out, 0)
        back_recv[it, sky] = back_send[it, sky]

        if not last:
            whole = abs_recv.at[it, pl.ds(0, devices - 1)]
            pltpu.make_async_copy(whole, whole, abs_sems.at[it, 1]).wait()
            abs_total = jnp.sum(jnp.sum(abs_recv[it], axis=0), axis=1, keepdims=True)

        whole = back_recv.at[it, pl.ds(0, n_sky - 1)]
        pltpu.make_async_copy(whole, whole, back_rsem.at[it]).wait()

        def put_back(zone, carry):
            if last:
                out_ref[pl.ds(zone, 1), :] = back_recv[it, zone]
            else:
                r_src[zone] = back_recv[it, zone]
            return carry

        each(zones, put_back, 0)

    srcp_ref[...] = src_total
    attp_ref[...] = att_total

    pltpu.make_async_copy(whole_stat, whole_stat, stat_sems.at[0]).wait()
    for it in range(ITERS):
        if it < ITERS - 1:
            whole = abs_recv.at[it, pl.ds(0, devices - 1)]
            pltpu.make_async_copy(whole, whole, abs_sems.at[it, 0]).wait()

        for recv, ssem in ((fwd_recv, fwd_ssem), (back_recv, back_ssem)):
            whole = recv.at[it, pl.ds(0, n_sky - 1)]
            pltpu.make_async_copy(whole, whole, ssem.at[it]).wait()
        for way, by in ((0, 1), (1, n_tm - 1)):
            pltpu.make_async_remote_copy(
                src_ref=rim_send.at[it, way],
                dst_ref=rim_recv.at[it, way],
                send_sem=rim_ssem.at[it, way],
                recv_sem=rim_rsem.at[it, way],
                device_id={"sky": sky, "tm": lax.rem(tm + by, n_tm)},
                device_id_type=MESH,
            ).wait_send()


def write_out(count, *refs):
    sems = refs[-1]
    copies = [
        pltpu.make_async_copy(refs[at], refs[count + at], sems.at[at]) for at in range(count)
    ]
    for copy in copies:
        copy.start()
    for copy in copies:
        copy.wait()


def shards(
    residual,
    counts,
    source_index,
    source_partials,
    segment_index,
    attitude_partials,
    unit_index,
    knot_base,
    calib_partials,
    n_sky,
    n_tm,
):
    zones, capacity = residual.shape[2:]
    cap = -(-capacity // LANES) * LANES
    devices = n_sky * n_tm

    def flat(value):
        value = value.reshape(value.shape[:-4] + (zones, capacity))
        if cap != capacity:
            value = jnp.pad(value, [(0, 0)] * (value.ndim - 1) + [(0, cap - capacity)])
        return value

    vmem = pl.BlockSpec(memory_space=pltpu.VMEM)
    row = lambda *lead: pltpu.VMEM(lead + (1, cap), F32)
    dma = pltpu.SemaphoreType.DMA
    corrected, src_params, att_params = pl.pallas_call(
        functools.partial(kernel, n_sky, n_tm),
        out_shape=(
            jax.ShapeDtypeStruct((zones, cap), F32),
            jax.ShapeDtypeStruct((SRC_PARAMS, SRC_DEV), F32),
            jax.ShapeDtypeStruct((ATT_PARAMS, SEG_DEV), F32),
        ),
        in_specs=[pl.BlockSpec(memory_space=pltpu.HBM)] * 9,
        out_specs=(vmem, vmem, vmem),
        scratch_shapes=[
            pltpu.VMEM((zones, cap), F32),
            pltpu.SMEM((zones,), jnp.int32),
            pltpu.VMEM((zones, cap), jnp.int32),
            pltpu.VMEM((SRC_PARAMS, zones, cap), BF16),
            pltpu.VMEM((zones, cap), jnp.int32),
            pltpu.VMEM((ATT_PARAMS, zones, cap), BF16),
            pltpu.VMEM((zones, cap), jnp.int32),
            pltpu.VMEM((zones, cap), jnp.int32),
            pltpu.VMEM((SPLINE, zones, cap), BF16),
            dma((9,)),
            pltpu.VMEM((zones, SRC_DEV // 2, cap), BF16),
            pltpu.VMEM((zones, SEG_DEV // 2, cap), BF16),
            row(zones),
            row(zones),
            pltpu.VMEM((zones, 2 * UNIT_ROWS, cap), BF16),
            pltpu.VMEM((zones, EXTENT, cap), BF16),
            pltpu.VMEM((zones, EXTENT, cap), BF16),
            pltpu.VMEM((zones, EXTENT, cap), BF16),
            pltpu.VMEM((zones, 2 * RIM, cap), F32),
            pltpu.VMEM((zones, 2 * RIM, cap), F32),
            pltpu.VMEM((zones, rows_of(SRC_PARAMS), cap), F32),
            pltpu.VMEM((zones, rows_of(ATT_PARAMS), cap), F32),
            pltpu.VMEM((zones, SPLINE, cap), F32),
            row(zones),
            row(zones),
            row(zones),
            row(zones),
            pltpu.VMEM((zones, 8, cap), F32),
            pltpu.VMEM((n_sky, 1, 3 * LANES), F32),
            pltpu.VMEM((devices, 1, 3 * LANES), F32),
            pltpu.VMEM((ITERS, 1, LANES), F32),
            pltpu.VMEM((ITERS, devices, 1, LANES), F32),
            row(ITERS, zones),
            row(ITERS, zones),
            row(ITERS, zones),
            row(ITERS, zones),
            pltpu.VMEM((ITERS, 2, 2, RIM, LANES), F32),
            pltpu.VMEM((ITERS, 2, 2, RIM, LANES), F32),
            dma((2,)),
            dma((ITERS, 2)),
            dma((ITERS,)),
            dma((ITERS, n_sky)),
            dma((ITERS,)),
            dma((ITERS,)),
            dma((ITERS, 2)),
            dma((ITERS, 2)),
        ],
        compiler_params=pltpu.CompilerParams(
            collective_id=0, has_side_effects=True, vmem_limit_bytes=67_043_328
        ),
        name="astrometry",
    )(
        flat(residual),
        counts.reshape(zones),
        flat(source_index),
        flat(source_partials),
        flat(segment_index),
        flat(attitude_partials),
        flat(unit_index),
        flat(knot_base),
        flat(calib_partials),
    )
    results = (corrected, src_params, att_params)
    corrected, src_params, att_params = pl.pallas_call(
        functools.partial(write_out, len(results)),
        out_shape=tuple(jax.ShapeDtypeStruct(value.shape, value.dtype) for value in results),
        in_specs=[vmem] * len(results),
        out_specs=tuple(pl.BlockSpec(memory_space=pltpu.HBM) for _ in results),
        scratch_shapes=[dma((len(results),))],
        name="write_out",
    )(*results)
    return corrected[:, :capacity].reshape(1, 1, zones, capacity), src_params, att_params


def solution(mesh):
    return jax.shard_map(
        functools.partial(shards, n_sky=mesh.shape["sky"], n_tm=mesh.shape["tm"]),
        mesh=mesh,
        in_specs=(
            P("sky", "tm", None, None),
            P("sky", "tm", None),
            P("sky", "tm", None, None),
            P(None, "sky", "tm", None, None),
            P("sky", "tm", None, None),
            P(None, "sky", "tm", None, None),
            P("sky", "tm", None, None),
            P("sky", "tm", None, None),
            P(None, "sky", "tm", None, None),
        ),
        out_specs=(P("sky", "tm", None, None), P(None, ("sky", "tm")), P(None, ("sky", "tm"))),
        check_vma=False,
    )
```

```python
import functools

import jax
import jax.numpy as jnp
from jax import lax
from jax.experimental import pallas as pl
from jax.experimental.pallas import tpu as pltpu
from jax.sharding import PartitionSpec as P

SRC_DEV = 256
SEG_DEV = 128
KNOT_DEV = 113
UNITS = 62
SPLINE = 16
SRC_PARAMS = 5
ATT_PARAMS = 4
ITERS = 2

clip_factor = 1.5
ridge = 1.0

LANES = 128
F32 = jnp.float32
BF16 = jnp.bfloat16
MESH = pl.DeviceIdType.MESH
UNIT_ROWS = -(-UNITS // 64) * 64
EXTENT = -(-(KNOT_DEV + SPLINE - 1) // LANES) * LANES
RIM = SPLINE


def lower_pairs(order):
    return [(row_at, col_at) for row_at in range(order) for col_at in range(row_at + 1)]


def rows_of(order):
    return -(-(order + len(lower_pairs(order))) // 8) * 8


def split_rows(value):
    high = value.astype(BF16).astype(F32)
    return jnp.concatenate([high, value - high], axis=0).astype(BF16)


def dot_nt(left, right):
    return lax.dot_general(left, right, (((1,), (1,)), ((), ())), preferred_element_type=F32)


def dot_nn(left, right):
    return lax.dot_general(left, right, (((1,), (0,)), ((), ())), preferred_element_type=F32)


def in_groups(count, size, body, carry):
    if count <= 16:
        for start in range(0, count, size):
            carry = body(list(range(start, min(start + size, count))), carry)
        return carry
    size = size if count % size == 0 else 1

    def group(number, carry):
        return body([number * size + at for at in range(size)], carry)

    return lax.fori_loop(0, count // size, group, carry)


def add_all(values):
    values = list(values)
    while len(values) > 1:
        values = [
            values[at] + values[at + 1] if at + 1 < len(values) else values[at]
            for at in range(0, len(values), 2)
        ]
    return values[0]


def each(count, body, carry):
    if count <= 16:
        for number in range(count):
            carry = body(number, carry)
        return carry
    return lax.fori_loop(0, count, body, carry)


def block_solve(sums, order):
    pairs = lower_pairs(order)
    matrix = {}
    for number, (row_at, col_at) in enumerate(pairs):
        at = order + number
        matrix[row_at, col_at] = sums[at : at + 1] + (ridge if row_at == col_at else 0.0)
    right = [sums[at : at + 1] for at in range(order)]
    inverse = []
    for pivot in range(order):
        inverse.append(1.0 / matrix[pivot, pivot])
        for row_at in range(pivot + 1, order):
            ratio = matrix[row_at, pivot] * inverse[pivot]
            for col_at in range(pivot + 1, row_at + 1):
                matrix[row_at, col_at] = matrix[row_at, col_at] - ratio * matrix[col_at, pivot]
            right[row_at] = right[row_at] - ratio * right[pivot]
    solved = [None] * order
    for row_at in reversed(range(order)):
        running = right[row_at]
        for inner_at in range(row_at + 1, order):
            running = running - matrix[inner_at, row_at] * solved[inner_at]
        solved[row_at] = running * inverse[row_at]
    return jnp.concatenate(solved, axis=0)


def store_products(partials_ref, prods, order):
    values = [partials_ref[at].astype(F32) for at in range(order)]
    listed = values + [values[row_at] * values[col_at] for row_at, col_at in lower_pairs(order)]
    while len(listed) < prods.shape[1]:
        listed.append(jnp.zeros_like(values[0]))
    for at, value in enumerate(listed):
        prods[:, at, :] = value


def kernel(
    n_sky,
    n_tm,
    res_hbm,
    cnt_hbm,
    src_hbm,
    sp_hbm,
    seg_hbm,
    ap_hbm,
    unit_hbm,
    base_hbm,
    cp_hbm,
    out_ref,
    srcp_ref,
    attp_ref,
    res_ref,
    cnt_ref,
    src_ref,
    sp_ref,
    seg_ref,
    ap_ref,
    unit_ref,
    base_ref,
    cp_ref,
    in_sems,
    src_hot,
    seg_hot,
    src_side,
    seg_side,
    unit_hot,
    placed,
    sq_high,
    sq_low,
    rim_part,
    rim_square,
    src_prods,
    att_prods,
    cal_rows,
    r_src,
    r_time,
    v_time,
    live_time,
    fit_time,
    stat_send,
    stat_recv,
    abs_send,
    abs_recv,
    fwd_send,
    fwd_recv,
    back_send,
    back_recv,
    rim_send,
    rim_recv,
    stat_sems,
    abs_sems,
    fwd_ssem,
    fwd_rsem,
    back_ssem,
    back_rsem,
    rim_ssem,
    rim_rsem,
):
    zones, cap = res_ref.shape
    tiles = cap // LANES
    devices = n_sky * n_tm
    sky = lax.axis_index("sky")
    tm = lax.axis_index("tm")
    me = sky * n_tm + tm

    def wrapped(value, size):
        return jnp.where(value >= size, value - size, value)

    lower = sky < n_sky // 2

    def far_first(number):
        down = n_sky - 1 - number
        down = jnp.where(down <= sky, down - 1, down)
        up = jnp.where(number >= sky, number + 1, number)
        peer = jnp.where(lower, down, up)
        if isinstance(number, int):
            return sky if number == n_sky - 1 else peer
        return jnp.where(number == n_sky - 1, sky, peer)

    def every_other(body):
        if devices <= 64:
            if n_tm & (n_tm - 1):
                tms = [wrapped(tm + at, n_tm) for at in range(n_tm)]
            else:
                tms = [tm ^ at for at in range(n_tm)]
            for number in range(n_sky):
                other = far_first(number)
                for at in reversed(range(n_tm)):
                    if number < n_sky - 1 or at:
                        body(other, tms[at])
            return

        @pl.loop(1, devices)
        def _(step):
            flat = lax.rem(me + step, devices)
            body(flat // n_tm, lax.rem(flat, n_tm))

    arriving = [
        pltpu.make_async_copy(source, target, in_sems.at[number])
        for number, (source, target) in enumerate(
            (
                (res_hbm, res_ref),
                (cnt_hbm, cnt_ref),
                (src_hbm, src_ref),
                (sp_hbm, sp_ref),
                (seg_hbm, seg_ref),
                (ap_hbm, ap_ref),
                (unit_hbm, unit_ref),
                (base_hbm, base_ref),
                (cp_hbm, cp_ref),
            )
        )
    ]
    for copy in arriving:
        copy.start()

    barrier = pltpu.get_barrier_semaphore()

    def greet(to_sky, to_tm):
        pl.semaphore_signal(
            barrier, inc=1, device_id={"sky": to_sky, "tm": to_tm}, device_id_type=MESH
        )

    every_other(greet)

    lane_row = lax.broadcasted_iota(jnp.int32, (1, cap), 1)

    def fold(row):
        total = row[:, :LANES]
        for at in range(1, tiles):
            total = total + row[:, at * LANES : (at + 1) * LANES]
        return total

    def widen(row):
        return jnp.concatenate([row] * tiles, axis=1) if tiles > 1 else row

    def live_of(zone):
        return (lane_row < cnt_ref[zone]).astype(F32)

    for copy in arriving[:2]:
        copy.wait()

    def first_stats(zone, carry):
        sums, lives = carry
        live = live_of(zone)
        row = res_ref[pl.ds(zone, 1), :] * live
        r_src[zone] = row
        stat_send[zone, :, 2 * LANES :] = jnp.full((1, LANES), cnt_ref[zone], jnp.int32).astype(F32)
        return sums + fold(jnp.abs(row)), lives + fold(live)

    zero_row = jnp.zeros((1, LANES), F32)
    sums, lives = each(zones, first_stats, (zero_row, zero_row))

    def put_stats(zone, carry):
        stat_send[zone, :, :LANES] = sums
        stat_send[zone, :, LANES : 2 * LANES] = lives
        return carry

    each(zones, put_stats, 0)
    stat_recv[me] = stat_send[sky]
    pl.semaphore_wait(barrier, devices - 1)

    def send_stats(to_sky, to_tm):
        pltpu.make_async_remote_copy(
            src_ref=stat_send.at[to_sky],
            dst_ref=stat_recv.at[me],
            send_sem=stat_sems.at[0],
            recv_sem=stat_sems.at[1],
            device_id={"sky": to_sky, "tm": to_tm},
            device_id_type=MESH,
        ).start()

    every_other(send_stats)

    for copy in arriving[2:]:
        copy.wait()

    store_products(sp_ref, src_prods, SRC_PARAMS)
    store_products(ap_ref, att_prods, ATT_PARAMS)
    for at in range(SPLINE):
        cal_rows[:, at, :] = cp_ref[at].astype(F32)

    def hot_rows(rows, labels):
        number = lax.broadcasted_iota(jnp.int32, (rows, cap), 0)
        return jnp.where(number == labels, 1.0, 0.0).astype(BF16)

    def tables(zone, carry):
        for labels_ref, hot_ref, side_ref in ((src_ref, src_hot, src_side), (seg_ref, seg_hot, seg_side)):
            labels = labels_ref[pl.ds(zone, 1), :]
            groups = hot_ref.shape[1]
            above = labels >= groups
            hot_ref[zone] = hot_rows(groups, jnp.where(above, labels - groups, labels))
            side_ref[zone] = jnp.where(above, 1.0, 0.0)
        hot = hot_rows(UNIT_ROWS, unit_ref[pl.ds(zone, 1), :])
        unit_hot[zone] = jnp.concatenate([hot, hot], axis=0)
        base = jnp.broadcast_to(base_ref[pl.ds(zone, 1), :], (8, cap))
        turned = []
        for part in range(SPLINE // 8):
            rows = cal_rows[zone, part * 8 : part * 8 + 8, :]
            for bit in (1, 2, 4):
                rows = jnp.where((base & bit) != 0, pltpu.roll(rows, bit, 0), rows)
            turned.append(rows)
        reach = lax.shift_right_arithmetic(
            lax.broadcasted_iota(jnp.int32, (8, cap), 0) - base, jnp.int32(3)
        )
        pieces = []
        for group in range(EXTENT // 8):
            piece = jnp.zeros((8, cap), F32)
            for part, rows in enumerate(turned):
                piece = jnp.where(reach == part - group, rows, piece)
            pieces.append(piece)
        spread = jnp.concatenate(pieces, axis=0)
        placed[zone] = spread.astype(BF16)
        square = spread * spread
        rim_part[zone] = jnp.concatenate([spread[:RIM], spread[EXTENT - RIM :]], axis=0)
        rim_square[zone] = jnp.concatenate([square[:RIM], square[EXTENT - RIM :]], axis=0)
        high = square.astype(BF16)
        sq_high[zone] = high
        sq_low[zone] = (square - high.astype(F32)).astype(BF16)
        return carry

    each(zones, tables, 0)

    whole_stat = stat_recv.at[pl.ds(0, devices - 1)]
    pltpu.make_async_copy(whole_stat, whole_stat, stat_sems.at[1]).wait()
    stats = jnp.sum(stat_recv[...], axis=0)
    live_total = jnp.sum(stats[:, LANES : 2 * LANES], axis=1, keepdims=True)
    abs_total = jnp.sum(stats[:, :LANES], axis=1, keepdims=True)

    def time_live(zone, carry):
        counts = stat_recv[zone * n_tm + tm][:, 2 * LANES :]
        live_time[zone] = (lane_row.astype(F32) < widen(counts)).astype(F32)
        return carry

    each(zones, time_live, 0)

    src_total = jnp.zeros((SRC_PARAMS, SRC_DEV), F32)
    att_total = jnp.zeros((ATT_PARAMS, SEG_DEV), F32)

    def group_sums(zone, prods, hot, side, order, weights, row):
        number = lax.broadcasted_iota(jnp.int32, (8, cap), 0)
        scaled = jnp.concatenate(
            [
                prods[zone, :8, :] * jnp.where(number < order, weights * row, weights),
                prods[zone, 8:, :] * weights,
            ],
            axis=0,
        )
        tall = split_rows(scaled)
        above = tall * side[zone].astype(BF16)
        return dot_nt(jnp.concatenate([tall - above, above], axis=0), hot[zone])

    def group_totals(both, order):
        rows = both.shape[0] // 4
        both = jnp.concatenate([both[: 2 * rows], both[2 * rows :]], axis=1)
        return both[:rows] + both[rows:]

    def padded_steps(step, order):
        groups = step.shape[1]
        tall = split_rows(jnp.concatenate([step, jnp.zeros((8 - order, groups), F32)], axis=0))
        return jnp.concatenate([tall[:, : groups // 2], tall[:, groups // 2 :]], axis=0)

    def fitted(zones_at, steps, prods, hot, side):
        picked = [dot_nn(steps, hot[zone]) for zone in zones_at]
        fits = []
        for zone, values in zip(zones_at, picked):
            values = jnp.where(side[zone] > 0.5, values[16:24] + values[24:], values[:8] + values[8:16])
            fits.append(jnp.sum(values * prods[zone, :8, :], axis=0, keepdims=True))
        return fits

    def zone_copy(send, recv, ssem, rsem, peer):
        return pltpu.make_async_remote_copy(
            src_ref=send.at[peer],
            dst_ref=recv.at[sky],
            send_sem=ssem,
            recv_sem=rsem,
            device_id={"sky": peer, "tm": tm},
            device_id_type=MESH,
        )

    wide = 2 * UNIT_ROWS

    def unit_weights(zone, row):
        high = row.astype(BF16).astype(F32)
        tall = jnp.concatenate(
            [
                jnp.broadcast_to(high, (UNIT_ROWS, cap)),
                jnp.broadcast_to(row - high, (UNIT_ROWS, cap)),
            ],
            axis=0,
        ).astype(BF16)
        return unit_hot[zone] * tall

    for it in range(ITERS):
        bound = clip_factor * (abs_total / live_total)

        def src_sums(numbers, total):
            rows = [r_src[zone] for zone in numbers]
            weights = [
                live_of(zone) * bound / jnp.maximum(jnp.abs(row), bound)
                for zone, row in zip(numbers, rows)
            ]
            return total + add_all(
                group_sums(zone, src_prods, src_hot, src_side, SRC_PARAMS, weight, row)
                for zone, weight, row in zip(numbers, weights, rows)
            )

        both = in_groups(
            zones, 8, src_sums, jnp.zeros((4 * rows_of(SRC_PARAMS), SRC_DEV // 2), F32)
        )
        step_x = block_solve(group_totals(both, SRC_PARAMS), SRC_PARAMS)
        src_total = src_total + step_x
        steps_x = padded_steps(step_x, SRC_PARAMS)

        def src_out(numbers, carry):
            zones_at = [far_first(number) for number in numbers]
            fits = fitted(zones_at, steps_x, src_prods, src_hot, src_side)
            for zone, fit in zip(zones_at, fits):
                fwd_send[it, zone] = r_src[zone] - live_of(zone) * fit

            for number, zone in zip(numbers, zones_at):

                def send():
                    zone_copy(
                        fwd_send.at[it], fwd_recv.at[it], fwd_ssem.at[it], fwd_rsem.at[it, sky], zone
                    ).start()

                if isinstance(number, int):
                    if number < n_sky - 1:
                        send()
                else:
                    pl.when(number < n_sky - 1)(send)
            return carry

        in_groups(zones, 4, src_out, 0)
        fwd_recv[it, sky] = fwd_send[it, sky]

        def att_sums(numbers, total):
            zones_at = [far_first(n_sky - 1 - number) for number in numbers]
            for number, zone in zip(numbers, zones_at):

                def arrive():
                    zone_copy(
                        fwd_send.at[it], fwd_recv.at[it], fwd_ssem.at[it], fwd_rsem.at[it, zone], zone
                    ).wait_recv()

                if isinstance(number, int):
                    if number > 0:
                        arrive()
                else:
                    pl.when(number > 0)(arrive)
            rows = [fwd_recv[it, zone] for zone in zones_at]
            weights = [
                live_time[zone] * bound / jnp.maximum(jnp.abs(row), bound)
                for zone, row in zip(zones_at, rows)
            ]
            for zone, weight in zip(zones_at, weights):
                v_time[zone] = weight
            att_part, h_part = total
            att_part = att_part + add_all(
                group_sums(zone, att_prods, seg_hot, seg_side, ATT_PARAMS, weight, row)
                for zone, weight, row in zip(zones_at, weights, rows)
            )
            h_part = h_part + add_all(
                dot_nt(split_rows(rim_square[zone] * weight), unit_hot[zone, :UNIT_ROWS, :])
                for zone, weight in zip(zones_at, weights)
            )
            return att_part, h_part

        rim_blank = jnp.zeros((4 * RIM, UNIT_ROWS), F32)
        both, h_rims = in_groups(
            zones,
            2,
            att_sums,
            (jnp.zeros((4 * rows_of(ATT_PARAMS), SEG_DEV // 2), F32), rim_blank),
        )
        step_y = block_solve(group_totals(both, ATT_PARAMS), ATT_PARAMS)
        att_total = att_total + step_y
        steps_y = padded_steps(step_y, ATT_PARAMS)

        def rim_sums(numbers, total):
            fits = fitted(numbers, steps_y, att_prods, seg_hot, seg_side)
            rows = [
                fwd_recv[it, zone] - live_time[zone] * fit for zone, fit in zip(numbers, fits)
            ]
            for zone, row in zip(numbers, rows):
                r_time[zone] = row
            return total + add_all(
                dot_nt(split_rows(rim_part[zone] * (v_time[zone] * row)), unit_hot[zone, :UNIT_ROWS, :])
                for zone, row in zip(numbers, rows)
            )

        g_rims = in_groups(zones, 8, rim_sums, rim_blank)
        g_rims = g_rims[: 2 * RIM] + g_rims[2 * RIM :]
        h_rims = h_rims[: 2 * RIM] + h_rims[2 * RIM :]

        def joined(g_part, h_part):
            g_part = g_part + pltpu.roll(g_part, UNIT_ROWS, 1)
            left_half = lax.broadcasted_iota(jnp.int32, g_part.shape, 1) < UNIT_ROWS
            return jnp.where(left_half, g_part, h_part)

        def coefs_of(knots):
            ratio = knots / (pltpu.roll(knots, UNIT_ROWS, 1) + ridge)
            left_half = lax.broadcasted_iota(jnp.int32, knots.shape, 1) < UNIT_ROWS
            ratio = jnp.where(left_half, ratio, 0.0)
            high = ratio.astype(BF16).astype(F32)
            return (high + pltpu.roll(ratio - high, UNIT_ROWS, 1)).astype(BF16)

        for way, rows in ((0, slice(RIM, 2 * RIM)), (1, slice(0, RIM))):
            rim_send[it, way, 0, :, :UNIT_ROWS] = g_rims[rows]
            rim_send[it, way, 1, :, :UNIT_ROWS] = h_rims[rows]
        rims = []
        for way, by in ((0, 1), (1, n_tm - 1)):
            copy = pltpu.make_async_remote_copy(
                src_ref=rim_send.at[it, way],
                dst_ref=rim_recv.at[it, way],
                send_sem=rim_ssem.at[it, way],
                recv_sem=rim_rsem.at[it, way],
                device_id={"sky": sky, "tm": lax.rem(tm + by, n_tm)},
                device_id_type=MESH,
            )
            copy.start()
            rims.append(copy)

        inner = slice(RIM, EXTENT - RIM)

        def inner_sums(numbers, total):
            g_part, h_part = total
            for zone in numbers:
                weight = v_time[zone]
                tall = unit_weights(zone, weight)
                h_part = h_part + dot_nt(sq_high[zone, inner, :], tall) + dot_nt(sq_low[zone, inner, :], tall)
                g_part = g_part + dot_nt(placed[zone, inner, :], unit_weights(zone, weight * r_time[zone]))
            return g_part, h_part

        middle = jnp.zeros((EXTENT - 2 * RIM, wide), F32)
        middle, h_total = in_groups(zones, 8, inner_sums, (middle, middle))
        h_total = h_total + pltpu.roll(h_total, UNIT_ROWS, 1)
        inner_coefs = coefs_of(joined(middle, h_total))

        def inner_fit(zone, carry):
            picked = dot_nn(inner_coefs, unit_hot[zone])
            fit = picked * placed[zone, inner, :].astype(F32)
            fit_time[zone] = jnp.sum(fit.reshape(-1, 8, cap), axis=0)
            return carry

        each(zones, inner_fit, 0)

        for copy in rims:
            copy.wait_recv()
        lead = KNOT_DEV - (EXTENT - RIM)
        shared = SPLINE - 1
        from_last = jnp.where(tm > 0, rim_recv[it, 0], 0.0)[:, lead : lead + shared, :UNIT_ROWS]
        from_next = jnp.where(tm < n_tm - 1, rim_recv[it, 1], 0.0)[:, :shared, :UNIT_ROWS]

        def added(rims, at):
            blank = lambda rows: [jnp.zeros((rows, UNIT_ROWS), F32)] if rows else []
            return rims + jnp.concatenate(
                [from_last[at]]
                + blank(RIM - shared + lead)
                + [from_next[at]]
                + blank(RIM - lead - shared),
                axis=0,
            )

        rim_coefs = split_rows(added(g_rims, 0) / (added(h_rims, 1) + ridge))

        last = it == ITERS - 1

        def cal_out(numbers, total):
            picked = [dot_nn(rim_coefs, unit_hot[zone, :UNIT_ROWS, :]) for zone in numbers]
            rows = []
            for zone, values in zip(numbers, picked):
                fit = (values[: 2 * RIM] + values[2 * RIM :]) * rim_part[zone]
                fit = jnp.sum(fit.reshape(-1, 8, cap), axis=0) + fit_time[zone]
                fit = jnp.sum(fit, axis=0, keepdims=True)
                rows.append(r_time[zone] - live_time[zone] * fit)
            for zone, row in zip(numbers, rows):
                back_send[it, zone] = row
            return total + add_all(fold(jnp.abs(row)) for row in rows)

        abs_sum = in_groups(zones, 8, cal_out, zero_row)

        if not last:
            abs_send[it] = abs_sum
            abs_recv[it, me] = abs_sum

            def send_abs(to_sky, to_tm):
                pltpu.make_async_remote_copy(
                    src_ref=abs_send.at[it],
                    dst_ref=abs_recv.at[it, me],
                    send_sem=abs_sems.at[it, 0],
                    recv_sem=abs_sems.at[it, 1],
                    device_id={"sky": to_sky, "tm": to_tm},
                    device_id_type=MESH,
                ).start()

            every_other(send_abs)

        def back_out(number, carry):
            zone_copy(
                back_send.at[it], back_recv.at[it], back_ssem.at[it], back_rsem.at[it], far_first(number)
            ).start()
            return carry

        each(n_sky - 1, back_out, 0)
        back_recv[it, sky] = back_send[it, sky]

        if not last:
            whole = abs_recv.at[it, pl.ds(0, devices - 1)]
            pltpu.make_async_copy(whole, whole, abs_sems.at[it, 1]).wait()
            abs_total = jnp.sum(jnp.sum(abs_recv[it], axis=0), axis=1, keepdims=True)

        whole = back_recv.at[it, pl.ds(0, n_sky - 1)]
        pltpu.make_async_copy(whole, whole, back_rsem.at[it]).wait()

        def put_back(zone, carry):
            if last:
                out_ref[pl.ds(zone, 1), :] = back_recv[it, zone]
            else:
                r_src[zone] = back_recv[it, zone]
            return carry

        each(zones, put_back, 0)

    srcp_ref[...] = src_total
    attp_ref[...] = att_total

    pltpu.make_async_copy(whole_stat, whole_stat, stat_sems.at[0]).wait()
    for it in range(ITERS):
        if it < ITERS - 1:
            whole = abs_recv.at[it, pl.ds(0, devices - 1)]
            pltpu.make_async_copy(whole, whole, abs_sems.at[it, 0]).wait()

        for recv, ssem in ((fwd_recv, fwd_ssem), (back_recv, back_ssem)):
            whole = recv.at[it, pl.ds(0, n_sky - 1)]
            pltpu.make_async_copy(whole, whole, ssem.at[it]).wait()
        for way, by in ((0, 1), (1, n_tm - 1)):
            pltpu.make_async_remote_copy(
                src_ref=rim_send.at[it, way],
                dst_ref=rim_recv.at[it, way],
                send_sem=rim_ssem.at[it, way],
                recv_sem=rim_rsem.at[it, way],
                device_id={"sky": sky, "tm": lax.rem(tm + by, n_tm)},
                device_id_type=MESH,
            ).wait_send()


def write_out(count, *refs):
    sems = refs[-1]
    copies = [
        pltpu.make_async_copy(refs[at], refs[count + at], sems.at[at]) for at in range(count)
    ]
    for copy in copies:
        copy.start()
    for copy in copies:
        copy.wait()


def shards(
    residual,
    counts,
    source_index,
    source_partials,
    segment_index,
    attitude_partials,
    unit_index,
    knot_base,
    calib_partials,
    n_sky,
    n_tm,
):
    zones, capacity = residual.shape[2:]
    cap = -(-capacity // LANES) * LANES
    devices = n_sky * n_tm

    def flat(value):
        value = value.reshape(value.shape[:-4] + (zones, capacity))
        if cap != capacity:
            value = jnp.pad(value, [(0, 0)] * (value.ndim - 1) + [(0, cap - capacity)])
        return value

    vmem = pl.BlockSpec(memory_space=pltpu.VMEM)
    row = lambda *lead: pltpu.VMEM(lead + (1, cap), F32)
    dma = pltpu.SemaphoreType.DMA
    result_bytes = 4 * (zones * cap + 8 * SRC_DEV + 8 * SEG_DEV)
    pinned = cap == capacity
    result = pltpu.VMEM if pinned else jax.ShapeDtypeStruct
    corrected, src_params, att_params = pl.pallas_call(
        functools.partial(kernel, n_sky, n_tm),
        out_shape=(
            result((zones, cap), F32),
            result((SRC_PARAMS, SRC_DEV), F32),
            result((ATT_PARAMS, SEG_DEV), F32),
        ),
        in_specs=[pl.BlockSpec(memory_space=pltpu.HBM)] * 9,
        out_specs=(vmem, vmem, vmem),
        scratch_shapes=[
            pltpu.VMEM((zones, cap), F32),
            pltpu.SMEM((zones,), jnp.int32),
            pltpu.VMEM((zones, cap), jnp.int32),
            pltpu.VMEM((SRC_PARAMS, zones, cap), BF16),
            pltpu.VMEM((zones, cap), jnp.int32),
            pltpu.VMEM((ATT_PARAMS, zones, cap), BF16),
            pltpu.VMEM((zones, cap), jnp.int32),
            pltpu.VMEM((zones, cap), jnp.int32),
            pltpu.VMEM((SPLINE, zones, cap), BF16),
            dma((9,)),
            pltpu.VMEM((zones, SRC_DEV // 2, cap), BF16),
            pltpu.VMEM((zones, SEG_DEV // 2, cap), BF16),
            row(zones),
            row(zones),
            pltpu.VMEM((zones, 2 * UNIT_ROWS, cap), BF16),
            pltpu.VMEM((zones, EXTENT, cap), BF16),
            pltpu.VMEM((zones, EXTENT, cap), BF16),
            pltpu.VMEM((zones, EXTENT, cap), BF16),
            pltpu.VMEM((zones, 2 * RIM, cap), F32),
            pltpu.VMEM((zones, 2 * RIM, cap), F32),
            pltpu.VMEM((zones, rows_of(SRC_PARAMS), cap), F32),
            pltpu.VMEM((zones, rows_of(ATT_PARAMS), cap), F32),
            pltpu.VMEM((zones, SPLINE, cap), F32),
            row(zones),
            row(zones),
            row(zones),
            row(zones),
            pltpu.VMEM((zones, 8, cap), F32),
            pltpu.VMEM((n_sky, 1, 3 * LANES), F32),
            pltpu.VMEM((devices, 1, 3 * LANES), F32),
            pltpu.VMEM((ITERS, 1, LANES), F32),
            pltpu.VMEM((ITERS, devices, 1, LANES), F32),
            row(ITERS, zones),
            row(ITERS, zones),
            row(ITERS, zones),
            row(ITERS, zones),
            pltpu.VMEM((ITERS, 2, 2, RIM, LANES), F32),
            pltpu.VMEM((ITERS, 2, 2, RIM, LANES), F32),
            dma((2,)),
            dma((ITERS, 2)),
            dma((ITERS,)),
            dma((ITERS, n_sky)),
            dma((ITERS,)),
            dma((ITERS,)),
            dma((ITERS, 2)),
            dma((ITERS, 2)),
        ],
        compiler_params=pltpu.CompilerParams(
            collective_id=0, has_side_effects=True, vmem_limit_bytes=67010000
        ),
        name="astrometry",
    )(
        flat(residual),
        counts.reshape(zones),
        flat(source_index),
        flat(source_partials),
        flat(segment_index),
        flat(attitude_partials),
        flat(unit_index),
        flat(knot_base),
        flat(calib_partials),
    )
    results = (corrected, src_params, att_params)
    if pinned:
        results = [pltpu.with_memory_space_constraint(value, pltpu.VMEM) for value in results]
    corrected, src_params, att_params = pl.pallas_call(
        functools.partial(write_out, len(results)),
        out_shape=tuple(jax.ShapeDtypeStruct(value.shape, value.dtype) for value in results),
        in_specs=[vmem] * len(results),
        out_specs=tuple(pl.BlockSpec(memory_space=pltpu.HBM) for _ in results),
        scratch_shapes=[dma((len(results),))],
        name="write_out",
    )(*results)
    return corrected[:, :capacity].reshape(1, 1, zones, capacity), src_params, att_params


def solution(mesh):
    return jax.shard_map(
        functools.partial(shards, n_sky=mesh.shape["sky"], n_tm=mesh.shape["tm"]),
        mesh=mesh,
        in_specs=(
            P("sky", "tm", None, None),
            P("sky", "tm", None),
            P("sky", "tm", None, None),
            P(None, "sky", "tm", None, None),
            P("sky", "tm", None, None),
            P(None, "sky", "tm", None, None),
            P("sky", "tm", None, None),
            P("sky", "tm", None, None),
            P(None, "sky", "tm", None, None),
        ),
        out_specs=(P("sky", "tm", None, None), P(None, ("sky", "tm")), P(None, ("sky", "tm"))),
        check_vma=False,
    )
```

```python
import functools

import jax
import jax.numpy as jnp
from jax import lax
from jax.experimental import pallas as pl
from jax.experimental.pallas import tpu as pltpu
from jax.sharding import PartitionSpec as P

SRC_DEV = 256
SEG_DEV = 128
KNOT_DEV = 113
UNITS = 62
SPLINE = 16
SRC_PARAMS = 5
ATT_PARAMS = 4
ITERS = 2

clip_factor = 1.5
ridge = 1.0

LANES = 128
F32 = jnp.float32
BF16 = jnp.bfloat16
MESH = pl.DeviceIdType.MESH
UNIT_ROWS = -(-UNITS // 64) * 64
EXTENT = -(-(KNOT_DEV + SPLINE - 1) // LANES) * LANES
RIM = SPLINE


def lower_pairs(order):
    return [(row_at, col_at) for row_at in range(order) for col_at in range(row_at + 1)]


def rows_of(order):
    return -(-(order + len(lower_pairs(order))) // 8) * 8


def split_rows(value):
    high = value.astype(BF16).astype(F32)
    return jnp.concatenate([high, value - high], axis=0).astype(BF16)


def dot_nt(left, right):
    return lax.dot_general(left, right, (((1,), (1,)), ((), ())), preferred_element_type=F32)


def dot_nn(left, right):
    return lax.dot_general(left, right, (((1,), (0,)), ((), ())), preferred_element_type=F32)


def in_groups(count, size, body, carry, first=None):
    if count <= 16:
        start = 0
        while start < count:
            end = min(start + (first if first and not start else size), count)
            carry = body(list(range(start, end)), carry)
            start = end
        return carry
    size = size if count % size == 0 else 1

    def group(number, carry):
        return body([number * size + at for at in range(size)], carry)

    return lax.fori_loop(0, count // size, group, carry)


def in_turns(totals, values):
    totals = list(totals)
    for number, value in enumerate(values):
        totals[number % 2] = totals[number % 2] + value
    return tuple(totals)


def add_all(values):
    values = list(values)
    while len(values) > 1:
        values = [
            values[at] + values[at + 1] if at + 1 < len(values) else values[at]
            for at in range(0, len(values), 2)
        ]
    return values[0]


def each(count, body, carry):
    if count <= 16:
        for number in range(count):
            carry = body(number, carry)
        return carry
    return lax.fori_loop(0, count, body, carry)


def block_solve(sums, order):
    pairs = lower_pairs(order)
    matrix = {}
    for number, (row_at, col_at) in enumerate(pairs):
        at = order + number
        matrix[row_at, col_at] = sums[at : at + 1] + (ridge if row_at == col_at else 0.0)
    right = [sums[at : at + 1] for at in range(order)]
    inverse = []
    for pivot in range(order):
        inverse.append(1.0 / matrix[pivot, pivot])
        for row_at in range(pivot + 1, order):
            ratio = matrix[row_at, pivot] * inverse[pivot]
            for col_at in range(pivot + 1, row_at + 1):
                matrix[row_at, col_at] = matrix[row_at, col_at] - ratio * matrix[col_at, pivot]
            right[row_at] = right[row_at] - ratio * right[pivot]
    solved = [None] * order
    for row_at in reversed(range(order)):
        running = right[row_at]
        for inner_at in range(row_at + 1, order):
            running = running - matrix[inner_at, row_at] * solved[inner_at]
        solved[row_at] = running * inverse[row_at]
    return jnp.concatenate(solved, axis=0)


def store_products(partials_ref, prods, order):
    values = [partials_ref[at].astype(F32) for at in range(order)]
    listed = values + [values[row_at] * values[col_at] for row_at, col_at in lower_pairs(order)]
    while len(listed) < prods.shape[1]:
        listed.append(jnp.zeros_like(values[0]))
    for at, value in enumerate(listed):
        prods[:, at, :] = value


def kernel(
    n_sky,
    n_tm,
    res_hbm,
    cnt_hbm,
    src_hbm,
    sp_hbm,
    seg_hbm,
    ap_hbm,
    unit_hbm,
    base_hbm,
    cp_hbm,
    out_ref,
    srcp_ref,
    attp_ref,
    res_ref,
    cnt_ref,
    src_ref,
    sp_ref,
    seg_ref,
    ap_ref,
    unit_ref,
    base_ref,
    cp_ref,
    in_sems,
    src_hot,
    seg_hot,
    src_side,
    seg_side,
    unit_hot,
    placed,
    sq_high,
    sq_low,
    rim_part,
    rim_square,
    src_prods,
    att_prods,
    cal_rows,
    r_src,
    r_time,
    v_time,
    live_time,
    fit_time,
    stat_send,
    stat_recv,
    abs_send,
    abs_recv,
    fwd_send,
    fwd_recv,
    back_send,
    back_recv,
    rim_send,
    rim_recv,
    stat_sems,
    abs_sems,
    fwd_ssem,
    fwd_rsem,
    back_ssem,
    back_rsem,
    rim_ssem,
    rim_rsem,
):
    zones, cap = res_ref.shape
    tiles = cap // LANES
    devices = n_sky * n_tm
    sky = lax.axis_index("sky")
    tm = lax.axis_index("tm")
    me = sky * n_tm + tm

    def wrapped(value, size):
        return jnp.where(value >= size, value - size, value)

    lower = sky < n_sky // 2

    def far_first(number):
        down = n_sky - 1 - number
        down = jnp.where(down <= sky, down - 1, down)
        up = jnp.where(number >= sky, number + 1, number)
        peer = jnp.where(lower, down, up)
        if isinstance(number, int):
            return sky if number == n_sky - 1 else peer
        return jnp.where(number == n_sky - 1, sky, peer)

    def every_other(body, after=None):
        if devices <= 64:
            if n_tm & (n_tm - 1):
                tms = [wrapped(tm + at, n_tm) for at in range(n_tm)]
            else:
                tms = [tm ^ at for at in range(n_tm)]
            for number in range(n_sky):
                other = far_first(number)
                for at in reversed(range(n_tm)):
                    if number < n_sky - 1 or at:
                        body(other, tms[at])
                if after and number < n_sky - 1:
                    after(other)
            return

        @pl.loop(1, devices)
        def _(step):
            flat = lax.rem(me + step, devices)
            body(flat // n_tm, lax.rem(flat, n_tm))

        if after:
            each(n_sky - 1, lambda number, carry: (after(far_first(number)), carry)[1], 0)

    arriving = [
        pltpu.make_async_copy(source, target, in_sems.at[number])
        for number, (source, target) in enumerate(
            (
                (res_hbm, res_ref),
                (cnt_hbm, cnt_ref),
                (src_hbm, src_ref),
                (sp_hbm, sp_ref),
                (seg_hbm, seg_ref),
                (ap_hbm, ap_ref),
                (unit_hbm, unit_ref),
                (base_hbm, base_ref),
                (cp_hbm, cp_ref),
            )
        )
    ]
    for copy in arriving:
        copy.start()

    barrier = pltpu.get_barrier_semaphore()

    def greet(to_sky, to_tm):
        pl.semaphore_signal(
            barrier, inc=1, device_id={"sky": to_sky, "tm": to_tm}, device_id_type=MESH
        )

    every_other(greet)

    lane_row = lax.broadcasted_iota(jnp.int32, (1, cap), 1)

    def fold(row):
        total = row[:, :LANES]
        for at in range(1, tiles):
            total = total + row[:, at * LANES : (at + 1) * LANES]
        return total

    def widen(row):
        return jnp.concatenate([row] * tiles, axis=1) if tiles > 1 else row

    def live_of(zone):
        return (lane_row < cnt_ref[zone]).astype(F32)

    for copy in arriving[:2]:
        copy.wait()

    def first_stats(zone, carry):
        sums, lives = carry
        live = live_of(zone)
        row = res_ref[pl.ds(zone, 1), :] * live
        r_src[zone] = row
        stat_send[zone, :, 2 * LANES :] = jnp.full((1, LANES), cnt_ref[zone], jnp.int32).astype(F32)
        return sums + fold(jnp.abs(row)), lives + fold(live)

    zero_row = jnp.zeros((1, LANES), F32)
    sums, lives = each(zones, first_stats, (zero_row, zero_row))

    def put_stats(zone, carry):
        stat_send[zone, :, :LANES] = sums
        stat_send[zone, :, LANES : 2 * LANES] = lives
        return carry

    each(zones, put_stats, 0)
    stat_recv[me] = stat_send[sky]
    pl.semaphore_wait(barrier, devices - 1)

    def send_stats(to_sky, to_tm):
        pltpu.make_async_remote_copy(
            src_ref=stat_send.at[to_sky],
            dst_ref=stat_recv.at[me],
            send_sem=stat_sems.at[0],
            recv_sem=stat_sems.at[1],
            device_id={"sky": to_sky, "tm": to_tm},
            device_id_type=MESH,
        ).start()

    every_other(send_stats)

    for copy in arriving[2:]:
        copy.wait()

    store_products(sp_ref, src_prods, SRC_PARAMS)
    store_products(ap_ref, att_prods, ATT_PARAMS)
    for at in range(SPLINE):
        cal_rows[:, at, :] = cp_ref[at].astype(F32)

    def hot_rows(rows, labels):
        number = lax.broadcasted_iota(jnp.int32, (rows, cap), 0)
        return jnp.where(number == labels, 1.0, 0.0).astype(BF16)

    def tables(zone, carry):
        for labels_ref, hot_ref, side_ref in ((src_ref, src_hot, src_side), (seg_ref, seg_hot, seg_side)):
            labels = labels_ref[pl.ds(zone, 1), :]
            groups = hot_ref.shape[1]
            above = labels >= groups
            hot_ref[zone] = hot_rows(groups, jnp.where(above, labels - groups, labels))
            side_ref[zone] = jnp.where(above, 1.0, 0.0)
        hot = hot_rows(UNIT_ROWS, unit_ref[pl.ds(zone, 1), :])
        unit_hot[zone] = jnp.concatenate([hot, hot], axis=0)
        base = jnp.broadcast_to(base_ref[pl.ds(zone, 1), :], (8, cap))
        turned = []
        for part in range(SPLINE // 8):
            rows = cal_rows[zone, part * 8 : part * 8 + 8, :]
            for bit in (1, 2, 4):
                rows = jnp.where((base & bit) != 0, pltpu.roll(rows, bit, 0), rows)
            turned.append(rows)
        reach = lax.shift_right_arithmetic(
            lax.broadcasted_iota(jnp.int32, (8, cap), 0) - base, jnp.int32(3)
        )
        pieces = []
        for group in range(EXTENT // 8):
            piece = jnp.zeros((8, cap), F32)
            for part, rows in enumerate(turned):
                piece = jnp.where(reach == part - group, rows, piece)
            pieces.append(piece)
        spread = jnp.concatenate(pieces, axis=0)
        placed[zone] = spread.astype(BF16)
        square = spread * spread
        rim_part[zone] = jnp.concatenate([spread[:RIM], spread[EXTENT - RIM :]], axis=0)
        rim_square[zone] = jnp.concatenate([square[:RIM], square[EXTENT - RIM :]], axis=0)
        high = square.astype(BF16)
        sq_high[zone] = high
        sq_low[zone] = (square - high.astype(F32)).astype(BF16)
        return carry

    each(zones, tables, 0)

    whole_stat = stat_recv.at[pl.ds(0, devices - 1)]
    pltpu.make_async_copy(whole_stat, whole_stat, stat_sems.at[1]).wait()
    stats = jnp.sum(stat_recv[...], axis=0)
    live_total = jnp.sum(stats[:, LANES : 2 * LANES], axis=1, keepdims=True)
    abs_total = jnp.sum(stats[:, :LANES], axis=1, keepdims=True)

    def time_live(zone, carry):
        counts = stat_recv[zone * n_tm + tm][:, 2 * LANES :]
        live_time[zone] = (lane_row.astype(F32) < widen(counts)).astype(F32)
        return carry

    each(zones, time_live, 0)

    src_total = jnp.zeros((SRC_PARAMS, SRC_DEV), F32)
    att_total = jnp.zeros((ATT_PARAMS, SEG_DEV), F32)

    chunk = min(cap, 256) if cap % 256 == 0 else cap
    parts = [slice(at, at + chunk) for at in range(0, cap, chunk)]

    def group_sums(zone, prods, hot, side, order, weights, row):
        number = lax.broadcasted_iota(jnp.int32, (8, cap), 0)
        scaled = jnp.concatenate(
            [
                prods[zone, :8, :] * jnp.where(number < order, weights * row, weights),
                prods[zone, 8:, :] * weights,
            ],
            axis=0,
        )
        tall = split_rows(scaled)
        above = tall * side[zone].astype(BF16)
        return dot_nt(jnp.concatenate([tall - above, above], axis=0), hot[zone])

    def group_totals(both, order):
        rows = both[0].shape[0] // 4
        halves = []
        for at in (0, 2 * rows):
            low, high = slice(at, at + rows), slice(at + rows, at + 2 * rows)
            halves.append((both[0][low] + both[0][high]) + (both[1][low] + both[1][high]))
        return jnp.concatenate(halves, axis=1)

    def padded_steps(step, order):
        groups = step.shape[1]
        tall = split_rows(jnp.concatenate([step, jnp.zeros((8 - order, groups), F32)], axis=0))
        return jnp.concatenate([tall[:, : groups // 2], tall[:, groups // 2 :]], axis=0)

    def fitted(zones_at, steps, prods, hot, side):
        picked = [[dot_nn(steps, hot[zone, :, part]) for part in parts] for zone in zones_at]
        fits = []
        for zone, values_of in zip(zones_at, picked):
            fit = []
            for part, values in zip(parts, values_of):
                values = jnp.where(
                    side[zone, :, part] > 0.5, values[16:24] + values[24:], values[:8] + values[8:16]
                )
                fit.append(jnp.sum(values * prods[zone, :8, part], axis=0, keepdims=True))
            fits.append(jnp.concatenate(fit, axis=1) if len(fit) > 1 else fit[0])
        return fits

    def zone_copy(send, recv, ssem, rsem, peer):
        return pltpu.make_async_remote_copy(
            src_ref=send.at[peer],
            dst_ref=recv.at[sky],
            send_sem=ssem,
            recv_sem=rsem,
            device_id={"sky": peer, "tm": tm},
            device_id_type=MESH,
        )

    def rim_copies(it, kind):
        return [
            pltpu.make_async_remote_copy(
                src_ref=rim_send.at[it, way, kind],
                dst_ref=rim_recv.at[it, way, kind],
                send_sem=rim_ssem.at[it, way, kind],
                recv_sem=rim_rsem.at[it, way, kind],
                device_id={"sky": sky, "tm": lax.rem(tm + by, n_tm)},
                device_id_type=MESH,
            )
            for way, by in ((0, 1), (1, n_tm - 1))
        ]

    def send_rims(it, kind, rims):
        for way, rows in ((0, slice(RIM, 2 * RIM)), (1, slice(0, RIM))):
            rim_send[it, way, kind, :, :UNIT_ROWS] = rims[rows]
        for copy in rim_copies(it, kind):
            copy.start()

    wide = 2 * UNIT_ROWS

    def unit_weights(zone, row):
        high = row.astype(BF16).astype(F32)
        tall = jnp.concatenate(
            [
                jnp.broadcast_to(high, (UNIT_ROWS, cap)),
                jnp.broadcast_to(row - high, (UNIT_ROWS, cap)),
            ],
            axis=0,
        ).astype(BF16)
        return unit_hot[zone] * tall

    for it in range(ITERS):
        bound = clip_factor * (abs_total / live_total)

        def src_sums(numbers, total):
            rows = [r_src[zone] for zone in numbers]
            weights = [
                live_of(zone) * bound / jnp.maximum(jnp.abs(row), bound)
                for zone, row in zip(numbers, rows)
            ]
            return in_turns(
                total,
                (group_sums(zone, src_prods, src_hot, src_side, SRC_PARAMS, weight, row)
                for zone, weight, row in zip(numbers, weights, rows)),
            )

        blank = jnp.zeros((4 * rows_of(SRC_PARAMS), SRC_DEV // 2), F32)
        both = in_groups(zones, 8, src_sums, (blank, blank))
        step_x = block_solve(group_totals(both, SRC_PARAMS), SRC_PARAMS)
        src_total = src_total + step_x
        steps_x = padded_steps(step_x, SRC_PARAMS)

        def src_out(numbers, carry):
            zones_at = [far_first(number) for number in numbers]
            fits = fitted(zones_at, steps_x, src_prods, src_hot, src_side)
            for zone, fit in zip(zones_at, fits):
                fwd_send[it, zone] = r_src[zone] - live_of(zone) * fit

            for number, zone in zip(numbers, zones_at):

                def send():
                    zone_copy(
                        fwd_send.at[it], fwd_recv.at[it], fwd_ssem.at[it], fwd_rsem.at[it, sky], zone
                    ).start()

                if isinstance(number, int):
                    if number < n_sky - 1:
                        send()
                else:
                    pl.when(number < n_sky - 1)(send)
            return carry

        in_groups(zones, 6, src_out, 0, first=2)
        fwd_recv[it, sky] = fwd_send[it, sky]

        def att_sums(numbers, total):
            zones_at = [far_first(n_sky - 1 - number) for number in numbers]
            for number, zone in zip(numbers, zones_at):

                def arrive():
                    zone_copy(
                        fwd_send.at[it], fwd_recv.at[it], fwd_ssem.at[it], fwd_rsem.at[it, zone], zone
                    ).wait_recv()

                if isinstance(number, int):
                    if number > 0:
                        arrive()
                else:
                    pl.when(number > 0)(arrive)
            rows = [fwd_recv[it, zone] for zone in zones_at]
            weights = [
                live_time[zone] * bound / jnp.maximum(jnp.abs(row), bound)
                for zone, row in zip(zones_at, rows)
            ]
            for zone, weight in zip(zones_at, weights):
                v_time[zone] = weight
            att_part, h_part = total
            att_part = in_turns(
                att_part,
                (
                    group_sums(zone, att_prods, seg_hot, seg_side, ATT_PARAMS, weight, row)
                    for zone, weight, row in zip(zones_at, weights, rows)
                ),
            )
            h_part = in_turns(
                h_part,
                (
                    dot_nt(split_rows(rim_square[zone] * weight), unit_hot[zone, :UNIT_ROWS, :])
                    for zone, weight in zip(zones_at, weights)
                ),
            )
            return att_part, h_part

        rim_blank = (jnp.zeros((4 * RIM, UNIT_ROWS), F32),) * 2
        blank = jnp.zeros((4 * rows_of(ATT_PARAMS), SEG_DEV // 2), F32)
        both, h_rims = in_groups(zones, 2, att_sums, ((blank, blank), rim_blank))

        def rim_total(sums):
            return add_all(half[at : at + 2 * RIM] for half in sums for at in (0, 2 * RIM))

        h_rims = rim_total(h_rims)
        step_y = block_solve(group_totals(both, ATT_PARAMS), ATT_PARAMS)
        att_total = att_total + step_y
        steps_y = padded_steps(step_y, ATT_PARAMS)

        send_rims(it, 1, h_rims)

        def rim_sums(numbers, total):
            fits = fitted(numbers, steps_y, att_prods, seg_hot, seg_side)
            rows = [
                fwd_recv[it, zone] - live_time[zone] * fit for zone, fit in zip(numbers, fits)
            ]
            for zone, row in zip(numbers, rows):
                r_time[zone] = row
            return in_turns(
                total,
                (
                    dot_nt(split_rows(rim_part[zone] * (v_time[zone] * row)), unit_hot[zone, :UNIT_ROWS, :])
                    for zone, row in zip(numbers, rows)
                ),
            )

        g_rims = in_groups(zones, 8, rim_sums, rim_blank)
        g_rims = rim_total(g_rims)

        def joined(g_part, h_part):
            g_part = g_part + pltpu.roll(g_part, UNIT_ROWS, 1)
            left_half = lax.broadcasted_iota(jnp.int32, g_part.shape, 1) < UNIT_ROWS
            return jnp.where(left_half, g_part, h_part)

        def coefs_of(knots):
            ratio = knots / (pltpu.roll(knots, UNIT_ROWS, 1) + ridge)
            left_half = lax.broadcasted_iota(jnp.int32, knots.shape, 1) < UNIT_ROWS
            ratio = jnp.where(left_half, ratio, 0.0)
            high = ratio.astype(BF16).astype(F32)
            return (high + pltpu.roll(ratio - high, UNIT_ROWS, 1)).astype(BF16)

        send_rims(it, 0, g_rims)
        inner = slice(RIM, EXTENT - RIM)

        def inner_sums(numbers, total):
            g_part, h_part = total
            for zone in numbers:
                weight = v_time[zone]
                tall = unit_weights(zone, weight)
                h_part = h_part + dot_nt(sq_high[zone, inner, :], tall) + dot_nt(sq_low[zone, inner, :], tall)
                g_part = g_part + dot_nt(placed[zone, inner, :], unit_weights(zone, weight * r_time[zone]))
            return g_part, h_part

        middle = jnp.zeros((EXTENT - 2 * RIM, wide), F32)
        middle, h_total = in_groups(zones, 8, inner_sums, (middle, middle))
        h_total = h_total + pltpu.roll(h_total, UNIT_ROWS, 1)
        inner_coefs = coefs_of(joined(middle, h_total))

        def inner_fit(zone, carry):
            picked = dot_nn(inner_coefs, unit_hot[zone])
            fit = picked * placed[zone, inner, :].astype(F32)
            fit_time[zone] = jnp.sum(fit.reshape(-1, 8, cap), axis=0)
            return carry

        each(zones, inner_fit, 0)

        for copy in rim_copies(it, 1) + rim_copies(it, 0):
            copy.wait_recv()
        lead = KNOT_DEV - (EXTENT - RIM)
        shared = SPLINE - 1
        from_last = jnp.where(tm > 0, rim_recv[it, 0], 0.0)[:, lead : lead + shared, :UNIT_ROWS]
        from_next = jnp.where(tm < n_tm - 1, rim_recv[it, 1], 0.0)[:, :shared, :UNIT_ROWS]

        def added(rims, at):
            blank = lambda rows: [jnp.zeros((rows, UNIT_ROWS), F32)] if rows else []
            return rims + jnp.concatenate(
                [from_last[at]]
                + blank(RIM - shared + lead)
                + [from_next[at]]
                + blank(RIM - lead - shared),
                axis=0,
            )

        rim_coefs = split_rows(added(g_rims, 0) / (added(h_rims, 1) + ridge))

        last = it == ITERS - 1

        def cal_out(numbers, total):
            picked = [dot_nn(rim_coefs, unit_hot[zone, :UNIT_ROWS, :]) for zone in numbers]
            rows = []
            for zone, values in zip(numbers, picked):
                fit = (values[: 2 * RIM] + values[2 * RIM :]) * rim_part[zone]
                fit = jnp.sum(fit.reshape(-1, 8, cap), axis=0) + fit_time[zone]
                fit = jnp.sum(fit, axis=0, keepdims=True)
                rows.append(r_time[zone] - live_time[zone] * fit)
            for zone, row in zip(numbers, rows):
                back_send[it, zone] = row
            return total + add_all(fold(jnp.abs(row)) for row in rows)

        abs_sum = in_groups(zones, 8, cal_out, zero_row)

        def back_out(peer):
            zone_copy(
                back_send.at[it], back_recv.at[it], back_ssem.at[it], back_rsem.at[it], peer
            ).start()

        if last:
            each(n_sky - 1, lambda number, carry: (back_out(far_first(number)), carry)[1], 0)
        else:
            abs_send[it] = abs_sum
            abs_recv[it, me] = abs_sum

            def send_abs(to_sky, to_tm):
                pltpu.make_async_remote_copy(
                    src_ref=abs_send.at[it],
                    dst_ref=abs_recv.at[it, me],
                    send_sem=abs_sems.at[it, 0],
                    recv_sem=abs_sems.at[it, 1],
                    device_id={"sky": to_sky, "tm": to_tm},
                    device_id_type=MESH,
                ).start()

            every_other(send_abs, back_out)

        back_recv[it, sky] = back_send[it, sky]

        if not last:
            whole = abs_recv.at[it, pl.ds(0, devices - 1)]
            pltpu.make_async_copy(whole, whole, abs_sems.at[it, 1]).wait()
            abs_total = jnp.sum(jnp.sum(abs_recv[it], axis=0), axis=1, keepdims=True)

        whole = back_recv.at[it, pl.ds(0, n_sky - 1)]
        pltpu.make_async_copy(whole, whole, back_rsem.at[it]).wait()

        def put_back(zone, carry):
            if last:
                out_ref[pl.ds(zone, 1), :] = back_recv[it, zone]
            else:
                r_src[zone] = back_recv[it, zone]
            return carry

        each(zones, put_back, 0)

    srcp_ref[...] = src_total
    attp_ref[...] = att_total

    pltpu.make_async_copy(whole_stat, whole_stat, stat_sems.at[0]).wait()
    for it in range(ITERS):
        if it < ITERS - 1:
            whole = abs_recv.at[it, pl.ds(0, devices - 1)]
            pltpu.make_async_copy(whole, whole, abs_sems.at[it, 0]).wait()

        for recv, ssem in ((fwd_recv, fwd_ssem), (back_recv, back_ssem)):
            whole = recv.at[it, pl.ds(0, n_sky - 1)]
            pltpu.make_async_copy(whole, whole, ssem.at[it]).wait()
        for copy in rim_copies(it, 1) + rim_copies(it, 0):
            copy.wait_send()


def write_out(count, *refs):
    sems = refs[-1]
    copies = [
        pltpu.make_async_copy(refs[at], refs[count + at], sems.at[at]) for at in range(count)
    ]
    for copy in copies:
        copy.start()
    for copy in copies:
        copy.wait()


def shards(
    residual,
    counts,
    source_index,
    source_partials,
    segment_index,
    attitude_partials,
    unit_index,
    knot_base,
    calib_partials,
    n_sky,
    n_tm,
):
    zones, capacity = residual.shape[2:]
    cap = -(-capacity // LANES) * LANES
    devices = n_sky * n_tm

    def flat(value):
        value = value.reshape(value.shape[:-4] + (zones, capacity))
        if cap != capacity:
            value = jnp.pad(value, [(0, 0)] * (value.ndim - 1) + [(0, cap - capacity)])
        return value

    vmem = pl.BlockSpec(memory_space=pltpu.VMEM)
    row = lambda *lead: pltpu.VMEM(lead + (1, cap), F32)
    dma = pltpu.SemaphoreType.DMA
    result_bytes = 4 * (zones * cap + 8 * SRC_DEV + 8 * SEG_DEV)
    pinned = cap == capacity
    result = pltpu.VMEM if pinned else jax.ShapeDtypeStruct
    corrected, src_params, att_params = pl.pallas_call(
        functools.partial(kernel, n_sky, n_tm),
        out_shape=(
            result((zones, cap), F32),
            result((SRC_PARAMS, SRC_DEV), F32),
            result((ATT_PARAMS, SEG_DEV), F32),
        ),
        in_specs=[pl.BlockSpec(memory_space=pltpu.HBM)] * 9,
        out_specs=(vmem, vmem, vmem),
        scratch_shapes=[
            pltpu.VMEM((zones, cap), F32),
            pltpu.SMEM((zones,), jnp.int32),
            pltpu.VMEM((zones, cap), jnp.int32),
            pltpu.VMEM((SRC_PARAMS, zones, cap), BF16),
            pltpu.VMEM((zones, cap), jnp.int32),
            pltpu.VMEM((ATT_PARAMS, zones, cap), BF16),
            pltpu.VMEM((zones, cap), jnp.int32),
            pltpu.VMEM((zones, cap), jnp.int32),
            pltpu.VMEM((SPLINE, zones, cap), BF16),
            dma((9,)),
            pltpu.VMEM((zones, SRC_DEV // 2, cap), BF16),
            pltpu.VMEM((zones, SEG_DEV // 2, cap), BF16),
            row(zones),
            row(zones),
            pltpu.VMEM((zones, 2 * UNIT_ROWS, cap), BF16),
            pltpu.VMEM((zones, EXTENT, cap), BF16),
            pltpu.VMEM((zones, EXTENT, cap), BF16),
            pltpu.VMEM((zones, EXTENT, cap), BF16),
            pltpu.VMEM((zones, 2 * RIM, cap), F32),
            pltpu.VMEM((zones, 2 * RIM, cap), F32),
            pltpu.VMEM((zones, rows_of(SRC_PARAMS), cap), F32),
            pltpu.VMEM((zones, rows_of(ATT_PARAMS), cap), F32),
            pltpu.VMEM((zones, SPLINE, cap), F32),
            row(zones),
            row(zones),
            row(zones),
            row(zones),
            pltpu.VMEM((zones, 8, cap), F32),
            pltpu.VMEM((n_sky, 1, 3 * LANES), F32),
            pltpu.VMEM((devices, 1, 3 * LANES), F32),
            pltpu.VMEM((ITERS, 1, LANES), F32),
            pltpu.VMEM((ITERS, devices, 1, LANES), F32),
            row(ITERS, zones),
            row(ITERS, zones),
            row(ITERS, zones),
            row(ITERS, zones),
            pltpu.VMEM((ITERS, 2, 2, RIM, LANES), F32),
            pltpu.VMEM((ITERS, 2, 2, RIM, LANES), F32),
            dma((2,)),
            dma((ITERS, 2)),
            dma((ITERS,)),
            dma((ITERS, n_sky)),
            dma((ITERS,)),
            dma((ITERS,)),
            dma((ITERS, 2, 2)),
            dma((ITERS, 2, 2)),
        ],
        compiler_params=pltpu.CompilerParams(
            collective_id=0, has_side_effects=True, vmem_limit_bytes=67010000
        ),
        name="astrometry",
    )(
        flat(residual),
        counts.reshape(zones),
        flat(source_index),
        flat(source_partials),
        flat(segment_index),
        flat(attitude_partials),
        flat(unit_index),
        flat(knot_base),
        flat(calib_partials),
    )
    results = (corrected, src_params, att_params)
    if pinned:
        results = [pltpu.with_memory_space_constraint(value, pltpu.VMEM) for value in results]
    corrected, src_params, att_params = pl.pallas_call(
        functools.partial(write_out, len(results)),
        out_shape=tuple(jax.ShapeDtypeStruct(value.shape, value.dtype) for value in results),
        in_specs=[vmem] * len(results),
        out_specs=tuple(pl.BlockSpec(memory_space=pltpu.HBM) for _ in results),
        scratch_shapes=[dma((len(results),))],
        name="write_out",
    )(*results)
    return corrected[:, :capacity].reshape(1, 1, zones, capacity), src_params, att_params


def solution(mesh):
    return jax.shard_map(
        functools.partial(shards, n_sky=mesh.shape["sky"], n_tm=mesh.shape["tm"]),
        mesh=mesh,
        in_specs=(
            P("sky", "tm", None, None),
            P("sky", "tm", None),
            P("sky", "tm", None, None),
            P(None, "sky", "tm", None, None),
            P("sky", "tm", None, None),
            P(None, "sky", "tm", None, None),
            P("sky", "tm", None, None),
            P("sky", "tm", None, None),
            P(None, "sky", "tm", None, None),
        ),
        out_specs=(P("sky", "tm", None, None), P(None, ("sky", "tm")), P(None, ("sky", "tm"))),
        check_vma=False,
    )
```

```python
import functools

import jax
import jax.numpy as jnp
from jax import lax
from jax.experimental import pallas as pl
from jax.experimental.pallas import tpu as pltpu
from jax.sharding import PartitionSpec as P

SRC_DEV = 256
SEG_DEV = 128
KNOT_DEV = 113
UNITS = 62
SPLINE = 16
SRC_PARAMS = 5
ATT_PARAMS = 4
ITERS = 2

clip_factor = 1.5
ridge = 1.0

LANES = 128
F32 = jnp.float32
BF16 = jnp.bfloat16
MESH = pl.DeviceIdType.MESH
UNIT_ROWS = -(-UNITS // 64) * 64
EXTENT = -(-(KNOT_DEV + SPLINE - 1) // LANES) * LANES
RIM = SPLINE


def lower_pairs(order):
    return [(row_at, col_at) for row_at in range(order) for col_at in range(row_at + 1)]


def rows_of(order):
    return -(-(order + len(lower_pairs(order))) // 8) * 8


def split_rows(value):
    high = value.astype(BF16).astype(F32)
    return jnp.concatenate([high, value - high], axis=0).astype(BF16)


def dot_nt(left, right):
    return lax.dot_general(left, right, (((1,), (1,)), ((), ())), preferred_element_type=F32)


def dot_nn(left, right):
    return lax.dot_general(left, right, (((1,), (0,)), ((), ())), preferred_element_type=F32)


def in_groups(count, size, body, carry, first=None):
    if count <= 16:
        start = 0
        while start < count:
            end = min(start + (first if first and not start else size), count)
            carry = body(list(range(start, end)), carry)
            start = end
        return carry
    size = size if count % size == 0 else 1

    def group(number, carry):
        return body([number * size + at for at in range(size)], carry)

    return lax.fori_loop(0, count // size, group, carry)


def in_turns(totals, values):
    totals = list(totals)
    for number, value in enumerate(values):
        totals[number % 2] = totals[number % 2] + value
    return tuple(totals)


def add_all(values):
    values = list(values)
    while len(values) > 1:
        values = [
            values[at] + values[at + 1] if at + 1 < len(values) else values[at]
            for at in range(0, len(values), 2)
        ]
    return values[0]


def each(count, body, carry):
    if count <= 16:
        for number in range(count):
            carry = body(number, carry)
        return carry
    return lax.fori_loop(0, count, body, carry)


def block_solve(sums, order):
    pairs = lower_pairs(order)
    matrix = {}
    for number, (row_at, col_at) in enumerate(pairs):
        at = order + number
        matrix[row_at, col_at] = sums[at : at + 1] + (ridge if row_at == col_at else 0.0)
    right = [sums[at : at + 1] for at in range(order)]
    inverse = []
    for pivot in range(order):
        inverse.append(1.0 / matrix[pivot, pivot])
        for row_at in range(pivot + 1, order):
            ratio = matrix[row_at, pivot] * inverse[pivot]
            for col_at in range(pivot + 1, row_at + 1):
                matrix[row_at, col_at] = matrix[row_at, col_at] - ratio * matrix[col_at, pivot]
            right[row_at] = right[row_at] - ratio * right[pivot]
    solved = [None] * order
    for row_at in reversed(range(order)):
        running = right[row_at]
        for inner_at in range(row_at + 1, order):
            running = running - matrix[inner_at, row_at] * solved[inner_at]
        solved[row_at] = running * inverse[row_at]
    return jnp.concatenate(solved, axis=0)


def store_products(partials_ref, prods, order):
    values = [partials_ref[at].astype(F32) for at in range(order)]
    listed = values + [values[row_at] * values[col_at] for row_at, col_at in lower_pairs(order)]
    while len(listed) < prods.shape[1]:
        listed.append(jnp.zeros_like(values[0]))
    for at, value in enumerate(listed):
        prods[:, at, :] = value


def kernel(
    n_sky,
    n_tm,
    res_hbm,
    cnt_hbm,
    src_hbm,
    sp_hbm,
    seg_hbm,
    ap_hbm,
    unit_hbm,
    base_hbm,
    cp_hbm,
    out_ref,
    srcp_ref,
    attp_ref,
    res_ref,
    cnt_ref,
    src_ref,
    sp_ref,
    seg_ref,
    ap_ref,
    unit_ref,
    base_ref,
    cp_ref,
    in_sems,
    src_hot,
    seg_hot,
    src_side,
    seg_side,
    unit_hot,
    placed,
    sq_high,
    sq_low,
    rim_part,
    rim_square,
    src_prods,
    att_prods,
    cal_rows,
    r_src,
    r_time,
    v_time,
    live_time,
    fit_time,
    stat_send,
    stat_recv,
    abs_send,
    abs_recv,
    fwd_send,
    fwd_recv,
    back_send,
    back_recv,
    rim_send,
    rim_recv,
    stat_sems,
    abs_sems,
    fwd_ssem,
    fwd_rsem,
    back_ssem,
    back_rsem,
    rim_ssem,
    rim_rsem,
):
    zones, cap = res_ref.shape
    tiles = cap // LANES
    devices = n_sky * n_tm
    sky = lax.axis_index("sky")
    tm = lax.axis_index("tm")
    me = sky * n_tm + tm

    def wrapped(value, size):
        return jnp.where(value >= size, value - size, value)

    lower = sky < n_sky // 2

    def far_first(number):
        down = n_sky - 1 - number
        down = jnp.where(down <= sky, down - 1, down)
        up = jnp.where(number >= sky, number + 1, number)
        peer = jnp.where(lower, down, up)
        if isinstance(number, int):
            return sky if number == n_sky - 1 else peer
        return jnp.where(number == n_sky - 1, sky, peer)

    def every_other(body, after=None):
        if devices <= 64:
            if n_tm & (n_tm - 1):
                tms = [wrapped(tm + at, n_tm) for at in range(n_tm)]
            else:
                tms = [tm ^ at for at in range(n_tm)]
            for number in range(n_sky):
                other = far_first(number)
                for at in reversed(range(n_tm)):
                    if number < n_sky - 1 or at:
                        body(other, tms[at])
                if after and number < n_sky - 1:
                    after(other)
            return

        @pl.loop(1, devices)
        def _(step):
            flat = lax.rem(me + step, devices)
            body(flat // n_tm, lax.rem(flat, n_tm))

        if after:
            each(n_sky - 1, lambda number, carry: (after(far_first(number)), carry)[1], 0)

    arriving = [
        pltpu.make_async_copy(source, target, in_sems.at[number])
        for number, (source, target) in enumerate(
            (
                (res_hbm, res_ref),
                (cnt_hbm, cnt_ref),
                (src_hbm, src_ref),
                (sp_hbm, sp_ref),
                (seg_hbm, seg_ref),
                (ap_hbm, ap_ref),
                (unit_hbm, unit_ref),
                (base_hbm, base_ref),
                (cp_hbm, cp_ref),
            )
        )
    ]
    for copy in arriving:
        copy.start()

    barrier = pltpu.get_barrier_semaphore()

    def greet(to_sky, to_tm):
        pl.semaphore_signal(
            barrier, inc=1, device_id={"sky": to_sky, "tm": to_tm}, device_id_type=MESH
        )

    every_other(greet)

    lane_row = lax.broadcasted_iota(jnp.int32, (1, cap), 1)

    def fold(row):
        total = row[:, :LANES]
        for at in range(1, tiles):
            total = total + row[:, at * LANES : (at + 1) * LANES]
        return total

    def widen(row):
        return jnp.concatenate([row] * tiles, axis=1) if tiles > 1 else row

    def live_of(zone):
        return (lane_row < cnt_ref[zone]).astype(F32)

    for copy in arriving[:2]:
        copy.wait()

    def first_stats(zone, carry):
        sums, lives = carry
        live = live_of(zone)
        row = res_ref[pl.ds(zone, 1), :] * live
        r_src[zone] = row
        stat_send[zone, :, 2 * LANES :] = jnp.full((1, LANES), cnt_ref[zone], jnp.int32).astype(F32)
        return sums + fold(jnp.abs(row)), lives + fold(live)

    zero_row = jnp.zeros((1, LANES), F32)
    sums, lives = each(zones, first_stats, (zero_row, zero_row))

    def put_stats(zone, carry):
        stat_send[zone, :, :LANES] = sums
        stat_send[zone, :, LANES : 2 * LANES] = lives
        return carry

    each(zones, put_stats, 0)
    stat_recv[me] = stat_send[sky]
    pl.semaphore_wait(barrier, devices - 1)

    def send_stats(to_sky, to_tm):
        pltpu.make_async_remote_copy(
            src_ref=stat_send.at[to_sky],
            dst_ref=stat_recv.at[me],
            send_sem=stat_sems.at[0],
            recv_sem=stat_sems.at[1],
            device_id={"sky": to_sky, "tm": to_tm},
            device_id_type=MESH,
        ).start()

    every_other(send_stats)

    for copy in arriving[2:]:
        copy.wait()

    store_products(sp_ref, src_prods, SRC_PARAMS)
    store_products(ap_ref, att_prods, ATT_PARAMS)
    for at in range(SPLINE):
        cal_rows[:, at, :] = cp_ref[at].astype(F32)

    def hot_rows(rows, labels):
        number = lax.broadcasted_iota(jnp.int32, (rows, cap), 0)
        return jnp.where(number == labels, 1.0, 0.0).astype(BF16)

    def tables(zone, carry):
        for labels_ref, hot_ref, side_ref in ((src_ref, src_hot, src_side), (seg_ref, seg_hot, seg_side)):
            labels = labels_ref[pl.ds(zone, 1), :]
            groups = hot_ref.shape[1]
            above = labels >= groups
            hot_ref[zone] = hot_rows(groups, jnp.where(above, labels - groups, labels))
            side_ref[zone] = jnp.where(above, 1.0, 0.0)
        hot = hot_rows(UNIT_ROWS, unit_ref[pl.ds(zone, 1), :])
        unit_hot[zone] = jnp.concatenate([hot, hot], axis=0)
        base = jnp.broadcast_to(base_ref[pl.ds(zone, 1), :], (8, cap))
        turned = []
        for part in range(SPLINE // 8):
            rows = cal_rows[zone, part * 8 : part * 8 + 8, :]
            for bit in (1, 2, 4):
                rows = jnp.where((base & bit) != 0, pltpu.roll(rows, bit, 0), rows)
            turned.append(rows)
        reach = lax.shift_right_arithmetic(
            lax.broadcasted_iota(jnp.int32, (8, cap), 0) - base, jnp.int32(3)
        )
        pieces = []
        for group in range(EXTENT // 8):
            piece = jnp.zeros((8, cap), F32)
            for part, rows in enumerate(turned):
                piece = jnp.where(reach == part - group, rows, piece)
            pieces.append(piece)
        spread = jnp.concatenate(pieces, axis=0)
        placed[zone] = spread.astype(BF16)
        square = spread * spread
        rim_part[zone] = jnp.concatenate([spread[:RIM], spread[EXTENT - RIM :]], axis=0)
        rim_square[zone] = jnp.concatenate([square[:RIM], square[EXTENT - RIM :]], axis=0)
        high = square.astype(BF16)
        sq_high[zone] = high
        sq_low[zone] = (square - high.astype(F32)).astype(BF16)
        return carry

    each(zones, tables, 0)

    whole_stat = stat_recv.at[pl.ds(0, devices - 1)]
    pltpu.make_async_copy(whole_stat, whole_stat, stat_sems.at[1]).wait()
    stats = jnp.sum(stat_recv[...], axis=0)
    live_total = jnp.sum(stats[:, LANES : 2 * LANES], axis=1, keepdims=True)
    abs_total = jnp.sum(stats[:, :LANES], axis=1, keepdims=True)

    def time_live(zone, carry):
        counts = stat_recv[zone * n_tm + tm][:, 2 * LANES :]
        live_time[zone] = (lane_row.astype(F32) < widen(counts)).astype(F32)
        return carry

    each(zones, time_live, 0)

    src_total = jnp.zeros((SRC_PARAMS, SRC_DEV), F32)
    att_total = jnp.zeros((ATT_PARAMS, SEG_DEV), F32)

    chunk = min(cap, 256) if cap % 256 == 0 else cap
    parts = [slice(at, at + chunk) for at in range(0, cap, chunk)]

    def group_sums(zone, prods, hot, side, order, weights, row):
        number = lax.broadcasted_iota(jnp.int32, (8, cap), 0)
        scaled = jnp.concatenate(
            [
                prods[zone, :8, :] * jnp.where(number < order, weights * row, weights),
                prods[zone, 8:, :] * weights,
            ],
            axis=0,
        )
        tall = split_rows(scaled)
        above = tall * side[zone].astype(BF16)
        return dot_nt(jnp.concatenate([tall - above, above], axis=0), hot[zone])

    def group_totals(both, order):
        rows = both[0].shape[0] // 4
        halves = []
        for at in (0, 2 * rows):
            low, high = slice(at, at + rows), slice(at + rows, at + 2 * rows)
            halves.append((both[0][low] + both[0][high]) + (both[1][low] + both[1][high]))
        return jnp.concatenate(halves, axis=1)

    def padded_steps(step, order):
        groups = step.shape[1]
        tall = split_rows(jnp.concatenate([step, jnp.zeros((8 - order, groups), F32)], axis=0))
        return jnp.concatenate([tall[:, : groups // 2], tall[:, groups // 2 :]], axis=0)

    def fitted(zones_at, steps, prods, hot, side):
        picked = [[dot_nn(steps, hot[zone, :, part]) for part in parts] for zone in zones_at]
        fits = []
        for zone, values_of in zip(zones_at, picked):
            fit = []
            for part, values in zip(parts, values_of):
                values = jnp.where(
                    side[zone, :, part] > 0.5, values[16:24] + values[24:], values[:8] + values[8:16]
                )
                fit.append(jnp.sum(values * prods[zone, :8, part], axis=0, keepdims=True))
            fits.append(jnp.concatenate(fit, axis=1) if len(fit) > 1 else fit[0])
        return fits

    def zone_copy(send, recv, ssem, rsem, peer):
        return pltpu.make_async_remote_copy(
            src_ref=send.at[peer],
            dst_ref=recv.at[sky],
            send_sem=ssem,
            recv_sem=rsem,
            device_id={"sky": peer, "tm": tm},
            device_id_type=MESH,
        )

    def rim_copy(it, way, kind):
        return pltpu.make_async_remote_copy(
            src_ref=rim_send.at[it, way, kind],
            dst_ref=rim_recv.at[it, way, kind],
            send_sem=rim_ssem.at[it, way, kind],
            recv_sem=rim_rsem.at[it, way, kind],
            device_id={"sky": sky, "tm": lax.rem(tm + (1, n_tm - 1)[way], n_tm)},
            device_id_type=MESH,
        )

    has_next, has_last = tm < n_tm - 1, tm > 0

    def to_rims(it, kind, act):
        for way, there in ((0, has_next), (1, has_last)):

            @pl.when(there)
            def _():
                act(rim_copy(it, way, kind))

    def from_rims(it, kind):
        for way, there in ((0, has_last), (1, has_next)):

            @pl.when(there)
            def _():
                rim_copy(it, way, kind).wait_recv()

    def send_rims(it, kind, rims):
        for way, rows in ((0, slice(RIM, 2 * RIM)), (1, slice(0, RIM))):
            rim_send[it, way, kind, :, :UNIT_ROWS] = rims[rows]
        to_rims(it, kind, lambda copy: copy.start())

    wide = 2 * UNIT_ROWS

    def unit_weights(zone, row):
        high = row.astype(BF16).astype(F32)
        tall = jnp.concatenate(
            [
                jnp.broadcast_to(high, (UNIT_ROWS, cap)),
                jnp.broadcast_to(row - high, (UNIT_ROWS, cap)),
            ],
            axis=0,
        ).astype(BF16)
        return unit_hot[zone] * tall

    for it in range(ITERS):
        bound = clip_factor * (abs_total / live_total)

        def src_sums(numbers, total):
            rows = [r_src[zone] for zone in numbers]
            weights = [
                live_of(zone) * bound / jnp.maximum(jnp.abs(row), bound)
                for zone, row in zip(numbers, rows)
            ]
            return in_turns(
                total,
                (group_sums(zone, src_prods, src_hot, src_side, SRC_PARAMS, weight, row)
                for zone, weight, row in zip(numbers, weights, rows)),
            )

        blank = jnp.zeros((4 * rows_of(SRC_PARAMS), SRC_DEV // 2), F32)
        both = in_groups(zones, 8, src_sums, (blank, blank))
        step_x = block_solve(group_totals(both, SRC_PARAMS), SRC_PARAMS)
        src_total = src_total + step_x
        steps_x = padded_steps(step_x, SRC_PARAMS)

        def src_out(numbers, carry):
            zones_at = [far_first(number) for number in numbers]
            fits = fitted(zones_at, steps_x, src_prods, src_hot, src_side)
            for zone, fit in zip(zones_at, fits):
                fwd_send[it, zone] = r_src[zone] - live_of(zone) * fit

            for number, zone in zip(numbers, zones_at):

                def send():
                    zone_copy(
                        fwd_send.at[it], fwd_recv.at[it], fwd_ssem.at[it], fwd_rsem.at[it, sky], zone
                    ).start()

                if isinstance(number, int):
                    if number < n_sky - 1:
                        send()
                else:
                    pl.when(number < n_sky - 1)(send)
            return carry

        in_groups(zones, 6, src_out, 0, first=2)
        fwd_recv[it, sky] = fwd_send[it, sky]

        def att_sums(numbers, total):
            zones_at = [far_first(n_sky - 1 - number) for number in numbers]
            for number, zone in zip(numbers, zones_at):

                def arrive():
                    zone_copy(
                        fwd_send.at[it], fwd_recv.at[it], fwd_ssem.at[it], fwd_rsem.at[it, zone], zone
                    ).wait_recv()

                if isinstance(number, int):
                    if number > 0:
                        arrive()
                else:
                    pl.when(number > 0)(arrive)
            rows = [fwd_recv[it, zone] for zone in zones_at]
            weights = [
                live_time[zone] * bound / jnp.maximum(jnp.abs(row), bound)
                for zone, row in zip(zones_at, rows)
            ]
            for zone, weight in zip(zones_at, weights):
                v_time[zone] = weight
            att_part, h_part = total
            att_part = in_turns(
                att_part,
                (
                    group_sums(zone, att_prods, seg_hot, seg_side, ATT_PARAMS, weight, row)
                    for zone, weight, row in zip(zones_at, weights, rows)
                ),
            )
            h_part = in_turns(
                h_part,
                (
                    dot_nt(split_rows(rim_square[zone] * weight), unit_hot[zone, :UNIT_ROWS, :])
                    for zone, weight in zip(zones_at, weights)
                ),
            )
            return att_part, h_part

        rim_blank = (jnp.zeros((4 * RIM, UNIT_ROWS), F32),) * 2
        blank = jnp.zeros((4 * rows_of(ATT_PARAMS), SEG_DEV // 2), F32)
        both, h_rims = in_groups(zones, 2, att_sums, ((blank, blank), rim_blank))

        def rim_total(sums):
            return add_all(half[at : at + 2 * RIM] for half in sums for at in (0, 2 * RIM))

        h_rims = rim_total(h_rims)
        step_y = block_solve(group_totals(both, ATT_PARAMS), ATT_PARAMS)
        att_total = att_total + step_y
        steps_y = padded_steps(step_y, ATT_PARAMS)

        send_rims(it, 1, h_rims)

        def rim_sums(numbers, total):
            fits = fitted(numbers, steps_y, att_prods, seg_hot, seg_side)
            rows = [
                fwd_recv[it, zone] - live_time[zone] * fit for zone, fit in zip(numbers, fits)
            ]
            for zone, row in zip(numbers, rows):
                r_time[zone] = row
            return in_turns(
                total,
                (
                    dot_nt(split_rows(rim_part[zone] * (v_time[zone] * row)), unit_hot[zone, :UNIT_ROWS, :])
                    for zone, row in zip(numbers, rows)
                ),
            )

        g_rims = in_groups(zones, 8, rim_sums, rim_blank)
        g_rims = rim_total(g_rims)

        def joined(g_part, h_part):
            g_part = g_part + pltpu.roll(g_part, UNIT_ROWS, 1)
            left_half = lax.broadcasted_iota(jnp.int32, g_part.shape, 1) < UNIT_ROWS
            return jnp.where(left_half, g_part, h_part)

        def coefs_of(knots):
            ratio = knots / (pltpu.roll(knots, UNIT_ROWS, 1) + ridge)
            left_half = lax.broadcasted_iota(jnp.int32, knots.shape, 1) < UNIT_ROWS
            ratio = jnp.where(left_half, ratio, 0.0)
            high = ratio.astype(BF16).astype(F32)
            return (high + pltpu.roll(ratio - high, UNIT_ROWS, 1)).astype(BF16)

        send_rims(it, 0, g_rims)
        inner = slice(RIM, EXTENT - RIM)

        def inner_sums(numbers, total):
            g_part, h_part = total
            for zone in numbers:
                weight = v_time[zone]
                tall = unit_weights(zone, weight)
                h_part = h_part + dot_nt(sq_high[zone, inner, :], tall) + dot_nt(sq_low[zone, inner, :], tall)
                g_part = g_part + dot_nt(placed[zone, inner, :], unit_weights(zone, weight * r_time[zone]))
            return g_part, h_part

        middle = jnp.zeros((EXTENT - 2 * RIM, wide), F32)
        middle, h_total = in_groups(zones, 8, inner_sums, (middle, middle))
        h_total = h_total + pltpu.roll(h_total, UNIT_ROWS, 1)
        inner_coefs = coefs_of(joined(middle, h_total))

        def inner_fit(zone, carry):
            picked = dot_nn(inner_coefs, unit_hot[zone])
            fit = picked * placed[zone, inner, :].astype(F32)
            fit_time[zone] = jnp.sum(fit.reshape(-1, 8, cap), axis=0)
            return carry

        each(zones, inner_fit, 0)

        for kind in (1, 0):
            from_rims(it, kind)
        lead = KNOT_DEV - (EXTENT - RIM)
        shared = SPLINE - 1
        from_last = jnp.where(tm > 0, rim_recv[it, 0], 0.0)[:, lead : lead + shared, :UNIT_ROWS]
        from_next = jnp.where(tm < n_tm - 1, rim_recv[it, 1], 0.0)[:, :shared, :UNIT_ROWS]

        def added(rims, at):
            blank = lambda rows: [jnp.zeros((rows, UNIT_ROWS), F32)] if rows else []
            return rims + jnp.concatenate(
                [from_last[at]]
                + blank(RIM - shared + lead)
                + [from_next[at]]
                + blank(RIM - lead - shared),
                axis=0,
            )

        rim_coefs = split_rows(added(g_rims, 0) / (added(h_rims, 1) + ridge))

        last = it == ITERS - 1

        def cal_out(numbers, total):
            picked = [dot_nn(rim_coefs, unit_hot[zone, :UNIT_ROWS, :]) for zone in numbers]
            rows = []
            for zone, values in zip(numbers, picked):
                fit = (values[: 2 * RIM] + values[2 * RIM :]) * rim_part[zone]
                fit = jnp.sum(fit.reshape(-1, 8, cap), axis=0) + fit_time[zone]
                fit = jnp.sum(fit, axis=0, keepdims=True)
                rows.append(r_time[zone] - live_time[zone] * fit)
            for zone, row in zip(numbers, rows):
                back_send[it, zone] = row
            return total + add_all(fold(jnp.abs(row)) for row in rows)

        abs_sum = in_groups(zones, 8, cal_out, zero_row)

        def back_out(peer):
            zone_copy(
                back_send.at[it], back_recv.at[it], back_ssem.at[it], back_rsem.at[it], peer
            ).start()

        if last:
            each(n_sky - 1, lambda number, carry: (back_out(far_first(number)), carry)[1], 0)
        else:
            abs_send[it] = abs_sum
            abs_recv[it, me] = abs_sum

            def send_abs(to_sky, to_tm):
                pltpu.make_async_remote_copy(
                    src_ref=abs_send.at[it],
                    dst_ref=abs_recv.at[it, me],
                    send_sem=abs_sems.at[it, 0],
                    recv_sem=abs_sems.at[it, 1],
                    device_id={"sky": to_sky, "tm": to_tm},
                    device_id_type=MESH,
                ).start()

            every_other(send_abs, back_out)

        back_recv[it, sky] = back_send[it, sky]

        if not last:
            whole = abs_recv.at[it, pl.ds(0, devices - 1)]
            pltpu.make_async_copy(whole, whole, abs_sems.at[it, 1]).wait()
            abs_total = jnp.sum(jnp.sum(abs_recv[it], axis=0), axis=1, keepdims=True)

        whole = back_recv.at[it, pl.ds(0, n_sky - 1)]
        pltpu.make_async_copy(whole, whole, back_rsem.at[it]).wait()

        def put_back(zone, carry):
            if last:
                out_ref[pl.ds(zone, 1), :] = back_recv[it, zone]
            else:
                r_src[zone] = back_recv[it, zone]
            return carry

        each(zones, put_back, 0)

    srcp_ref[...] = src_total
    attp_ref[...] = att_total

    pltpu.make_async_copy(whole_stat, whole_stat, stat_sems.at[0]).wait()
    for it in range(ITERS):
        if it < ITERS - 1:
            whole = abs_recv.at[it, pl.ds(0, devices - 1)]
            pltpu.make_async_copy(whole, whole, abs_sems.at[it, 0]).wait()

        for recv, ssem in ((fwd_recv, fwd_ssem), (back_recv, back_ssem)):
            whole = recv.at[it, pl.ds(0, n_sky - 1)]
            pltpu.make_async_copy(whole, whole, ssem.at[it]).wait()
        for kind in (1, 0):
            to_rims(it, kind, lambda copy: copy.wait_send())


def write_out(count, *refs):
    sems = refs[-1]
    copies = [
        pltpu.make_async_copy(refs[at], refs[count + at], sems.at[at]) for at in range(count)
    ]
    for copy in copies:
        copy.start()
    for copy in copies:
        copy.wait()


def shards(
    residual,
    counts,
    source_index,
    source_partials,
    segment_index,
    attitude_partials,
    unit_index,
    knot_base,
    calib_partials,
    n_sky,
    n_tm,
):
    zones, capacity = residual.shape[2:]
    cap = -(-capacity // LANES) * LANES
    devices = n_sky * n_tm

    def flat(value):
        value = value.reshape(value.shape[:-4] + (zones, capacity))
        if cap != capacity:
            value = jnp.pad(value, [(0, 0)] * (value.ndim - 1) + [(0, cap - capacity)])
        return value

    vmem = pl.BlockSpec(memory_space=pltpu.VMEM)
    row = lambda *lead: pltpu.VMEM(lead + (1, cap), F32)
    dma = pltpu.SemaphoreType.DMA
    result_bytes = 4 * (zones * cap + 8 * SRC_DEV + 8 * SEG_DEV)
    pinned = cap == capacity
    result = pltpu.VMEM if pinned else jax.ShapeDtypeStruct
    corrected, src_params, att_params = pl.pallas_call(
        functools.partial(kernel, n_sky, n_tm),
        out_shape=(
            result((zones, cap), F32),
            result((SRC_PARAMS, SRC_DEV), F32),
            result((ATT_PARAMS, SEG_DEV), F32),
        ),
        in_specs=[pl.BlockSpec(memory_space=pltpu.HBM)] * 9,
        out_specs=(vmem, vmem, vmem),
        scratch_shapes=[
            pltpu.VMEM((zones, cap), F32),
            pltpu.SMEM((zones,), jnp.int32),
            pltpu.VMEM((zones, cap), jnp.int32),
            pltpu.VMEM((SRC_PARAMS, zones, cap), BF16),
            pltpu.VMEM((zones, cap), jnp.int32),
            pltpu.VMEM((ATT_PARAMS, zones, cap), BF16),
            pltpu.VMEM((zones, cap), jnp.int32),
            pltpu.VMEM((zones, cap), jnp.int32),
            pltpu.VMEM((SPLINE, zones, cap), BF16),
            dma((9,)),
            pltpu.VMEM((zones, SRC_DEV // 2, cap), BF16),
            pltpu.VMEM((zones, SEG_DEV // 2, cap), BF16),
            row(zones),
            row(zones),
            pltpu.VMEM((zones, 2 * UNIT_ROWS, cap), BF16),
            pltpu.VMEM((zones, EXTENT, cap), BF16),
            pltpu.VMEM((zones, EXTENT, cap), BF16),
            pltpu.VMEM((zones, EXTENT, cap), BF16),
            pltpu.VMEM((zones, 2 * RIM, cap), F32),
            pltpu.VMEM((zones, 2 * RIM, cap), F32),
            pltpu.VMEM((zones, rows_of(SRC_PARAMS), cap), F32),
            pltpu.VMEM((zones, rows_of(ATT_PARAMS), cap), F32),
            pltpu.VMEM((zones, SPLINE, cap), F32),
            row(zones),
            row(zones),
            row(zones),
            row(zones),
            pltpu.VMEM((zones, 8, cap), F32),
            pltpu.VMEM((n_sky, 1, 3 * LANES), F32),
            pltpu.VMEM((devices, 1, 3 * LANES), F32),
            pltpu.VMEM((ITERS, 1, LANES), F32),
            pltpu.VMEM((ITERS, devices, 1, LANES), F32),
            row(ITERS, zones),
            row(ITERS, zones),
            row(ITERS, zones),
            row(ITERS, zones),
            pltpu.VMEM((ITERS, 2, 2, RIM, LANES), F32),
            pltpu.VMEM((ITERS, 2, 2, RIM, LANES), F32),
            dma((2,)),
            dma((ITERS, 2)),
            dma((ITERS,)),
            dma((ITERS, n_sky)),
            dma((ITERS,)),
            dma((ITERS,)),
            dma((ITERS, 2, 2)),
            dma((ITERS, 2, 2)),
        ],
        compiler_params=pltpu.CompilerParams(
            collective_id=0, has_side_effects=True, vmem_limit_bytes=67010000
        ),
        name="astrometry",
    )(
        flat(residual),
        counts.reshape(zones),
        flat(source_index),
        flat(source_partials),
        flat(segment_index),
        flat(attitude_partials),
        flat(unit_index),
        flat(knot_base),
        flat(calib_partials),
    )
    results = (corrected, src_params, att_params)
    if pinned:
        results = [pltpu.with_memory_space_constraint(value, pltpu.VMEM) for value in results]
    corrected, src_params, att_params = pl.pallas_call(
        functools.partial(write_out, len(results)),
        out_shape=tuple(jax.ShapeDtypeStruct(value.shape, value.dtype) for value in results),
        in_specs=[vmem] * len(results),
        out_specs=tuple(pl.BlockSpec(memory_space=pltpu.HBM) for _ in results),
        scratch_shapes=[dma((len(results),))],
        name="write_out",
    )(*results)
    return corrected[:, :capacity].reshape(1, 1, zones, capacity), src_params, att_params


def solution(mesh):
    return jax.shard_map(
        functools.partial(shards, n_sky=mesh.shape["sky"], n_tm=mesh.shape["tm"]),
        mesh=mesh,
        in_specs=(
            P("sky", "tm", None, None),
            P("sky", "tm", None),
            P("sky", "tm", None, None),
            P(None, "sky", "tm", None, None),
            P("sky", "tm", None, None),
            P(None, "sky", "tm", None, None),
            P("sky", "tm", None, None),
            P("sky", "tm", None, None),
            P(None, "sky", "tm", None, None),
        ),
        out_specs=(P("sky", "tm", None, None), P(None, ("sky", "tm")), P(None, ("sky", "tm"))),
        check_vma=False,
    )
```

```python
import functools

import jax
import jax.numpy as jnp
from jax import lax
from jax.experimental import pallas as pl
from jax.experimental.pallas import tpu as pltpu
from jax.sharding import PartitionSpec as P

SRC_DEV = 256
SEG_DEV = 128
KNOT_DEV = 113
UNITS = 62
SPLINE = 16
SRC_PARAMS = 5
ATT_PARAMS = 4
ITERS = 2

clip_factor = 1.5
ridge = 1.0

LANES = 128
F32 = jnp.float32
BF16 = jnp.bfloat16
MESH = pl.DeviceIdType.MESH
UNIT_ROWS = -(-UNITS // 64) * 64
EXTENT = -(-(KNOT_DEV + SPLINE - 1) // LANES) * LANES
RIM = SPLINE


def lower_pairs(order):
    return [(row_at, col_at) for row_at in range(order) for col_at in range(row_at + 1)]


def rows_of(order):
    return -(-(order + len(lower_pairs(order))) // 8) * 8


def split_rows(value):
    high = value.astype(BF16).astype(F32)
    return jnp.concatenate([high, value - high], axis=0).astype(BF16)


def dot_nt(left, right):
    return lax.dot_general(left, right, (((1,), (1,)), ((), ())), preferred_element_type=F32)


def dot_nn(left, right):
    return lax.dot_general(left, right, (((1,), (0,)), ((), ())), preferred_element_type=F32)


def in_groups(count, size, body, carry, first=None):
    if count <= 16:
        start = 0
        while start < count:
            end = min(start + (first if first and not start else size), count)
            carry = body(list(range(start, end)), carry)
            start = end
        return carry
    size = size if count % size == 0 else 1

    def group(number, carry):
        return body([number * size + at for at in range(size)], carry)

    return lax.fori_loop(0, count // size, group, carry)


def in_turns(totals, values):
    totals = list(totals)
    for number, value in enumerate(values):
        totals[number % 2] = totals[number % 2] + value
    return tuple(totals)


def add_all(values):
    values = list(values)
    while len(values) > 1:
        values = [
            values[at] + values[at + 1] if at + 1 < len(values) else values[at]
            for at in range(0, len(values), 2)
        ]
    return values[0]


def each(count, body, carry):
    if count <= 16:
        for number in range(count):
            carry = body(number, carry)
        return carry
    return lax.fori_loop(0, count, body, carry)


def block_solve(sums, order):
    pairs = lower_pairs(order)
    matrix = {}
    for number, (row_at, col_at) in enumerate(pairs):
        at = order + number
        matrix[row_at, col_at] = sums[at : at + 1] + (ridge if row_at == col_at else 0.0)
    right = [sums[at : at + 1] for at in range(order)]
    inverse = []
    for pivot in range(order):
        inverse.append(1.0 / matrix[pivot, pivot])
        for row_at in range(pivot + 1, order):
            ratio = matrix[row_at, pivot] * inverse[pivot]
            for col_at in range(pivot + 1, row_at + 1):
                matrix[row_at, col_at] = matrix[row_at, col_at] - ratio * matrix[col_at, pivot]
            right[row_at] = right[row_at] - ratio * right[pivot]
    solved = [None] * order
    for row_at in reversed(range(order)):
        running = right[row_at]
        for inner_at in range(row_at + 1, order):
            running = running - matrix[inner_at, row_at] * solved[inner_at]
        solved[row_at] = running * inverse[row_at]
    return jnp.concatenate(solved, axis=0)


def store_products(partials_ref, prods, order):
    values = [partials_ref[at].astype(F32) for at in range(order)]
    listed = values + [values[row_at] * values[col_at] for row_at, col_at in lower_pairs(order)]
    while len(listed) < prods.shape[1]:
        listed.append(jnp.zeros_like(values[0]))
    for at, value in enumerate(listed):
        prods[:, at, :] = value


def kernel(
    n_sky,
    n_tm,
    res_hbm,
    cnt_hbm,
    src_hbm,
    sp_hbm,
    seg_hbm,
    ap_hbm,
    unit_hbm,
    base_hbm,
    cp_hbm,
    out_ref,
    srcp_ref,
    attp_ref,
    res_ref,
    cnt_ref,
    src_ref,
    sp_ref,
    seg_ref,
    ap_ref,
    unit_ref,
    base_ref,
    cp_ref,
    in_sems,
    src_hot,
    seg_hot,
    src_side,
    seg_side,
    unit_hot,
    placed,
    sq_high,
    sq_low,
    rim_part,
    rim_square,
    src_prods,
    att_prods,
    att_twice,
    cal_rows,
    r_src,
    r_time,
    v_time,
    live_time,
    fit_time,
    stat_send,
    stat_recv,
    abs_send,
    abs_recv,
    fwd_send,
    fwd_recv,
    back_send,
    back_recv,
    rim_send,
    rim_recv,
    stat_sems,
    abs_sems,
    fwd_ssem,
    fwd_rsem,
    back_ssem,
    back_rsem,
    rim_ssem,
    rim_rsem,
):
    zones, cap = res_ref.shape
    tiles = cap // LANES
    devices = n_sky * n_tm
    sky = lax.axis_index("sky")
    tm = lax.axis_index("tm")
    me = sky * n_tm + tm

    def wrapped(value, size):
        return jnp.where(value >= size, value - size, value)

    lower = sky < n_sky // 2

    def far_first(number):
        down = n_sky - 1 - number
        down = jnp.where(down <= sky, down - 1, down)
        up = jnp.where(number >= sky, number + 1, number)
        peer = jnp.where(lower, down, up)
        if isinstance(number, int):
            return sky if number == n_sky - 1 else peer
        return jnp.where(number == n_sky - 1, sky, peer)

    def every_other(body, after=None):
        if devices <= 64:
            if n_tm & (n_tm - 1):
                tms = [wrapped(tm + at, n_tm) for at in range(n_tm)]
            else:
                tms = [tm ^ at for at in range(n_tm)]
            for number in range(n_sky):
                other = far_first(number)
                for at in reversed(range(n_tm)):
                    if number < n_sky - 1 or at:
                        body(other, tms[at])
                if after and number < n_sky - 1:
                    after(other)
            return

        @pl.loop(1, devices)
        def _(step):
            flat = lax.rem(me + step, devices)
            body(flat // n_tm, lax.rem(flat, n_tm))

        if after:
            each(n_sky - 1, lambda number, carry: (after(far_first(number)), carry)[1], 0)

    arriving = [
        pltpu.make_async_copy(source, target, in_sems.at[number])
        for number, (source, target) in enumerate(
            (
                (res_hbm, res_ref),
                (cnt_hbm, cnt_ref),
                (src_hbm, src_ref),
                (sp_hbm, sp_ref),
                (seg_hbm, seg_ref),
                (ap_hbm, ap_ref),
                (unit_hbm, unit_ref),
                (base_hbm, base_ref),
                (cp_hbm, cp_ref),
            )
        )
    ]
    for copy in arriving:
        copy.start()

    barrier = pltpu.get_barrier_semaphore()

    def greet(to_sky, to_tm):
        pl.semaphore_signal(
            barrier, inc=1, device_id={"sky": to_sky, "tm": to_tm}, device_id_type=MESH
        )

    every_other(greet)

    lane_row = lax.broadcasted_iota(jnp.int32, (1, cap), 1)

    def fold(row):
        total = row[:, :LANES]
        for at in range(1, tiles):
            total = total + row[:, at * LANES : (at + 1) * LANES]
        return total

    def widen(row):
        return jnp.concatenate([row] * tiles, axis=1) if tiles > 1 else row

    def live_of(zone):
        return (lane_row < cnt_ref[zone]).astype(F32)

    for copy in arriving[:2]:
        copy.wait()

    def first_stats(zone, carry):
        sums, lives = carry
        live = live_of(zone)
        row = res_ref[pl.ds(zone, 1), :] * live
        r_src[zone] = row
        stat_send[zone, :, 2 * LANES :] = jnp.full((1, LANES), cnt_ref[zone], jnp.int32).astype(F32)
        return sums + fold(jnp.abs(row)), lives + fold(live)

    zero_row = jnp.zeros((1, LANES), F32)
    sums, lives = each(zones, first_stats, (zero_row, zero_row))

    def put_stats(zone, carry):
        stat_send[zone, :, :LANES] = sums
        stat_send[zone, :, LANES : 2 * LANES] = lives
        return carry

    each(zones, put_stats, 0)
    stat_recv[me] = stat_send[sky]
    pl.semaphore_wait(barrier, devices - 1)

    def send_stats(to_sky, to_tm):
        pltpu.make_async_remote_copy(
            src_ref=stat_send.at[to_sky],
            dst_ref=stat_recv.at[me],
            send_sem=stat_sems.at[0],
            recv_sem=stat_sems.at[1],
            device_id={"sky": to_sky, "tm": to_tm},
            device_id_type=MESH,
        ).start()

    every_other(send_stats)

    for copy in arriving[2:]:
        copy.wait()

    store_products(sp_ref, src_prods, SRC_PARAMS)
    store_products(ap_ref, att_prods, ATT_PARAMS)
    for at in range(2 * ATT_PARAMS):
        att_twice[:, at, :] = ap_ref[at % ATT_PARAMS].astype(F32)
    for at in range(SPLINE):
        cal_rows[:, at, :] = cp_ref[at].astype(F32)

    def hot_rows(rows, labels):
        number = lax.broadcasted_iota(jnp.int32, (rows, cap), 0)
        return jnp.where(number == labels, 1.0, 0.0).astype(BF16)

    def tables(zone, carry):
        for labels_ref, hot_ref, side_ref in ((src_ref, src_hot, src_side), (seg_ref, seg_hot, seg_side)):
            labels = labels_ref[pl.ds(zone, 1), :]
            groups = hot_ref.shape[1]
            above = labels >= groups
            hot_ref[zone] = hot_rows(groups, jnp.where(above, labels - groups, labels))
            side_ref[zone] = jnp.where(above, 1.0, 0.0)
        hot = hot_rows(UNIT_ROWS, unit_ref[pl.ds(zone, 1), :])
        unit_hot[zone] = jnp.concatenate([hot, hot], axis=0)
        base = jnp.broadcast_to(base_ref[pl.ds(zone, 1), :], (8, cap))
        turned = []
        for part in range(SPLINE // 8):
            rows = cal_rows[zone, part * 8 : part * 8 + 8, :]
            for bit in (1, 2, 4):
                rows = jnp.where((base & bit) != 0, pltpu.roll(rows, bit, 0), rows)
            turned.append(rows)
        reach = lax.shift_right_arithmetic(
            lax.broadcasted_iota(jnp.int32, (8, cap), 0) - base, jnp.int32(3)
        )
        pieces = []
        for group in range(EXTENT // 8):
            piece = jnp.zeros((8, cap), F32)
            for part, rows in enumerate(turned):
                piece = jnp.where(reach == part - group, rows, piece)
            pieces.append(piece)
        spread = jnp.concatenate(pieces, axis=0)
        placed[zone] = spread.astype(BF16)
        square = spread * spread
        rim_part[zone] = jnp.concatenate([spread[:RIM], spread[EXTENT - RIM :]], axis=0)
        rim_square[zone] = jnp.concatenate([square[:RIM], square[EXTENT - RIM :]], axis=0)
        high = square.astype(BF16)
        sq_high[zone] = high
        sq_low[zone] = (square - high.astype(F32)).astype(BF16)
        return carry

    each(zones, tables, 0)

    whole_stat = stat_recv.at[pl.ds(0, devices - 1)]
    pltpu.make_async_copy(whole_stat, whole_stat, stat_sems.at[1]).wait()
    stats = jnp.sum(stat_recv[...], axis=0)
    live_total = jnp.sum(stats[:, LANES : 2 * LANES], axis=1, keepdims=True)
    abs_total = jnp.sum(stats[:, :LANES], axis=1, keepdims=True)

    def time_live(zone, carry):
        counts = stat_recv[zone * n_tm + tm][:, 2 * LANES :]
        live_time[zone] = (lane_row.astype(F32) < widen(counts)).astype(F32)
        return carry

    each(zones, time_live, 0)

    src_total = jnp.zeros((SRC_PARAMS, SRC_DEV), F32)
    att_total = jnp.zeros((ATT_PARAMS, SEG_DEV), F32)

    chunk = min(cap, 256) if cap % 256 == 0 else cap
    parts = [slice(at, at + chunk) for at in range(0, cap, chunk)]

    def group_sums(zone, prods, hot, side, order, weights, row):
        number = lax.broadcasted_iota(jnp.int32, (8, cap), 0)
        scaled = jnp.concatenate(
            [
                prods[zone, :8, :] * jnp.where(number < order, weights * row, weights),
                prods[zone, 8:, :] * weights,
            ],
            axis=0,
        )
        tall = split_rows(scaled)
        above = tall * side[zone].astype(BF16)
        return dot_nt(jnp.concatenate([tall - above, above], axis=0), hot[zone])

    def group_totals(both, order):
        rows = both[0].shape[0] // 4
        halves = []
        for at in (0, 2 * rows):
            low, high = slice(at, at + rows), slice(at + rows, at + 2 * rows)
            halves.append((both[0][low] + both[0][high]) + (both[1][low] + both[1][high]))
        return jnp.concatenate(halves, axis=1)

    def padded_steps(step, order):
        groups = step.shape[1]
        tall = split_rows(jnp.concatenate([step, jnp.zeros((8 - order, groups), F32)], axis=0))
        return jnp.concatenate([tall[:, : groups // 2], tall[:, groups // 2 :]], axis=0)

    def att_steps(step):
        high = step.astype(BF16).astype(F32)
        tall = jnp.concatenate([high, step - high], axis=0)
        groups = step.shape[1] // 2
        return jnp.concatenate([tall[:, :groups], tall[:, groups:]], axis=0).astype(BF16)

    def att_fitted(zones_at, steps):
        picked = [[dot_nn(steps, seg_hot[zone, :, part]) for part in parts] for zone in zones_at]
        fits = []
        for zone, values_of in zip(zones_at, picked):
            fit = []
            for part, values in zip(parts, values_of):
                values = jnp.where(seg_side[zone, :, part] > 0.5, values[8:], values[:8])
                fit.append(jnp.sum(values * att_twice[zone, :, part], axis=0, keepdims=True))
            fits.append(jnp.concatenate(fit, axis=1) if len(fit) > 1 else fit[0])
        return fits

    def fitted(zones_at, steps, prods, hot, side):
        picked = [[dot_nn(steps, hot[zone, :, part]) for part in parts] for zone in zones_at]
        fits = []
        for zone, values_of in zip(zones_at, picked):
            fit = []
            for part, values in zip(parts, values_of):
                values = jnp.where(
                    side[zone, :, part] > 0.5, values[16:24] + values[24:], values[:8] + values[8:16]
                )
                fit.append(jnp.sum(values * prods[zone, :8, part], axis=0, keepdims=True))
            fits.append(jnp.concatenate(fit, axis=1) if len(fit) > 1 else fit[0])
        return fits

    def zone_copy(send, recv, ssem, rsem, peer):
        return pltpu.make_async_remote_copy(
            src_ref=send.at[peer],
            dst_ref=recv.at[sky],
            send_sem=ssem,
            recv_sem=rsem,
            device_id={"sky": peer, "tm": tm},
            device_id_type=MESH,
        )

    def rim_copy(it, way, kind):
        return pltpu.make_async_remote_copy(
            src_ref=rim_send.at[it, way, kind],
            dst_ref=rim_recv.at[it, way, kind],
            send_sem=rim_ssem.at[it, way, kind],
            recv_sem=rim_rsem.at[it, way, kind],
            device_id={"sky": sky, "tm": lax.rem(tm + (1, n_tm - 1)[way], n_tm)},
            device_id_type=MESH,
        )

    has_next, has_last = tm < n_tm - 1, tm > 0

    def to_rims(it, kind, act):
        for way, there in ((0, has_next), (1, has_last)):

            @pl.when(there)
            def _():
                act(rim_copy(it, way, kind))

    def from_rims(it, kind):
        for way, there in ((0, has_last), (1, has_next)):

            @pl.when(there)
            def _():
                rim_copy(it, way, kind).wait_recv()

    def send_rims(it, kind, rims):
        for way, rows in ((0, slice(RIM, 2 * RIM)), (1, slice(0, RIM))):
            rim_send[it, way, kind, :, :UNIT_ROWS] = rims[rows]
        to_rims(it, kind, lambda copy: copy.start())

    wide = 2 * UNIT_ROWS

    def unit_weights(zone, row):
        high = row.astype(BF16).astype(F32)
        tall = jnp.concatenate(
            [
                jnp.broadcast_to(high, (UNIT_ROWS, cap)),
                jnp.broadcast_to(row - high, (UNIT_ROWS, cap)),
            ],
            axis=0,
        ).astype(BF16)
        return unit_hot[zone] * tall

    for it in range(ITERS):
        bound = clip_factor * (abs_total / live_total)

        def src_sums(numbers, total):
            rows = [r_src[zone] for zone in numbers]
            weights = [
                live_of(zone) * bound / jnp.maximum(jnp.abs(row), bound)
                for zone, row in zip(numbers, rows)
            ]
            return in_turns(
                total,
                (group_sums(zone, src_prods, src_hot, src_side, SRC_PARAMS, weight, row)
                for zone, weight, row in zip(numbers, weights, rows)),
            )

        blank = jnp.zeros((4 * rows_of(SRC_PARAMS), SRC_DEV // 2), F32)
        both = in_groups(zones, 8, src_sums, (blank, blank))
        step_x = block_solve(group_totals(both, SRC_PARAMS), SRC_PARAMS)
        src_total = src_total + step_x
        steps_x = padded_steps(step_x, SRC_PARAMS)

        def src_out(numbers, carry):
            zones_at = [far_first(number) for number in numbers]
            fits = fitted(zones_at, steps_x, src_prods, src_hot, src_side)
            for zone, fit in zip(zones_at, fits):
                fwd_send[it, zone] = r_src[zone] - live_of(zone) * fit

            for number, zone in zip(numbers, zones_at):

                def send():
                    zone_copy(
                        fwd_send.at[it], fwd_recv.at[it], fwd_ssem.at[it], fwd_rsem.at[it, sky], zone
                    ).start()

                if isinstance(number, int):
                    if number < n_sky - 1:
                        send()
                else:
                    pl.when(number < n_sky - 1)(send)
            return carry

        in_groups(zones, 6, src_out, 0, first=2)
        fwd_recv[it, sky] = fwd_send[it, sky]

        def att_sums(numbers, total):
            zones_at = [far_first(n_sky - 1 - number) for number in numbers]
            for number, zone in zip(numbers, zones_at):

                def arrive():
                    zone_copy(
                        fwd_send.at[it], fwd_recv.at[it], fwd_ssem.at[it], fwd_rsem.at[it, zone], zone
                    ).wait_recv()

                if isinstance(number, int):
                    if number > 0:
                        arrive()
                else:
                    pl.when(number > 0)(arrive)
            rows = [fwd_recv[it, zone] for zone in zones_at]
            weights = [
                live_time[zone] * bound / jnp.maximum(jnp.abs(row), bound)
                for zone, row in zip(zones_at, rows)
            ]
            for zone, weight in zip(zones_at, weights):
                v_time[zone] = weight
            att_part, h_part = total
            att_part = in_turns(
                att_part,
                (
                    group_sums(zone, att_prods, seg_hot, seg_side, ATT_PARAMS, weight, row)
                    for zone, weight, row in zip(zones_at, weights, rows)
                ),
            )
            h_part = in_turns(
                h_part,
                (
                    dot_nt(split_rows(rim_square[zone] * weight), unit_hot[zone, :UNIT_ROWS, :])
                    for zone, weight in zip(zones_at, weights)
                ),
            )
            return att_part, h_part

        rim_blank = (jnp.zeros((4 * RIM, UNIT_ROWS), F32),) * 2
        blank = jnp.zeros((4 * rows_of(ATT_PARAMS), SEG_DEV // 2), F32)
        both, h_rims = in_groups(zones, 2, att_sums, ((blank, blank), rim_blank))

        def rim_total(sums):
            return add_all(half[at : at + 2 * RIM] for half in sums for at in (0, 2 * RIM))

        h_rims = rim_total(h_rims)
        step_y = block_solve(group_totals(both, ATT_PARAMS), ATT_PARAMS)
        att_total = att_total + step_y
        steps_y = att_steps(step_y)

        send_rims(it, 1, h_rims)

        def rim_sums(numbers, total):
            fits = att_fitted(numbers, steps_y)
            rows = [
                fwd_recv[it, zone] - live_time[zone] * fit for zone, fit in zip(numbers, fits)
            ]
            for zone, row in zip(numbers, rows):
                r_time[zone] = row
            return in_turns(
                total,
                (
                    dot_nt(split_rows(rim_part[zone] * (v_time[zone] * row)), unit_hot[zone, :UNIT_ROWS, :])
                    for zone, row in zip(numbers, rows)
                ),
            )

        g_rims = in_groups(zones, 8, rim_sums, rim_blank)
        g_rims = rim_total(g_rims)

        def joined(g_part, h_part):
            g_part = g_part + pltpu.roll(g_part, UNIT_ROWS, 1)
            left_half = lax.broadcasted_iota(jnp.int32, g_part.shape, 1) < UNIT_ROWS
            return jnp.where(left_half, g_part, h_part)

        def coefs_of(knots):
            ratio = knots / (pltpu.roll(knots, UNIT_ROWS, 1) + ridge)
            left_half = lax.broadcasted_iota(jnp.int32, knots.shape, 1) < UNIT_ROWS
            ratio = jnp.where(left_half, ratio, 0.0)
            high = ratio.astype(BF16).astype(F32)
            return (high + pltpu.roll(ratio - high, UNIT_ROWS, 1)).astype(BF16)

        send_rims(it, 0, g_rims)
        inner = slice(RIM, EXTENT - RIM)

        def inner_sums(numbers, total):
            g_part, h_part = total
            for zone in numbers:
                weight = v_time[zone]
                tall = unit_weights(zone, weight)
                h_part = h_part + dot_nt(sq_high[zone, inner, :], tall) + dot_nt(sq_low[zone, inner, :], tall)
                g_part = g_part + dot_nt(placed[zone, inner, :], unit_weights(zone, weight * r_time[zone]))
            return g_part, h_part

        middle = jnp.zeros((EXTENT - 2 * RIM, wide), F32)
        middle, h_total = in_groups(zones, 8, inner_sums, (middle, middle))
        h_total = h_total + pltpu.roll(h_total, UNIT_ROWS, 1)
        inner_coefs = coefs_of(joined(middle, h_total))

        def inner_fit(zone, carry):
            picked = dot_nn(inner_coefs, unit_hot[zone])
            fit = picked * placed[zone, inner, :].astype(F32)
            fit_time[zone] = jnp.sum(fit.reshape(-1, 8, cap), axis=0)
            return carry

        each(zones, inner_fit, 0)

        for kind in (1, 0):
            from_rims(it, kind)
        lead = KNOT_DEV - (EXTENT - RIM)
        shared = SPLINE - 1
        from_last = jnp.where(tm > 0, rim_recv[it, 0], 0.0)[:, lead : lead + shared, :UNIT_ROWS]
        from_next = jnp.where(tm < n_tm - 1, rim_recv[it, 1], 0.0)[:, :shared, :UNIT_ROWS]

        def added(rims, at):
            blank = lambda rows: [jnp.zeros((rows, UNIT_ROWS), F32)] if rows else []
            return rims + jnp.concatenate(
                [from_last[at]]
                + blank(RIM - shared + lead)
                + [from_next[at]]
                + blank(RIM - lead - shared),
                axis=0,
            )

        rim_coefs = split_rows(added(g_rims, 0) / (added(h_rims, 1) + ridge))

        last = it == ITERS - 1

        def back_out(peer):
            zone_copy(
                back_send.at[it], back_recv.at[it], back_ssem.at[it], back_rsem.at[it], peer
            ).start()

        def cal_out(numbers, total):
            zones_at = [far_first(number) for number in numbers] if last else numbers
            picked = [dot_nn(rim_coefs, unit_hot[zone, :UNIT_ROWS, :]) for zone in zones_at]
            rows = []
            for zone, values in zip(zones_at, picked):
                fit = (values[: 2 * RIM] + values[2 * RIM :]) * rim_part[zone]
                fit = jnp.sum(fit.reshape(-1, 8, cap), axis=0) + fit_time[zone]
                fit = jnp.sum(fit, axis=0, keepdims=True)
                rows.append(r_time[zone] - live_time[zone] * fit)
            for zone, row in zip(zones_at, rows):
                back_send[it, zone] = row
            if not last:
                return total + add_all(fold(jnp.abs(row)) for row in rows)
            for number, zone in zip(numbers, zones_at):
                if isinstance(number, int):
                    if number < n_sky - 1:
                        back_out(zone)
                else:
                    pl.when(number < n_sky - 1)(functools.partial(back_out, zone))
            return total

        if last:
            in_groups(zones, 6, cal_out, zero_row, first=2)
            srcp_ref[...] = src_total
            attp_ref[...] = att_total
        else:
            abs_sum = in_groups(zones, 8, cal_out, zero_row)
            abs_send[it] = abs_sum
            abs_recv[it, me] = abs_sum

            def send_abs(to_sky, to_tm):
                pltpu.make_async_remote_copy(
                    src_ref=abs_send.at[it],
                    dst_ref=abs_recv.at[it, me],
                    send_sem=abs_sems.at[it, 0],
                    recv_sem=abs_sems.at[it, 1],
                    device_id={"sky": to_sky, "tm": to_tm},
                    device_id_type=MESH,
                ).start()

            every_other(send_abs, back_out)

        back_recv[it, sky] = back_send[it, sky]

        if not last:
            whole = abs_recv.at[it, pl.ds(0, devices - 1)]
            pltpu.make_async_copy(whole, whole, abs_sems.at[it, 1]).wait()
            abs_total = jnp.sum(jnp.sum(abs_recv[it], axis=0), axis=1, keepdims=True)

        whole = back_recv.at[it, pl.ds(0, n_sky - 1)]
        pltpu.make_async_copy(whole, whole, back_rsem.at[it]).wait()

        def put_back(zone, carry):
            if last:
                out_ref[pl.ds(zone, 1), :] = back_recv[it, zone]
            else:
                r_src[zone] = back_recv[it, zone]
            return carry

        each(zones, put_back, 0)

    pltpu.make_async_copy(whole_stat, whole_stat, stat_sems.at[0]).wait()
    for it in range(ITERS):
        if it < ITERS - 1:
            whole = abs_recv.at[it, pl.ds(0, devices - 1)]
            pltpu.make_async_copy(whole, whole, abs_sems.at[it, 0]).wait()

        for recv, ssem in ((fwd_recv, fwd_ssem), (back_recv, back_ssem)):
            whole = recv.at[it, pl.ds(0, n_sky - 1)]
            pltpu.make_async_copy(whole, whole, ssem.at[it]).wait()
        for kind in (1, 0):
            to_rims(it, kind, lambda copy: copy.wait_send())


def write_out(count, *refs):
    sems = refs[-1]
    copies = [
        pltpu.make_async_copy(refs[at], refs[count + at], sems.at[at]) for at in range(count)
    ]
    for copy in copies:
        copy.start()
    for copy in copies:
        copy.wait()


def shards(
    residual,
    counts,
    source_index,
    source_partials,
    segment_index,
    attitude_partials,
    unit_index,
    knot_base,
    calib_partials,
    n_sky,
    n_tm,
):
    zones, capacity = residual.shape[2:]
    cap = -(-capacity // LANES) * LANES
    devices = n_sky * n_tm

    def flat(value):
        value = value.reshape(value.shape[:-4] + (zones, capacity))
        if cap != capacity:
            value = jnp.pad(value, [(0, 0)] * (value.ndim - 1) + [(0, cap - capacity)])
        return value

    vmem = pl.BlockSpec(memory_space=pltpu.VMEM)
    row = lambda *lead: pltpu.VMEM(lead + (1, cap), F32)
    dma = pltpu.SemaphoreType.DMA
    result_bytes = 4 * (zones * cap + 8 * SRC_DEV + 8 * SEG_DEV)
    pinned = cap == capacity
    result = pltpu.VMEM if pinned else jax.ShapeDtypeStruct
    corrected, src_params, att_params = pl.pallas_call(
        functools.partial(kernel, n_sky, n_tm),
        out_shape=(
            result((zones, cap), F32),
            result((SRC_PARAMS, SRC_DEV), F32),
            result((ATT_PARAMS, SEG_DEV), F32),
        ),
        in_specs=[pl.BlockSpec(memory_space=pltpu.HBM)] * 9,
        out_specs=(vmem, vmem, vmem),
        scratch_shapes=[
            pltpu.VMEM((zones, cap), F32),
            pltpu.SMEM((zones,), jnp.int32),
            pltpu.VMEM((zones, cap), jnp.int32),
            pltpu.VMEM((SRC_PARAMS, zones, cap), BF16),
            pltpu.VMEM((zones, cap), jnp.int32),
            pltpu.VMEM((ATT_PARAMS, zones, cap), BF16),
            pltpu.VMEM((zones, cap), jnp.int32),
            pltpu.VMEM((zones, cap), jnp.int32),
            pltpu.VMEM((SPLINE, zones, cap), BF16),
            dma((9,)),
            pltpu.VMEM((zones, SRC_DEV // 2, cap), BF16),
            pltpu.VMEM((zones, SEG_DEV // 2, cap), BF16),
            row(zones),
            row(zones),
            pltpu.VMEM((zones, 2 * UNIT_ROWS, cap), BF16),
            pltpu.VMEM((zones, EXTENT, cap), BF16),
            pltpu.VMEM((zones, EXTENT, cap), BF16),
            pltpu.VMEM((zones, EXTENT, cap), BF16),
            pltpu.VMEM((zones, 2 * RIM, cap), F32),
            pltpu.VMEM((zones, 2 * RIM, cap), F32),
            pltpu.VMEM((zones, rows_of(SRC_PARAMS), cap), F32),
            pltpu.VMEM((zones, rows_of(ATT_PARAMS), cap), F32),
            pltpu.VMEM((zones, 2 * ATT_PARAMS, cap), F32),
            pltpu.VMEM((zones, SPLINE, cap), F32),
            row(zones),
            row(zones),
            row(zones),
            row(zones),
            pltpu.VMEM((zones, 8, cap), F32),
            pltpu.VMEM((n_sky, 1, 3 * LANES), F32),
            pltpu.VMEM((devices, 1, 3 * LANES), F32),
            pltpu.VMEM((ITERS, 1, LANES), F32),
            pltpu.VMEM((ITERS, devices, 1, LANES), F32),
            row(ITERS, zones),
            row(ITERS, zones),
            row(ITERS, zones),
            row(ITERS, zones),
            pltpu.VMEM((ITERS, 2, 2, RIM, LANES), F32),
            pltpu.VMEM((ITERS, 2, 2, RIM, LANES), F32),
            dma((2,)),
            dma((ITERS, 2)),
            dma((ITERS,)),
            dma((ITERS, n_sky)),
            dma((ITERS,)),
            dma((ITERS,)),
            dma((ITERS, 2, 2)),
            dma((ITERS, 2, 2)),
        ],
        compiler_params=pltpu.CompilerParams(
            collective_id=0, has_side_effects=True, vmem_limit_bytes=67010000
        ),
        name="astrometry",
    )(
        flat(residual),
        counts.reshape(zones),
        flat(source_index),
        flat(source_partials),
        flat(segment_index),
        flat(attitude_partials),
        flat(unit_index),
        flat(knot_base),
        flat(calib_partials),
    )
    results = (corrected, src_params, att_params)
    if pinned:
        results = [pltpu.with_memory_space_constraint(value, pltpu.VMEM) for value in results]
    corrected, src_params, att_params = pl.pallas_call(
        functools.partial(write_out, len(results)),
        out_shape=tuple(jax.ShapeDtypeStruct(value.shape, value.dtype) for value in results),
        in_specs=[vmem] * len(results),
        out_specs=tuple(pl.BlockSpec(memory_space=pltpu.HBM) for _ in results),
        scratch_shapes=[dma((len(results),))],
        name="write_out",
    )(*results)
    return corrected[:, :capacity].reshape(1, 1, zones, capacity), src_params, att_params


def solution(mesh):
    return jax.shard_map(
        functools.partial(shards, n_sky=mesh.shape["sky"], n_tm=mesh.shape["tm"]),
        mesh=mesh,
        in_specs=(
            P("sky", "tm", None, None),
            P("sky", "tm", None),
            P("sky", "tm", None, None),
            P(None, "sky", "tm", None, None),
            P("sky", "tm", None, None),
            P(None, "sky", "tm", None, None),
            P("sky", "tm", None, None),
            P("sky", "tm", None, None),
            P(None, "sky", "tm", None, None),
        ),
        out_specs=(P("sky", "tm", None, None), P(None, ("sky", "tm")), P(None, ("sky", "tm"))),
        check_vma=False,
    )
```

```python
import functools

import jax
import jax.numpy as jnp
from jax import lax
from jax.experimental import pallas as pl
from jax.experimental.pallas import tpu as pltpu
from jax.sharding import PartitionSpec as P

SRC_DEV = 256
SEG_DEV = 128
KNOT_DEV = 113
UNITS = 62
SPLINE = 16
SRC_PARAMS = 5
ATT_PARAMS = 4
ITERS = 2

clip_factor = 1.5
ridge = 1.0

LANES = 128
F32 = jnp.float32
BF16 = jnp.bfloat16
MESH = pl.DeviceIdType.MESH
UNIT_ROWS = -(-UNITS // 64) * 64
EXTENT = -(-(KNOT_DEV + SPLINE - 1) // LANES) * LANES
RIM = SPLINE


def lower_pairs(order):
    return [(row_at, col_at) for row_at in range(order) for col_at in range(row_at + 1)]


def rows_of(order):
    return -(-(order + len(lower_pairs(order))) // 8) * 8


def split_rows(value):
    high = value.astype(BF16).astype(F32)
    return jnp.concatenate([high, value - high], axis=0).astype(BF16)


def dot_nt(left, right):
    return lax.dot_general(left, right, (((1,), (1,)), ((), ())), preferred_element_type=F32)


def dot_nn(left, right):
    return lax.dot_general(left, right, (((1,), (0,)), ((), ())), preferred_element_type=F32)


def in_groups(count, size, body, carry, first=None):
    if count <= 16:
        start = 0
        while start < count:
            end = min(start + (first if first and not start else size), count)
            carry = body(list(range(start, end)), carry)
            start = end
        return carry
    size = size if count % size == 0 else 1

    def group(number, carry):
        return body([number * size + at for at in range(size)], carry)

    return lax.fori_loop(0, count // size, group, carry)


def in_turns(totals, values):
    totals = list(totals)
    for number, value in enumerate(values):
        totals[number % 2] = totals[number % 2] + value
    return tuple(totals)


def add_all(values):
    values = list(values)
    while len(values) > 1:
        values = [
            values[at] + values[at + 1] if at + 1 < len(values) else values[at]
            for at in range(0, len(values), 2)
        ]
    return values[0]


def each(count, body, carry):
    if count <= 16:
        for number in range(count):
            carry = body(number, carry)
        return carry
    return lax.fori_loop(0, count, body, carry)


def block_solve(sums, order):
    pairs = lower_pairs(order)
    matrix = {}
    for number, (row_at, col_at) in enumerate(pairs):
        at = order + number
        matrix[row_at, col_at] = sums[at : at + 1] + (ridge if row_at == col_at else 0.0)
    right = [sums[at : at + 1] for at in range(order)]
    inverse = []
    for pivot in range(order):
        inverse.append(1.0 / matrix[pivot, pivot])
        for row_at in range(pivot + 1, order):
            ratio = matrix[row_at, pivot] * inverse[pivot]
            for col_at in range(pivot + 1, row_at + 1):
                matrix[row_at, col_at] = matrix[row_at, col_at] - ratio * matrix[col_at, pivot]
            right[row_at] = right[row_at] - ratio * right[pivot]
    solved = [None] * order
    for row_at in reversed(range(order)):
        running = right[row_at]
        for inner_at in range(row_at + 1, order):
            running = running - matrix[inner_at, row_at] * solved[inner_at]
        solved[row_at] = running * inverse[row_at]
    return jnp.concatenate(solved, axis=0)


def store_products(partials_ref, prods, order):
    values = [partials_ref[at].astype(F32) for at in range(order)]
    listed = values + [values[row_at] * values[col_at] for row_at, col_at in lower_pairs(order)]
    while len(listed) < prods.shape[1]:
        listed.append(jnp.zeros_like(values[0]))
    for at, value in enumerate(listed):
        prods[:, at, :] = value


def kernel(
    n_sky,
    n_tm,
    res_hbm,
    cnt_hbm,
    src_hbm,
    sp_hbm,
    seg_hbm,
    ap_hbm,
    unit_hbm,
    base_hbm,
    cp_hbm,
    out_ref,
    srcp_ref,
    attp_ref,
    res_ref,
    cnt_ref,
    src_ref,
    sp_ref,
    seg_ref,
    ap_ref,
    unit_ref,
    base_ref,
    cp_ref,
    in_sems,
    src_hot,
    seg_hot,
    src_side,
    seg_side,
    src_mask,
    seg_mask,
    src_lead,
    unit_hot,
    placed,
    sq_high,
    sq_low,
    rim_part,
    rim_square,
    src_prods,
    att_prods,
    att_twice,
    cal_rows,
    r_src,
    r_time,
    v_time,
    live_time,
    fit_time,
    stat_send,
    stat_recv,
    abs_send,
    abs_recv,
    fwd_send,
    fwd_recv,
    back_send,
    back_recv,
    rim_send,
    rim_recv,
    stat_sems,
    abs_sems,
    fwd_ssem,
    fwd_rsem,
    back_ssem,
    back_rsem,
    rim_ssem,
    rim_rsem,
):
    zones, cap = res_ref.shape
    tiles = cap // LANES
    devices = n_sky * n_tm
    sky = lax.axis_index("sky")
    tm = lax.axis_index("tm")
    me = sky * n_tm + tm

    def wrapped(value, size):
        return jnp.where(value >= size, value - size, value)

    lower = sky < n_sky // 2

    def far_first(number):
        down = n_sky - 1 - number
        down = jnp.where(down <= sky, down - 1, down)
        up = jnp.where(number >= sky, number + 1, number)
        peer = jnp.where(lower, down, up)
        if isinstance(number, int):
            return sky if number == n_sky - 1 else peer
        return jnp.where(number == n_sky - 1, sky, peer)

    def every_other(body, after=None):
        if devices <= 64:
            if n_tm & (n_tm - 1):
                tms = [wrapped(tm + at, n_tm) for at in range(n_tm)]
            else:
                tms = [tm ^ at for at in range(n_tm)]
            for number in range(n_sky):
                other = far_first(number)
                for at in reversed(range(n_tm)):
                    if number < n_sky - 1 or at:
                        body(other, tms[at])
                if after and number < n_sky - 1:
                    after(other)
            return

        @pl.loop(1, devices)
        def _(step):
            flat = lax.rem(me + step, devices)
            body(flat // n_tm, lax.rem(flat, n_tm))

        if after:
            each(n_sky - 1, lambda number, carry: (after(far_first(number)), carry)[1], 0)

    arriving = [
        pltpu.make_async_copy(source, target, in_sems.at[number])
        for number, (source, target) in enumerate(
            (
                (res_hbm, res_ref),
                (cnt_hbm, cnt_ref),
                (src_hbm, src_ref),
                (sp_hbm, sp_ref),
                (seg_hbm, seg_ref),
                (ap_hbm, ap_ref),
                (unit_hbm, unit_ref),
                (base_hbm, base_ref),
                (cp_hbm, cp_ref),
            )
        )
    ]
    for copy in arriving:
        copy.start()

    barrier = pltpu.get_barrier_semaphore()

    def greet(to_sky, to_tm):
        pl.semaphore_signal(
            barrier, inc=1, device_id={"sky": to_sky, "tm": to_tm}, device_id_type=MESH
        )

    every_other(greet)

    lane_row = lax.broadcasted_iota(jnp.int32, (1, cap), 1)

    def fold(row):
        total = row[:, :LANES]
        for at in range(1, tiles):
            total = total + row[:, at * LANES : (at + 1) * LANES]
        return total

    def widen(row):
        return jnp.concatenate([row] * tiles, axis=1) if tiles > 1 else row

    def live_of(zone):
        return (lane_row < cnt_ref[zone]).astype(F32)

    for copy in arriving[:2]:
        copy.wait()

    def first_stats(zone, carry):
        sums, lives = carry
        live = live_of(zone)
        row = res_ref[pl.ds(zone, 1), :] * live
        r_src[zone] = row
        stat_send[zone, :, 2 * LANES :] = jnp.full((1, LANES), cnt_ref[zone], jnp.int32).astype(F32)
        return sums + fold(jnp.abs(row)), lives + fold(live)

    zero_row = jnp.zeros((1, LANES), F32)
    sums, lives = each(zones, first_stats, (zero_row, zero_row))

    def put_stats(zone, carry):
        stat_send[zone, :, :LANES] = sums
        stat_send[zone, :, LANES : 2 * LANES] = lives
        return carry

    each(zones, put_stats, 0)
    stat_recv[me] = stat_send[sky]
    pl.semaphore_wait(barrier, devices - 1)

    def send_stats(to_sky, to_tm):
        pltpu.make_async_remote_copy(
            src_ref=stat_send.at[to_sky],
            dst_ref=stat_recv.at[me],
            send_sem=stat_sems.at[0],
            recv_sem=stat_sems.at[1],
            device_id={"sky": to_sky, "tm": to_tm},
            device_id_type=MESH,
        ).start()

    every_other(send_stats)

    for copy in arriving[2:]:
        copy.wait()

    store_products(sp_ref, src_prods, SRC_PARAMS)
    store_products(ap_ref, att_prods, ATT_PARAMS)
    for at in range(2 * ATT_PARAMS):
        att_twice[:, at, :] = ap_ref[at % ATT_PARAMS].astype(F32)
    for at in range(SPLINE):
        cal_rows[:, at, :] = cp_ref[at].astype(F32)

    def hot_rows(rows, labels):
        number = lax.broadcasted_iota(jnp.int32, (rows, cap), 0)
        return jnp.where(number == labels, 1.0, 0.0).astype(BF16)

    def tables(zone, carry):
        for labels_ref, hot_ref, side_ref, mask_ref in (
            (src_ref, src_hot, src_side, src_mask),
            (seg_ref, seg_hot, seg_side, seg_mask),
        ):
            labels = labels_ref[pl.ds(zone, 1), :]
            groups = hot_ref.shape[1]
            above = labels >= groups
            hot_ref[zone] = hot_rows(groups, jnp.where(above, labels - groups, labels))
            side = jnp.where(above, 1.0, 0.0)
            side_ref[zone] = side
            mask_ref[zone] = jnp.broadcast_to(side, (16, cap)).astype(BF16)
        hot = hot_rows(UNIT_ROWS, unit_ref[pl.ds(zone, 1), :])
        unit_hot[zone] = jnp.concatenate([hot, hot], axis=0)
        base = jnp.broadcast_to(base_ref[pl.ds(zone, 1), :], (8, cap))
        turned = []
        for part in range(SPLINE // 8):
            rows = cal_rows[zone, part * 8 : part * 8 + 8, :]
            for bit in (1, 2, 4):
                rows = jnp.where((base & bit) != 0, pltpu.roll(rows, bit, 0), rows)
            turned.append(rows)
        reach = lax.shift_right_arithmetic(
            lax.broadcasted_iota(jnp.int32, (8, cap), 0) - base, jnp.int32(3)
        )
        pieces = []
        for group in range(EXTENT // 8):
            piece = jnp.zeros((8, cap), F32)
            for part, rows in enumerate(turned):
                piece = jnp.where(reach == part - group, rows, piece)
            pieces.append(piece)
        spread = jnp.concatenate(pieces, axis=0)
        placed[zone] = spread.astype(BF16)
        square = spread * spread
        rim_part[zone] = jnp.concatenate([spread[:RIM], spread[EXTENT - RIM :]], axis=0)
        rim_square[zone] = jnp.concatenate([square[:RIM], square[EXTENT - RIM :]], axis=0)
        high = square.astype(BF16)
        sq_high[zone] = high
        sq_low[zone] = (square - high.astype(F32)).astype(BF16)
        return carry

    each(zones, tables, 0)

    def lead_rows(zone, prods, order, row):
        number = lax.broadcasted_iota(jnp.int32, (8, cap), 0)
        return prods[zone, :8, :] * jnp.where(number < order, row, 1.0)

    def src_ready(zone, carry):
        src_lead[zone] = lead_rows(zone, src_prods, SRC_PARAMS, r_src[zone])
        return carry

    each(zones, src_ready, 0)

    whole_stat = stat_recv.at[pl.ds(0, devices - 1)]
    pltpu.make_async_copy(whole_stat, whole_stat, stat_sems.at[1]).wait()
    stats = jnp.sum(stat_recv[...], axis=0)
    live_total = jnp.sum(stats[:, LANES : 2 * LANES], axis=1, keepdims=True)
    abs_total = jnp.sum(stats[:, :LANES], axis=1, keepdims=True)

    def time_live(zone, carry):
        counts = stat_recv[zone * n_tm + tm][:, 2 * LANES :]
        live_time[zone] = (lane_row.astype(F32) < widen(counts)).astype(F32)
        return carry

    each(zones, time_live, 0)

    src_total = jnp.zeros((SRC_PARAMS, SRC_DEV), F32)
    att_total = jnp.zeros((ATT_PARAMS, SEG_DEV), F32)

    chunk = min(cap, 256) if cap % 256 == 0 else cap
    parts = [slice(at, at + chunk) for at in range(0, cap, chunk)]

    def group_sums(zone, lead, prods, hot, mask, weights):
        tall = split_rows(jnp.concatenate([lead * weights, prods[zone, 8:, :] * weights], axis=0))
        above = jnp.concatenate(
            [tall[at : at + 16] * mask[zone] for at in range(0, tall.shape[0], 16)], axis=0
        )
        return dot_nt(jnp.concatenate([tall - above, above], axis=0), hot[zone])

    def group_totals(both, order):
        rows = both[0].shape[0] // 4
        halves = []
        for at in (0, 2 * rows):
            low, high = slice(at, at + rows), slice(at + rows, at + 2 * rows)
            halves.append((both[0][low] + both[0][high]) + (both[1][low] + both[1][high]))
        return jnp.concatenate(halves, axis=1)

    def padded_steps(step, order):
        groups = step.shape[1]
        tall = split_rows(jnp.concatenate([step, jnp.zeros((8 - order, groups), F32)], axis=0))
        return jnp.concatenate([tall[:, : groups // 2], tall[:, groups // 2 :]], axis=0)

    def att_steps(step):
        high = step.astype(BF16).astype(F32)
        tall = jnp.concatenate([high, step - high], axis=0)
        groups = step.shape[1] // 2
        return jnp.concatenate([tall[:, :groups], tall[:, groups:]], axis=0).astype(BF16)

    def att_fitted(zones_at, steps):
        picked = [[dot_nn(steps, seg_hot[zone, :, part]) for part in parts] for zone in zones_at]
        fits = []
        for zone, values_of in zip(zones_at, picked):
            fit = []
            for part, values in zip(parts, values_of):
                values = jnp.where(seg_side[zone, :, part] > 0.5, values[8:], values[:8])
                fit.append(jnp.sum(values * att_twice[zone, :, part], axis=0, keepdims=True))
            fits.append(jnp.concatenate(fit, axis=1) if len(fit) > 1 else fit[0])
        return fits

    def fitted(zones_at, steps, prods, hot, side):
        picked = [[dot_nn(steps, hot[zone, :, part]) for part in parts] for zone in zones_at]
        fits = []
        for zone, values_of in zip(zones_at, picked):
            fit = []
            for part, values in zip(parts, values_of):
                values = jnp.where(
                    side[zone, :, part] > 0.5, values[16:24] + values[24:], values[:8] + values[8:16]
                )
                fit.append(jnp.sum(values * prods[zone, :8, part], axis=0, keepdims=True))
            fits.append(jnp.concatenate(fit, axis=1) if len(fit) > 1 else fit[0])
        return fits

    def zone_copy(send, recv, ssem, rsem, peer):
        return pltpu.make_async_remote_copy(
            src_ref=send.at[peer],
            dst_ref=recv.at[sky],
            send_sem=ssem,
            recv_sem=rsem,
            device_id={"sky": peer, "tm": tm},
            device_id_type=MESH,
        )

    def rim_copy(it, way, kind):
        return pltpu.make_async_remote_copy(
            src_ref=rim_send.at[it, way, kind],
            dst_ref=rim_recv.at[it, way, kind],
            send_sem=rim_ssem.at[it, way, kind],
            recv_sem=rim_rsem.at[it, way, kind],
            device_id={"sky": sky, "tm": lax.rem(tm + (1, n_tm - 1)[way], n_tm)},
            device_id_type=MESH,
        )

    has_next, has_last = tm < n_tm - 1, tm > 0

    def to_rims(it, kind, act):
        for way, there in ((0, has_next), (1, has_last)):

            @pl.when(there)
            def _():
                act(rim_copy(it, way, kind))

    def from_rims(it, kind):
        for way, there in ((0, has_last), (1, has_next)):

            @pl.when(there)
            def _():
                rim_copy(it, way, kind).wait_recv()

    def send_rims(it, kind, rims):
        for way, rows in ((0, slice(RIM, 2 * RIM)), (1, slice(0, RIM))):
            rim_send[it, way, kind, :, :UNIT_ROWS] = rims[rows]
        to_rims(it, kind, lambda copy: copy.start())

    wide = 2 * UNIT_ROWS

    def unit_weights(zone, row):
        high = row.astype(BF16).astype(F32)
        tall = jnp.concatenate(
            [
                jnp.broadcast_to(high, (UNIT_ROWS, cap)),
                jnp.broadcast_to(row - high, (UNIT_ROWS, cap)),
            ],
            axis=0,
        ).astype(BF16)
        return unit_hot[zone] * tall

    for it in range(ITERS):
        bound = clip_factor * (abs_total / live_total)

        def src_sums(numbers, total):
            rows = [r_src[zone] for zone in numbers]
            weights = [
                live_of(zone) * bound / jnp.maximum(jnp.abs(row), bound)
                for zone, row in zip(numbers, rows)
            ]
            return in_turns(
                total,
                (group_sums(zone, src_lead[zone], src_prods, src_hot, src_mask, weight)
                for zone, weight in zip(numbers, weights)),
            )

        blank = jnp.zeros((4 * rows_of(SRC_PARAMS), SRC_DEV // 2), F32)
        both = in_groups(zones, 8, src_sums, (blank, blank))
        step_x = block_solve(group_totals(both, SRC_PARAMS), SRC_PARAMS)
        src_total = src_total + step_x
        steps_x = padded_steps(step_x, SRC_PARAMS)

        def src_out(numbers, carry):
            zones_at = [far_first(number) for number in numbers]
            fits = fitted(zones_at, steps_x, src_prods, src_hot, src_side)
            for zone, fit in zip(zones_at, fits):
                fwd_send[it, zone] = r_src[zone] - live_of(zone) * fit

            for number, zone in zip(numbers, zones_at):

                def send():
                    zone_copy(
                        fwd_send.at[it], fwd_recv.at[it], fwd_ssem.at[it], fwd_rsem.at[it, sky], zone
                    ).start()

                if isinstance(number, int):
                    if number < n_sky - 1:
                        send()
                else:
                    pl.when(number < n_sky - 1)(send)
            return carry

        in_groups(zones, 6, src_out, 0, first=2)
        fwd_recv[it, sky] = fwd_send[it, sky]

        def att_sums(numbers, total):
            zones_at = [far_first(n_sky - 1 - number) for number in numbers]
            for number, zone in zip(numbers, zones_at):

                def arrive():
                    zone_copy(
                        fwd_send.at[it], fwd_recv.at[it], fwd_ssem.at[it], fwd_rsem.at[it, zone], zone
                    ).wait_recv()

                if isinstance(number, int):
                    if number > 0:
                        arrive()
                else:
                    pl.when(number > 0)(arrive)
            rows = [fwd_recv[it, zone] for zone in zones_at]
            weights = [
                live_time[zone] * bound / jnp.maximum(jnp.abs(row), bound)
                for zone, row in zip(zones_at, rows)
            ]
            for zone, weight in zip(zones_at, weights):
                v_time[zone] = weight
            att_part, h_part = total
            att_part = in_turns(
                att_part,
                (
                    group_sums(
                        zone, lead_rows(zone, att_prods, ATT_PARAMS, row), att_prods, seg_hot, seg_mask, weight
                    )
                    for zone, weight, row in zip(zones_at, weights, rows)
                ),
            )
            h_part = in_turns(
                h_part,
                (
                    dot_nt(split_rows(rim_square[zone] * weight), unit_hot[zone, :UNIT_ROWS, :])
                    for zone, weight in zip(zones_at, weights)
                ),
            )
            return att_part, h_part

        rim_blank = (jnp.zeros((4 * RIM, UNIT_ROWS), F32),) * 2
        blank = jnp.zeros((4 * rows_of(ATT_PARAMS), SEG_DEV // 2), F32)
        both, h_rims = in_groups(zones, 2, att_sums, ((blank, blank), rim_blank))

        def rim_total(sums):
            return add_all(half[at : at + 2 * RIM] for half in sums for at in (0, 2 * RIM))

        h_rims = rim_total(h_rims)
        step_y = block_solve(group_totals(both, ATT_PARAMS), ATT_PARAMS)
        att_total = att_total + step_y
        steps_y = att_steps(step_y)

        send_rims(it, 1, h_rims)

        def rim_sums(numbers, total):
            fits = att_fitted(numbers, steps_y)
            rows = [
                fwd_recv[it, zone] - live_time[zone] * fit for zone, fit in zip(numbers, fits)
            ]
            for zone, row in zip(numbers, rows):
                r_time[zone] = row
            return in_turns(
                total,
                (
                    dot_nt(split_rows(rim_part[zone] * (v_time[zone] * row)), unit_hot[zone, :UNIT_ROWS, :])
                    for zone, row in zip(numbers, rows)
                ),
            )

        g_rims = in_groups(zones, 8, rim_sums, rim_blank)
        g_rims = rim_total(g_rims)

        def joined(g_part, h_part):
            g_part = g_part + pltpu.roll(g_part, UNIT_ROWS, 1)
            left_half = lax.broadcasted_iota(jnp.int32, g_part.shape, 1) < UNIT_ROWS
            return jnp.where(left_half, g_part, h_part)

        def coefs_of(knots):
            ratio = knots / (pltpu.roll(knots, UNIT_ROWS, 1) + ridge)
            left_half = lax.broadcasted_iota(jnp.int32, knots.shape, 1) < UNIT_ROWS
            ratio = jnp.where(left_half, ratio, 0.0)
            high = ratio.astype(BF16).astype(F32)
            return (high + pltpu.roll(ratio - high, UNIT_ROWS, 1)).astype(BF16)

        send_rims(it, 0, g_rims)
        inner = slice(RIM, EXTENT - RIM)

        def inner_sums(numbers, total):
            g_part, h_part = total
            for zone in numbers:
                weight = v_time[zone]
                tall = unit_weights(zone, weight)
                h_part = h_part + dot_nt(sq_high[zone, inner, :], tall) + dot_nt(sq_low[zone, inner, :], tall)
                g_part = g_part + dot_nt(placed[zone, inner, :], unit_weights(zone, weight * r_time[zone]))
            return g_part, h_part

        middle = jnp.zeros((EXTENT - 2 * RIM, wide), F32)
        middle, h_total = in_groups(zones, 8, inner_sums, (middle, middle))
        h_total = h_total + pltpu.roll(h_total, UNIT_ROWS, 1)
        inner_coefs = coefs_of(joined(middle, h_total))

        def inner_fit(zone, carry):
            picked = dot_nn(inner_coefs, unit_hot[zone])
            fit = picked * placed[zone, inner, :].astype(F32)
            fit_time[zone] = jnp.sum(fit.reshape(-1, 8, cap), axis=0)
            return carry

        each(zones, inner_fit, 0)

        for kind in (1, 0):
            from_rims(it, kind)
        lead = KNOT_DEV - (EXTENT - RIM)
        shared = SPLINE - 1
        from_last = jnp.where(tm > 0, rim_recv[it, 0], 0.0)[:, lead : lead + shared, :UNIT_ROWS]
        from_next = jnp.where(tm < n_tm - 1, rim_recv[it, 1], 0.0)[:, :shared, :UNIT_ROWS]

        def added(rims, at):
            blank = lambda rows: [jnp.zeros((rows, UNIT_ROWS), F32)] if rows else []
            return rims + jnp.concatenate(
                [from_last[at]]
                + blank(RIM - shared + lead)
                + [from_next[at]]
                + blank(RIM - lead - shared),
                axis=0,
            )

        rim_coefs = split_rows(added(g_rims, 0) / (added(h_rims, 1) + ridge))

        last = it == ITERS - 1

        def back_out(peer):
            zone_copy(
                back_send.at[it], back_recv.at[it], back_ssem.at[it], back_rsem.at[it], peer
            ).start()

        def cal_out(numbers, total):
            zones_at = [far_first(number) for number in numbers] if last else numbers
            picked = [dot_nn(rim_coefs, unit_hot[zone, :UNIT_ROWS, :]) for zone in zones_at]
            rows = []
            for zone, values in zip(zones_at, picked):
                fit = (values[: 2 * RIM] + values[2 * RIM :]) * rim_part[zone]
                fit = jnp.sum(fit.reshape(-1, 8, cap), axis=0) + fit_time[zone]
                fit = jnp.sum(fit, axis=0, keepdims=True)
                rows.append(r_time[zone] - live_time[zone] * fit)
            for zone, row in zip(zones_at, rows):
                back_send[it, zone] = row
            if not last:
                return total + add_all(fold(jnp.abs(row)) for row in rows)
            for number, zone in zip(numbers, zones_at):
                if isinstance(number, int):
                    if number < n_sky - 1:
                        back_out(zone)
                else:
                    pl.when(number < n_sky - 1)(functools.partial(back_out, zone))
            return total

        if last:
            in_groups(zones, 6, cal_out, zero_row, first=2)
            srcp_ref[...] = src_total
            attp_ref[...] = att_total
        else:
            abs_sum = in_groups(zones, 8, cal_out, zero_row)
            abs_send[it] = abs_sum
            abs_recv[it, me] = abs_sum

            def send_abs(to_sky, to_tm):
                pltpu.make_async_remote_copy(
                    src_ref=abs_send.at[it],
                    dst_ref=abs_recv.at[it, me],
                    send_sem=abs_sems.at[it, 0],
                    recv_sem=abs_sems.at[it, 1],
                    device_id={"sky": to_sky, "tm": to_tm},
                    device_id_type=MESH,
                ).start()

            every_other(send_abs)
            each(n_sky - 1, lambda number, carry: (back_out(far_first(number)), carry)[1], 0)

        back_recv[it, sky] = back_send[it, sky]

        whole = back_recv.at[it, pl.ds(0, n_sky - 1)]
        pltpu.make_async_copy(whole, whole, back_rsem.at[it]).wait()

        def put_back(zone, carry):
            if last:
                out_ref[pl.ds(zone, 1), :] = back_recv[it, zone]
            else:
                r_src[zone] = back_recv[it, zone]
            return carry

        each(zones, put_back, 0)

        if not last:
            each(zones, src_ready, 0)
            whole = abs_recv.at[it, pl.ds(0, devices - 1)]
            pltpu.make_async_copy(whole, whole, abs_sems.at[it, 1]).wait()
            abs_total = jnp.sum(jnp.sum(abs_recv[it], axis=0), axis=1, keepdims=True)

    pltpu.make_async_copy(whole_stat, whole_stat, stat_sems.at[0]).wait()
    for it in range(ITERS):
        if it < ITERS - 1:
            whole = abs_recv.at[it, pl.ds(0, devices - 1)]
            pltpu.make_async_copy(whole, whole, abs_sems.at[it, 0]).wait()

        for recv, ssem in ((fwd_recv, fwd_ssem), (back_recv, back_ssem)):
            whole = recv.at[it, pl.ds(0, n_sky - 1)]
            pltpu.make_async_copy(whole, whole, ssem.at[it]).wait()
        for kind in (1, 0):
            to_rims(it, kind, lambda copy: copy.wait_send())


def write_out(count, *refs):
    sems = refs[-1]
    copies = [
        pltpu.make_async_copy(refs[at], refs[count + at], sems.at[at]) for at in range(count)
    ]
    for copy in copies:
        copy.start()
    for copy in copies:
        copy.wait()


def shards(
    residual,
    counts,
    source_index,
    source_partials,
    segment_index,
    attitude_partials,
    unit_index,
    knot_base,
    calib_partials,
    n_sky,
    n_tm,
):
    zones, capacity = residual.shape[2:]
    cap = -(-capacity // LANES) * LANES
    devices = n_sky * n_tm

    def flat(value):
        value = value.reshape(value.shape[:-4] + (zones, capacity))
        if cap != capacity:
            value = jnp.pad(value, [(0, 0)] * (value.ndim - 1) + [(0, cap - capacity)])
        return value

    vmem = pl.BlockSpec(memory_space=pltpu.VMEM)
    row = lambda *lead: pltpu.VMEM(lead + (1, cap), F32)
    dma = pltpu.SemaphoreType.DMA
    result_bytes = 4 * (zones * cap + 8 * SRC_DEV + 8 * SEG_DEV)
    pinned = cap == capacity
    result = pltpu.VMEM if pinned else jax.ShapeDtypeStruct
    corrected, src_params, att_params = pl.pallas_call(
        functools.partial(kernel, n_sky, n_tm),
        out_shape=(
            result((zones, cap), F32),
            result((SRC_PARAMS, SRC_DEV), F32),
            result((ATT_PARAMS, SEG_DEV), F32),
        ),
        in_specs=[pl.BlockSpec(memory_space=pltpu.HBM)] * 9,
        out_specs=(vmem, vmem, vmem),
        scratch_shapes=[
            pltpu.VMEM((zones, cap), F32),
            pltpu.SMEM((zones,), jnp.int32),
            pltpu.VMEM((zones, cap), jnp.int32),
            pltpu.VMEM((SRC_PARAMS, zones, cap), BF16),
            pltpu.VMEM((zones, cap), jnp.int32),
            pltpu.VMEM((ATT_PARAMS, zones, cap), BF16),
            pltpu.VMEM((zones, cap), jnp.int32),
            pltpu.VMEM((zones, cap), jnp.int32),
            pltpu.VMEM((SPLINE, zones, cap), BF16),
            dma((9,)),
            pltpu.VMEM((zones, SRC_DEV // 2, cap), BF16),
            pltpu.VMEM((zones, SEG_DEV // 2, cap), BF16),
            row(zones),
            row(zones),
            pltpu.VMEM((zones, 16, cap), BF16),
            pltpu.VMEM((zones, 16, cap), BF16),
            pltpu.VMEM((zones, 8, cap), F32),
            pltpu.VMEM((zones, 2 * UNIT_ROWS, cap), BF16),
            pltpu.VMEM((zones, EXTENT, cap), BF16),
            pltpu.VMEM((zones, EXTENT, cap), BF16),
            pltpu.VMEM((zones, EXTENT, cap), BF16),
            pltpu.VMEM((zones, 2 * RIM, cap), F32),
            pltpu.VMEM((zones, 2 * RIM, cap), F32),
            pltpu.VMEM((zones, rows_of(SRC_PARAMS), cap), F32),
            pltpu.VMEM((zones, rows_of(ATT_PARAMS), cap), F32),
            pltpu.VMEM((zones, 2 * ATT_PARAMS, cap), F32),
            pltpu.VMEM((zones, SPLINE, cap), F32),
            row(zones),
            row(zones),
            row(zones),
            row(zones),
            pltpu.VMEM((zones, 8, cap), F32),
            pltpu.VMEM((n_sky, 1, 3 * LANES), F32),
            pltpu.VMEM((devices, 1, 3 * LANES), F32),
            pltpu.VMEM((ITERS, 1, LANES), F32),
            pltpu.VMEM((ITERS, devices, 1, LANES), F32),
            row(ITERS, zones),
            row(ITERS, zones),
            row(ITERS, zones),
            row(ITERS, zones),
            pltpu.VMEM((ITERS, 2, 2, RIM, LANES), F32),
            pltpu.VMEM((ITERS, 2, 2, RIM, LANES), F32),
            dma((2,)),
            dma((ITERS, 2)),
            dma((ITERS,)),
            dma((ITERS, n_sky)),
            dma((ITERS,)),
            dma((ITERS,)),
            dma((ITERS, 2, 2)),
            dma((ITERS, 2, 2)),
        ],
        compiler_params=pltpu.CompilerParams(
            collective_id=0, has_side_effects=True, vmem_limit_bytes=67010000
        ),
        name="astrometry",
    )(
        flat(residual),
        counts.reshape(zones),
        flat(source_index),
        flat(source_partials),
        flat(segment_index),
        flat(attitude_partials),
        flat(unit_index),
        flat(knot_base),
        flat(calib_partials),
    )
    results = (corrected, src_params, att_params)
    if pinned:
        results = [pltpu.with_memory_space_constraint(value, pltpu.VMEM) for value in results]
    corrected, src_params, att_params = pl.pallas_call(
        functools.partial(write_out, len(results)),
        out_shape=tuple(jax.ShapeDtypeStruct(value.shape, value.dtype) for value in results),
        in_specs=[vmem] * len(results),
        out_specs=tuple(pl.BlockSpec(memory_space=pltpu.HBM) for _ in results),
        scratch_shapes=[dma((len(results),))],
        name="write_out",
    )(*results)
    return corrected[:, :capacity].reshape(1, 1, zones, capacity), src_params, att_params


def solution(mesh):
    return jax.shard_map(
        functools.partial(shards, n_sky=mesh.shape["sky"], n_tm=mesh.shape["tm"]),
        mesh=mesh,
        in_specs=(
            P("sky", "tm", None, None),
            P("sky", "tm", None),
            P("sky", "tm", None, None),
            P(None, "sky", "tm", None, None),
            P("sky", "tm", None, None),
            P(None, "sky", "tm", None, None),
            P("sky", "tm", None, None),
            P("sky", "tm", None, None),
            P(None, "sky", "tm", None, None),
        ),
        out_specs=(P("sky", "tm", None, None), P(None, ("sky", "tm")), P(None, ("sky", "tm"))),
        check_vma=False,
    )
```

```python
import functools

import jax
import jax.numpy as jnp
from jax import lax
from jax.experimental import pallas as pl
from jax.experimental.pallas import tpu as pltpu
from jax.sharding import PartitionSpec as P

SRC_DEV = 256
SEG_DEV = 128
KNOT_DEV = 113
UNITS = 62
SPLINE = 16
SRC_PARAMS = 5
ATT_PARAMS = 4
ITERS = 2

clip_factor = 1.5
ridge = 1.0

LANES = 128
F32 = jnp.float32
BF16 = jnp.bfloat16
MESH = pl.DeviceIdType.MESH
UNIT_ROWS = -(-UNITS // 64) * 64
EXTENT = -(-(KNOT_DEV + SPLINE - 1) // LANES) * LANES
RIM = SPLINE


def lower_pairs(order):
    return [(row_at, col_at) for row_at in range(order) for col_at in range(row_at + 1)]


def rows_of(order):
    return -(-(order + len(lower_pairs(order))) // 8) * 8


def split_rows(value):
    high = value.astype(BF16).astype(F32)
    return jnp.concatenate([high, value - high], axis=0).astype(BF16)


def dot_nt(left, right):
    return lax.dot_general(left, right, (((1,), (1,)), ((), ())), preferred_element_type=F32)


def dot_nn(left, right):
    return lax.dot_general(left, right, (((1,), (0,)), ((), ())), preferred_element_type=F32)


def in_groups(count, size, body, carry, first=None):
    if count <= 16:
        start = 0
        while start < count:
            end = min(start + (first if first and not start else size), count)
            carry = body(list(range(start, end)), carry)
            start = end
        return carry
    size = size if count % size == 0 else 1

    def group(number, carry):
        return body([number * size + at for at in range(size)], carry)

    return lax.fori_loop(0, count // size, group, carry)


def in_turns(totals, values):
    totals = list(totals)
    for number, value in enumerate(values):
        totals[number % 2] = totals[number % 2] + value
    return tuple(totals)


def add_all(values):
    values = list(values)
    while len(values) > 1:
        values = [
            values[at] + values[at + 1] if at + 1 < len(values) else values[at]
            for at in range(0, len(values), 2)
        ]
    return values[0]


def each(count, body, carry):
    if count <= 16:
        for number in range(count):
            carry = body(number, carry)
        return carry
    return lax.fori_loop(0, count, body, carry)


def block_solve(sums, order):
    pairs = lower_pairs(order)
    matrix = {}
    for number, (row_at, col_at) in enumerate(pairs):
        at = order + number
        matrix[row_at, col_at] = sums[at : at + 1] + (ridge if row_at == col_at else 0.0)
    right = [sums[at : at + 1] for at in range(order)]
    inverse = []
    for pivot in range(order):
        inverse.append(1.0 / matrix[pivot, pivot])
        for row_at in range(pivot + 1, order):
            ratio = matrix[row_at, pivot] * inverse[pivot]
            for col_at in range(pivot + 1, row_at + 1):
                matrix[row_at, col_at] = matrix[row_at, col_at] - ratio * matrix[col_at, pivot]
            right[row_at] = right[row_at] - ratio * right[pivot]
    solved = [None] * order
    for row_at in reversed(range(order)):
        running = right[row_at]
        for inner_at in range(row_at + 1, order):
            running = running - matrix[inner_at, row_at] * solved[inner_at]
        solved[row_at] = running * inverse[row_at]
    return jnp.concatenate(solved, axis=0)


def store_products(partials_ref, prods, order):
    values = [partials_ref[at].astype(F32) for at in range(order)]
    listed = values + [values[row_at] * values[col_at] for row_at, col_at in lower_pairs(order)]
    while len(listed) < prods.shape[1]:
        listed.append(jnp.zeros_like(values[0]))
    for at, value in enumerate(listed):
        prods[:, at, :] = value


def kernel(
    n_sky,
    n_tm,
    res_hbm,
    cnt_hbm,
    src_hbm,
    sp_hbm,
    seg_hbm,
    ap_hbm,
    unit_hbm,
    base_hbm,
    cp_hbm,
    out_ref,
    srcp_ref,
    attp_ref,
    res_ref,
    cnt_ref,
    src_ref,
    sp_ref,
    seg_ref,
    ap_ref,
    unit_ref,
    base_ref,
    cp_ref,
    in_sems,
    src_hot,
    seg_hot,
    src_side,
    seg_side,
    src_mask,
    seg_mask,
    src_lead,
    unit_hot,
    placed,
    sq_high,
    sq_low,
    rim_part,
    rim_square,
    src_prods,
    att_prods,
    att_twice,
    cal_rows,
    r_src,
    r_time,
    v_time,
    live_time,
    fit_time,
    stat_send,
    stat_recv,
    abs_send,
    abs_recv,
    fwd_send,
    fwd_recv,
    back_send,
    back_recv,
    rim_send,
    rim_recv,
    stat_sems,
    abs_sems,
    fwd_ssem,
    fwd_rsem,
    back_ssem,
    back_rsem,
    rim_ssem,
    rim_rsem,
):
    zones, cap = res_ref.shape
    tiles = cap // LANES
    devices = n_sky * n_tm
    sky = lax.axis_index("sky")
    tm = lax.axis_index("tm")
    me = sky * n_tm + tm

    def wrapped(value, size):
        return jnp.where(value >= size, value - size, value)

    lower = sky < n_sky // 2

    def far_first(number):
        down = n_sky - 1 - number
        down = jnp.where(down <= sky, down - 1, down)
        up = jnp.where(number >= sky, number + 1, number)
        peer = jnp.where(lower, down, up)
        if isinstance(number, int):
            return sky if number == n_sky - 1 else peer
        return jnp.where(number == n_sky - 1, sky, peer)

    def every_other(body, after=None):
        if devices <= 64:
            if n_tm & (n_tm - 1):
                tms = [wrapped(tm + at, n_tm) for at in range(n_tm)]
            else:
                tms = [tm ^ at for at in range(n_tm)]
            for number in range(n_sky):
                other = far_first(number)
                for at in reversed(range(n_tm)):
                    if number < n_sky - 1 or at:
                        body(other, tms[at])
                if after and number < n_sky - 1:
                    after(other)
            return

        @pl.loop(1, devices)
        def _(step):
            flat = lax.rem(me + step, devices)
            body(flat // n_tm, lax.rem(flat, n_tm))

        if after:
            each(n_sky - 1, lambda number, carry: (after(far_first(number)), carry)[1], 0)

    arriving = [
        pltpu.make_async_copy(source, target, in_sems.at[number])
        for number, (source, target) in enumerate(
            (
                (res_hbm, res_ref),
                (cnt_hbm, cnt_ref),
                (src_hbm, src_ref),
                (sp_hbm, sp_ref),
                (seg_hbm, seg_ref),
                (ap_hbm, ap_ref),
                (unit_hbm, unit_ref),
                (base_hbm, base_ref),
                (cp_hbm, cp_ref),
            )
        )
    ]
    for copy in arriving:
        copy.start()

    barrier = pltpu.get_barrier_semaphore()

    def greet(to_sky, to_tm):
        pl.semaphore_signal(
            barrier, inc=1, device_id={"sky": to_sky, "tm": to_tm}, device_id_type=MESH
        )

    every_other(greet)

    lane_row = lax.broadcasted_iota(jnp.int32, (1, cap), 1)

    def fold(row):
        total = row[:, :LANES]
        for at in range(1, tiles):
            total = total + row[:, at * LANES : (at + 1) * LANES]
        return total

    def live_of(zone):
        return (lane_row < cnt_ref[zone]).astype(F32)

    for copy in arriving[:2]:
        copy.wait()

    def first_stats(zone, carry):
        sums, lives = carry
        row = res_ref[pl.ds(zone, 1), :] * live_of(zone)
        r_src[zone] = row
        return sums + fold(jnp.abs(row)), lives + cnt_ref[zone]

    zero_row = jnp.zeros((1, LANES), F32)
    lane = lax.broadcasted_iota(jnp.int32, (1, LANES), 1)
    count_lane, live_lane = LANES - 1, LANES - 2
    sums, lives = each(zones, first_stats, (zero_row, jnp.int32(0)))
    sums = sums + jnp.where(lane < 2, pltpu.roll(sums, 2, 1), 0.0)
    sums = jnp.where(lane == live_lane, jnp.full((1, LANES), lives, jnp.int32).astype(F32), sums)

    def put_stats(zone, carry):
        count = jnp.full((1, LANES), cnt_ref[zone], jnp.int32).astype(F32)
        stat_send[zone] = jnp.where(lane == count_lane, count, sums)
        return carry

    each(zones, put_stats, 0)
    stat_recv[me] = stat_send[sky]
    pl.semaphore_wait(barrier, devices - 1)

    def send_stats(to_sky, to_tm):
        pltpu.make_async_remote_copy(
            src_ref=stat_send.at[to_sky],
            dst_ref=stat_recv.at[me],
            send_sem=stat_sems.at[0],
            recv_sem=stat_sems.at[1],
            device_id={"sky": to_sky, "tm": to_tm},
            device_id_type=MESH,
        ).start()

    every_other(send_stats)

    for copy in arriving[2:]:
        copy.wait()

    store_products(sp_ref, src_prods, SRC_PARAMS)
    store_products(ap_ref, att_prods, ATT_PARAMS)
    for at in range(2 * ATT_PARAMS):
        att_twice[:, at, :] = ap_ref[at % ATT_PARAMS].astype(F32)
    for at in range(SPLINE):
        cal_rows[:, at, :] = cp_ref[at].astype(F32)

    def hot_rows(rows, labels):
        number = lax.broadcasted_iota(jnp.int32, (rows, cap), 0)
        return jnp.where(number == labels, 1.0, 0.0).astype(BF16)

    def tables(zone, carry):
        for labels_ref, hot_ref, side_ref, mask_ref in (
            (src_ref, src_hot, src_side, src_mask),
            (seg_ref, seg_hot, seg_side, seg_mask),
        ):
            labels = labels_ref[pl.ds(zone, 1), :]
            groups = hot_ref.shape[1]
            above = labels >= groups
            hot_ref[zone] = hot_rows(groups, jnp.where(above, labels - groups, labels))
            side = jnp.where(above, 1.0, 0.0)
            side_ref[zone] = side
            mask_ref[zone] = jnp.broadcast_to(side, (16, cap)).astype(BF16)
        hot = hot_rows(UNIT_ROWS, unit_ref[pl.ds(zone, 1), :])
        unit_hot[zone] = jnp.concatenate([hot, hot], axis=0)
        base = jnp.broadcast_to(base_ref[pl.ds(zone, 1), :], (8, cap))
        turned = []
        for part in range(SPLINE // 8):
            rows = cal_rows[zone, part * 8 : part * 8 + 8, :]
            for bit in (1, 2, 4):
                rows = jnp.where((base & bit) != 0, pltpu.roll(rows, bit, 0), rows)
            turned.append(rows)
        reach = lax.shift_right_arithmetic(
            lax.broadcasted_iota(jnp.int32, (8, cap), 0) - base, jnp.int32(3)
        )
        pieces = []
        for group in range(EXTENT // 8):
            piece = jnp.zeros((8, cap), F32)
            for part, rows in enumerate(turned):
                piece = jnp.where(reach == part - group, rows, piece)
            pieces.append(piece)
        spread = jnp.concatenate(pieces, axis=0)
        placed[zone] = spread.astype(BF16)
        square = spread * spread
        rim_part[zone] = jnp.concatenate([spread[:RIM], spread[EXTENT - RIM :]], axis=0)
        rim_square[zone] = jnp.concatenate([square[:RIM], square[EXTENT - RIM :]], axis=0)
        high = square.astype(BF16)
        sq_high[zone] = high
        sq_low[zone] = (square - high.astype(F32)).astype(BF16)
        return carry

    each(zones, tables, 0)

    def lead_rows(zone, prods, order, row):
        number = lax.broadcasted_iota(jnp.int32, (8, cap), 0)
        return prods[zone, :8, :] * jnp.where(number < order, row, 1.0)

    def src_ready(zone, carry):
        src_lead[zone] = lead_rows(zone, src_prods, SRC_PARAMS, r_src[zone])
        return carry

    each(zones, src_ready, 0)

    whole_stat = stat_recv.at[pl.ds(0, devices - 1)]
    pltpu.make_async_copy(whole_stat, whole_stat, stat_sems.at[1]).wait()
    stats = jnp.sum(stat_recv[...], axis=0)
    live_total = jnp.sum(jnp.where(lane == live_lane, stats, 0.0), axis=1, keepdims=True)
    abs_total = jnp.sum(jnp.where(lane < live_lane, stats, 0.0), axis=1, keepdims=True)

    def time_live(zone, carry):
        held = stat_recv[zone * n_tm + tm]
        count = jnp.sum(jnp.where(lane == count_lane, held, 0.0), axis=1, keepdims=True)
        live_time[zone] = (lane_row.astype(F32) < count).astype(F32)
        return carry

    src_total = jnp.zeros((SRC_PARAMS, SRC_DEV), F32)
    att_total = jnp.zeros((ATT_PARAMS, SEG_DEV), F32)

    chunk = min(cap, 256) if cap % 256 == 0 else cap
    parts = [slice(at, at + chunk) for at in range(0, cap, chunk)]

    def group_sums(zone, lead, prods, hot, mask, weights):
        tall = split_rows(jnp.concatenate([lead * weights, prods[zone, 8:, :] * weights], axis=0))
        above = jnp.concatenate(
            [tall[at : at + 16] * mask[zone] for at in range(0, tall.shape[0], 16)], axis=0
        )
        return dot_nt(jnp.concatenate([tall - above, above], axis=0), hot[zone])

    def group_totals(both, order):
        rows = both[0].shape[0] // 4
        halves = []
        for at in (0, 2 * rows):
            low, high = slice(at, at + rows), slice(at + rows, at + 2 * rows)
            halves.append((both[0][low] + both[0][high]) + (both[1][low] + both[1][high]))
        return jnp.concatenate(halves, axis=1)

    def padded_steps(step, order):
        groups = step.shape[1]
        tall = split_rows(jnp.concatenate([step, jnp.zeros((8 - order, groups), F32)], axis=0))
        return jnp.concatenate([tall[:, : groups // 2], tall[:, groups // 2 :]], axis=0)

    def att_steps(step):
        high = step.astype(BF16).astype(F32)
        tall = jnp.concatenate([high, step - high], axis=0)
        groups = step.shape[1] // 2
        return jnp.concatenate([tall[:, :groups], tall[:, groups:]], axis=0).astype(BF16)

    def att_fitted(zones_at, steps):
        picked = [[dot_nn(steps, seg_hot[zone, :, part]) for part in parts] for zone in zones_at]
        fits = []
        for zone, values_of in zip(zones_at, picked):
            fit = []
            for part, values in zip(parts, values_of):
                values = jnp.where(seg_side[zone, :, part] > 0.5, values[8:], values[:8])
                fit.append(jnp.sum(values * att_twice[zone, :, part], axis=0, keepdims=True))
            fits.append(jnp.concatenate(fit, axis=1) if len(fit) > 1 else fit[0])
        return fits

    def fitted(zones_at, steps, prods, hot, side):
        picked = [[dot_nn(steps, hot[zone, :, part]) for part in parts] for zone in zones_at]
        fits = []
        for zone, values_of in zip(zones_at, picked):
            fit = []
            for part, values in zip(parts, values_of):
                values = jnp.where(
                    side[zone, :, part] > 0.5, values[16:24] + values[24:], values[:8] + values[8:16]
                )
                fit.append(jnp.sum(values * prods[zone, :8, part], axis=0, keepdims=True))
            fits.append(jnp.concatenate(fit, axis=1) if len(fit) > 1 else fit[0])
        return fits

    def zone_copy(send, recv, ssem, rsem, peer):
        return pltpu.make_async_remote_copy(
            src_ref=send.at[peer],
            dst_ref=recv.at[sky],
            send_sem=ssem,
            recv_sem=rsem,
            device_id={"sky": peer, "tm": tm},
            device_id_type=MESH,
        )

    def rim_copy(it, way, kind):
        return pltpu.make_async_remote_copy(
            src_ref=rim_send.at[it, way, kind],
            dst_ref=rim_recv.at[it, way, kind],
            send_sem=rim_ssem.at[it, way, kind],
            recv_sem=rim_rsem.at[it, way, kind],
            device_id={"sky": sky, "tm": lax.rem(tm + (1, n_tm - 1)[way], n_tm)},
            device_id_type=MESH,
        )

    has_next, has_last = tm < n_tm - 1, tm > 0

    def to_rims(it, kind, act):
        for way, there in ((0, has_next), (1, has_last)):

            @pl.when(there)
            def _():
                act(rim_copy(it, way, kind))

    def from_rims(it, kind):
        for way, there in ((0, has_last), (1, has_next)):

            @pl.when(there)
            def _():
                rim_copy(it, way, kind).wait_recv()

    def send_rims(it, kind, rims):
        for way, rows in ((0, slice(RIM, 2 * RIM)), (1, slice(0, RIM))):
            rim_send[it, way, kind, :, :UNIT_ROWS] = rims[rows]
        to_rims(it, kind, lambda copy: copy.start())

    wide = 2 * UNIT_ROWS

    def unit_weights(zone, row):
        high = row.astype(BF16).astype(F32)
        tall = jnp.concatenate(
            [
                jnp.broadcast_to(high, (UNIT_ROWS, cap)),
                jnp.broadcast_to(row - high, (UNIT_ROWS, cap)),
            ],
            axis=0,
        ).astype(BF16)
        return unit_hot[zone] * tall

    for it in range(ITERS):
        bound = clip_factor * (abs_total / live_total)

        def src_sums(numbers, total):
            rows = [r_src[zone] for zone in numbers]
            weights = [
                live_of(zone) * bound / jnp.maximum(jnp.abs(row), bound)
                for zone, row in zip(numbers, rows)
            ]
            return in_turns(
                total,
                (group_sums(zone, src_lead[zone], src_prods, src_hot, src_mask, weight)
                for zone, weight in zip(numbers, weights)),
            )

        blank = jnp.zeros((4 * rows_of(SRC_PARAMS), SRC_DEV // 2), F32)
        both = in_groups(zones, 8, src_sums, (blank, blank))
        step_x = block_solve(group_totals(both, SRC_PARAMS), SRC_PARAMS)
        src_total = src_total + step_x
        steps_x = padded_steps(step_x, SRC_PARAMS)

        def src_out(numbers, carry):
            zones_at = [far_first(number) for number in numbers]
            fits = fitted(zones_at, steps_x, src_prods, src_hot, src_side)
            for zone, fit in zip(zones_at, fits):
                fwd_send[it, zone] = r_src[zone] - live_of(zone) * fit

            for number, zone in zip(numbers, zones_at):

                def send():
                    zone_copy(
                        fwd_send.at[it], fwd_recv.at[it], fwd_ssem.at[it], fwd_rsem.at[it, sky], zone
                    ).start()

                if isinstance(number, int):
                    if number < n_sky - 1:
                        send()
                else:
                    pl.when(number < n_sky - 1)(send)
            return carry

        in_groups(zones, 6, src_out, 0, first=2)
        fwd_recv[it, sky] = fwd_send[it, sky]
        if it == 0:
            each(zones, time_live, 0)

        def att_sums(numbers, total):
            zones_at = [far_first(n_sky - 1 - number) for number in numbers]
            for number, zone in zip(numbers, zones_at):

                def arrive():
                    zone_copy(
                        fwd_send.at[it], fwd_recv.at[it], fwd_ssem.at[it], fwd_rsem.at[it, zone], zone
                    ).wait_recv()

                if isinstance(number, int):
                    if number > 0:
                        arrive()
                else:
                    pl.when(number > 0)(arrive)
            rows = [fwd_recv[it, zone] for zone in zones_at]
            weights = [
                live_time[zone] * bound / jnp.maximum(jnp.abs(row), bound)
                for zone, row in zip(zones_at, rows)
            ]
            for zone, weight in zip(zones_at, weights):
                v_time[zone] = weight
            att_part, h_part = total
            att_part = in_turns(
                att_part,
                (
                    group_sums(
                        zone, lead_rows(zone, att_prods, ATT_PARAMS, row), att_prods, seg_hot, seg_mask, weight
                    )
                    for zone, weight, row in zip(zones_at, weights, rows)
                ),
            )
            h_part = in_turns(
                h_part,
                (
                    dot_nt(split_rows(rim_square[zone] * weight), unit_hot[zone, :UNIT_ROWS, :])
                    for zone, weight in zip(zones_at, weights)
                ),
            )
            return att_part, h_part

        rim_blank = (jnp.zeros((4 * RIM, UNIT_ROWS), F32),) * 2
        blank = jnp.zeros((4 * rows_of(ATT_PARAMS), SEG_DEV // 2), F32)
        both, h_rims = in_groups(zones, 2, att_sums, ((blank, blank), rim_blank))

        def rim_total(sums):
            return add_all(half[at : at + 2 * RIM] for half in sums for at in (0, 2 * RIM))

        h_rims = rim_total(h_rims)
        step_y = block_solve(group_totals(both, ATT_PARAMS), ATT_PARAMS)
        att_total = att_total + step_y
        steps_y = att_steps(step_y)

        send_rims(it, 1, h_rims)

        def rim_sums(numbers, total):
            fits = att_fitted(numbers, steps_y)
            rows = [
                fwd_recv[it, zone] - live_time[zone] * fit for zone, fit in zip(numbers, fits)
            ]
            for zone, row in zip(numbers, rows):
                r_time[zone] = row
            return in_turns(
                total,
                (
                    dot_nt(split_rows(rim_part[zone] * (v_time[zone] * row)), unit_hot[zone, :UNIT_ROWS, :])
                    for zone, row in zip(numbers, rows)
                ),
            )

        g_rims = in_groups(zones, 8, rim_sums, rim_blank)
        g_rims = rim_total(g_rims)

        def joined(g_part, h_part):
            g_part = g_part + pltpu.roll(g_part, UNIT_ROWS, 1)
            left_half = lax.broadcasted_iota(jnp.int32, g_part.shape, 1) < UNIT_ROWS
            return jnp.where(left_half, g_part, h_part)

        def coefs_of(knots):
            ratio = knots / (pltpu.roll(knots, UNIT_ROWS, 1) + ridge)
            left_half = lax.broadcasted_iota(jnp.int32, knots.shape, 1) < UNIT_ROWS
            ratio = jnp.where(left_half, ratio, 0.0)
            high = ratio.astype(BF16).astype(F32)
            return (high + pltpu.roll(ratio - high, UNIT_ROWS, 1)).astype(BF16)

        send_rims(it, 0, g_rims)
        inner = slice(RIM, EXTENT - RIM)

        def inner_sums(numbers, total):
            g_part, h_part = total
            for zone in numbers:
                weight = v_time[zone]
                tall = unit_weights(zone, weight)
                h_part = h_part + dot_nt(sq_high[zone, inner, :], tall) + dot_nt(sq_low[zone, inner, :], tall)
                g_part = g_part + dot_nt(placed[zone, inner, :], unit_weights(zone, weight * r_time[zone]))
            return g_part, h_part

        middle = jnp.zeros((EXTENT - 2 * RIM, wide), F32)
        middle, h_total = in_groups(zones, 8, inner_sums, (middle, middle))
        h_total = h_total + pltpu.roll(h_total, UNIT_ROWS, 1)
        inner_coefs = coefs_of(joined(middle, h_total))

        def inner_fit(zone, carry):
            picked = dot_nn(inner_coefs, unit_hot[zone])
            fit = picked * placed[zone, inner, :].astype(F32)
            fit_time[zone] = jnp.sum(fit.reshape(-1, 8, cap), axis=0)
            return carry

        each(zones, inner_fit, 0)

        for kind in (1, 0):
            from_rims(it, kind)
        lead = KNOT_DEV - (EXTENT - RIM)
        shared = SPLINE - 1
        from_last = jnp.where(tm > 0, rim_recv[it, 0], 0.0)[:, lead : lead + shared, :UNIT_ROWS]
        from_next = jnp.where(tm < n_tm - 1, rim_recv[it, 1], 0.0)[:, :shared, :UNIT_ROWS]

        def added(rims, at):
            blank = lambda rows: [jnp.zeros((rows, UNIT_ROWS), F32)] if rows else []
            return rims + jnp.concatenate(
                [from_last[at]]
                + blank(RIM - shared + lead)
                + [from_next[at]]
                + blank(RIM - lead - shared),
                axis=0,
            )

        rim_coefs = split_rows(added(g_rims, 0) / (added(h_rims, 1) + ridge))

        last = it == ITERS - 1

        def back_out(peer):
            zone_copy(
                back_send.at[it], back_recv.at[it], back_ssem.at[it], back_rsem.at[it], peer
            ).start()

        def cal_out(numbers, total):
            zones_at = [far_first(number) for number in numbers] if last else numbers
            picked = [dot_nn(rim_coefs, unit_hot[zone, :UNIT_ROWS, :]) for zone in zones_at]
            rows = []
            for zone, values in zip(zones_at, picked):
                fit = (values[: 2 * RIM] + values[2 * RIM :]) * rim_part[zone]
                fit = jnp.sum(fit.reshape(-1, 8, cap), axis=0) + fit_time[zone]
                fit = jnp.sum(fit, axis=0, keepdims=True)
                rows.append(r_time[zone] - live_time[zone] * fit)
            for zone, row in zip(zones_at, rows):
                back_send[it, zone] = row
            if not last:
                return total + add_all(fold(jnp.abs(row)) for row in rows)
            for number, zone in zip(numbers, zones_at):
                if isinstance(number, int):
                    if number < n_sky - 1:
                        back_out(zone)
                else:
                    pl.when(number < n_sky - 1)(functools.partial(back_out, zone))
            return total

        if last:
            in_groups(zones, 6, cal_out, zero_row, first=2)
            srcp_ref[...] = src_total
            attp_ref[...] = att_total
        else:
            abs_sum = in_groups(zones, 8, cal_out, zero_row)
            abs_send[it] = abs_sum
            abs_recv[it, me] = abs_sum

            def send_abs(to_sky, to_tm):
                pltpu.make_async_remote_copy(
                    src_ref=abs_send.at[it],
                    dst_ref=abs_recv.at[it, me],
                    send_sem=abs_sems.at[it, 0],
                    recv_sem=abs_sems.at[it, 1],
                    device_id={"sky": to_sky, "tm": to_tm},
                    device_id_type=MESH,
                ).start()

            every_other(send_abs)
            each(n_sky - 1, lambda number, carry: (back_out(far_first(number)), carry)[1], 0)

        back_recv[it, sky] = back_send[it, sky]

        whole = back_recv.at[it, pl.ds(0, n_sky - 1)]
        pltpu.make_async_copy(whole, whole, back_rsem.at[it]).wait()

        def put_back(zone, carry):
            if last:
                out_ref[pl.ds(zone, 1), :] = back_recv[it, zone]
            else:
                r_src[zone] = back_recv[it, zone]
            return carry

        each(zones, put_back, 0)

        if not last:
            each(zones, src_ready, 0)
            whole = abs_recv.at[it, pl.ds(0, devices - 1)]
            pltpu.make_async_copy(whole, whole, abs_sems.at[it, 1]).wait()
            abs_total = jnp.sum(jnp.sum(abs_recv[it], axis=0), axis=1, keepdims=True)

    pltpu.make_async_copy(whole_stat, whole_stat, stat_sems.at[0]).wait()
    for it in range(ITERS):
        if it < ITERS - 1:
            whole = abs_recv.at[it, pl.ds(0, devices - 1)]
            pltpu.make_async_copy(whole, whole, abs_sems.at[it, 0]).wait()

        for recv, ssem in ((fwd_recv, fwd_ssem), (back_recv, back_ssem)):
            whole = recv.at[it, pl.ds(0, n_sky - 1)]
            pltpu.make_async_copy(whole, whole, ssem.at[it]).wait()
        for kind in (1, 0):
            to_rims(it, kind, lambda copy: copy.wait_send())


def write_out(count, *refs):
    sems = refs[-1]
    copies = [
        pltpu.make_async_copy(refs[at], refs[count + at], sems.at[at]) for at in range(count)
    ]
    for copy in copies:
        copy.start()
    for copy in copies:
        copy.wait()


def shards(
    residual,
    counts,
    source_index,
    source_partials,
    segment_index,
    attitude_partials,
    unit_index,
    knot_base,
    calib_partials,
    n_sky,
    n_tm,
):
    zones, capacity = residual.shape[2:]
    cap = -(-capacity // LANES) * LANES
    devices = n_sky * n_tm

    def flat(value):
        value = value.reshape(value.shape[:-4] + (zones, capacity))
        if cap != capacity:
            value = jnp.pad(value, [(0, 0)] * (value.ndim - 1) + [(0, cap - capacity)])
        return value

    vmem = pl.BlockSpec(memory_space=pltpu.VMEM)
    row = lambda *lead: pltpu.VMEM(lead + (1, cap), F32)
    dma = pltpu.SemaphoreType.DMA
    result_bytes = 4 * (zones * cap + 8 * SRC_DEV + 8 * SEG_DEV)
    pinned = cap == capacity
    result = pltpu.VMEM if pinned else jax.ShapeDtypeStruct
    corrected, src_params, att_params = pl.pallas_call(
        functools.partial(kernel, n_sky, n_tm),
        out_shape=(
            result((zones, cap), F32),
            result((SRC_PARAMS, SRC_DEV), F32),
            result((ATT_PARAMS, SEG_DEV), F32),
        ),
        in_specs=[pl.BlockSpec(memory_space=pltpu.HBM)] * 9,
        out_specs=(vmem, vmem, vmem),
        scratch_shapes=[
            pltpu.VMEM((zones, cap), F32),
            pltpu.SMEM((zones,), jnp.int32),
            pltpu.VMEM((zones, cap), jnp.int32),
            pltpu.VMEM((SRC_PARAMS, zones, cap), BF16),
            pltpu.VMEM((zones, cap), jnp.int32),
            pltpu.VMEM((ATT_PARAMS, zones, cap), BF16),
            pltpu.VMEM((zones, cap), jnp.int32),
            pltpu.VMEM((zones, cap), jnp.int32),
            pltpu.VMEM((SPLINE, zones, cap), BF16),
            dma((9,)),
            pltpu.VMEM((zones, SRC_DEV // 2, cap), BF16),
            pltpu.VMEM((zones, SEG_DEV // 2, cap), BF16),
            row(zones),
            row(zones),
            pltpu.VMEM((zones, 16, cap), BF16),
            pltpu.VMEM((zones, 16, cap), BF16),
            pltpu.VMEM((zones, 8, cap), F32),
            pltpu.VMEM((zones, 2 * UNIT_ROWS, cap), BF16),
            pltpu.VMEM((zones, EXTENT, cap), BF16),
            pltpu.VMEM((zones, EXTENT, cap), BF16),
            pltpu.VMEM((zones, EXTENT, cap), BF16),
            pltpu.VMEM((zones, 2 * RIM, cap), F32),
            pltpu.VMEM((zones, 2 * RIM, cap), F32),
            pltpu.VMEM((zones, rows_of(SRC_PARAMS), cap), F32),
            pltpu.VMEM((zones, rows_of(ATT_PARAMS), cap), F32),
            pltpu.VMEM((zones, 2 * ATT_PARAMS, cap), F32),
            pltpu.VMEM((zones, SPLINE, cap), F32),
            row(zones),
            row(zones),
            row(zones),
            row(zones),
            pltpu.VMEM((zones, 8, cap), F32),
            pltpu.VMEM((n_sky, 1, LANES), F32),
            pltpu.VMEM((devices, 1, LANES), F32),
            pltpu.VMEM((ITERS, 1, LANES), F32),
            pltpu.VMEM((ITERS, devices, 1, LANES), F32),
            row(ITERS, zones),
            row(ITERS, zones),
            row(ITERS, zones),
            row(ITERS, zones),
            pltpu.VMEM((ITERS, 2, 2, RIM, LANES), F32),
            pltpu.VMEM((ITERS, 2, 2, RIM, LANES), F32),
            dma((2,)),
            dma((ITERS, 2)),
            dma((ITERS,)),
            dma((ITERS, n_sky)),
            dma((ITERS,)),
            dma((ITERS,)),
            dma((ITERS, 2, 2)),
            dma((ITERS, 2, 2)),
        ],
        compiler_params=pltpu.CompilerParams(
            collective_id=0, has_side_effects=True, vmem_limit_bytes=67010000
        ),
        name="astrometry",
    )(
        flat(residual),
        counts.reshape(zones),
        flat(source_index),
        flat(source_partials),
        flat(segment_index),
        flat(attitude_partials),
        flat(unit_index),
        flat(knot_base),
        flat(calib_partials),
    )
    results = (corrected, src_params, att_params)
    if pinned:
        results = [pltpu.with_memory_space_constraint(value, pltpu.VMEM) for value in results]
    corrected, src_params, att_params = pl.pallas_call(
        functools.partial(write_out, len(results)),
        out_shape=tuple(jax.ShapeDtypeStruct(value.shape, value.dtype) for value in results),
        in_specs=[vmem] * len(results),
        out_specs=tuple(pl.BlockSpec(memory_space=pltpu.HBM) for _ in results),
        scratch_shapes=[dma((len(results),))],
        name="write_out",
    )(*results)
    return corrected[:, :capacity].reshape(1, 1, zones, capacity), src_params, att_params


def solution(mesh):
    return jax.shard_map(
        functools.partial(shards, n_sky=mesh.shape["sky"], n_tm=mesh.shape["tm"]),
        mesh=mesh,
        in_specs=(
            P("sky", "tm", None, None),
            P("sky", "tm", None),
            P("sky", "tm", None, None),
            P(None, "sky", "tm", None, None),
            P("sky", "tm", None, None),
            P(None, "sky", "tm", None, None),
            P("sky", "tm", None, None),
            P("sky", "tm", None, None),
            P(None, "sky", "tm", None, None),
        ),
        out_specs=(P("sky", "tm", None, None), P(None, ("sky", "tm")), P(None, ("sky", "tm"))),
        check_vma=False,
    )
```

```python
import functools

import jax
import jax.numpy as jnp
from jax import lax
from jax.experimental import pallas as pl
from jax.experimental.pallas import tpu as pltpu
from jax.sharding import PartitionSpec as P

SRC_DEV = 256
SEG_DEV = 128
KNOT_DEV = 113
UNITS = 62
SPLINE = 16
SRC_PARAMS = 5
ATT_PARAMS = 4
ITERS = 2

clip_factor = 1.5
ridge = 1.0

LANES = 128
F32 = jnp.float32
BF16 = jnp.bfloat16
MESH = pl.DeviceIdType.MESH
UNIT_ROWS = -(-UNITS // 64) * 64
EXTENT = -(-(KNOT_DEV + SPLINE - 1) // LANES) * LANES
RIM = SPLINE


def lower_pairs(order):
    return [(row_at, col_at) for row_at in range(order) for col_at in range(row_at + 1)]


def rows_of(order):
    return -(-(order + len(lower_pairs(order))) // 8) * 8


def split_rows(value):
    high = value.astype(BF16).astype(F32)
    return jnp.concatenate([high, value - high], axis=0).astype(BF16)


def dot_nt(left, right):
    return lax.dot_general(left, right, (((1,), (1,)), ((), ())), preferred_element_type=F32)


def dot_nn(left, right):
    return lax.dot_general(left, right, (((1,), (0,)), ((), ())), preferred_element_type=F32)


def in_groups(count, size, body, carry, first=None):
    if count <= 16:
        start = 0
        while start < count:
            end = min(start + (first if first and not start else size), count)
            carry = body(list(range(start, end)), carry)
            start = end
        return carry
    size = size if count % size == 0 else 1

    def group(number, carry):
        return body([number * size + at for at in range(size)], carry)

    return lax.fori_loop(0, count // size, group, carry)


def in_turns(totals, values):
    totals = list(totals)
    for number, value in enumerate(values):
        totals[number % 2] = totals[number % 2] + value
    return tuple(totals)


def add_all(values):
    values = list(values)
    while len(values) > 1:
        values = [
            values[at] + values[at + 1] if at + 1 < len(values) else values[at]
            for at in range(0, len(values), 2)
        ]
    return values[0]


def each(count, body, carry):
    if count <= 16:
        for number in range(count):
            carry = body(number, carry)
        return carry
    return lax.fori_loop(0, count, body, carry)


def block_solve(sums, order):
    pairs = lower_pairs(order)
    matrix = {}
    for number, (row_at, col_at) in enumerate(pairs):
        at = order + number
        matrix[row_at, col_at] = sums[at : at + 1] + (ridge if row_at == col_at else 0.0)
    right = [sums[at : at + 1] for at in range(order)]
    inverse = []
    for pivot in range(order):
        inverse.append(1.0 / matrix[pivot, pivot])
        for row_at in range(pivot + 1, order):
            ratio = matrix[row_at, pivot] * inverse[pivot]
            for col_at in range(pivot + 1, row_at + 1):
                matrix[row_at, col_at] = matrix[row_at, col_at] - ratio * matrix[col_at, pivot]
            right[row_at] = right[row_at] - ratio * right[pivot]
    solved = [None] * order
    for row_at in reversed(range(order)):
        running = right[row_at]
        for inner_at in range(row_at + 1, order):
            running = running - matrix[inner_at, row_at] * solved[inner_at]
        solved[row_at] = running * inverse[row_at]
    return jnp.concatenate(solved, axis=0)


def store_products(partials_ref, prods, order):
    values = [partials_ref[at].astype(F32) for at in range(order)]
    listed = values + [values[row_at] * values[col_at] for row_at, col_at in lower_pairs(order)]
    while len(listed) < prods.shape[1]:
        listed.append(jnp.zeros_like(values[0]))
    for at, value in enumerate(listed):
        prods[:, at, :] = value


def kernel(
    n_sky,
    n_tm,
    res_hbm,
    cnt_hbm,
    src_hbm,
    sp_hbm,
    seg_hbm,
    ap_hbm,
    unit_hbm,
    base_hbm,
    cp_hbm,
    out_ref,
    srcp_ref,
    attp_ref,
    res_ref,
    cnt_ref,
    src_ref,
    sp_ref,
    seg_ref,
    ap_ref,
    unit_ref,
    base_ref,
    cp_ref,
    in_sems,
    src_hot,
    seg_hot,
    src_side,
    seg_side,
    src_mask,
    seg_mask,
    src_lead,
    unit_hot,
    placed,
    sq_high,
    sq_low,
    rim_part,
    rim_square,
    src_prods,
    att_prods,
    att_twice,
    cal_rows,
    r_src,
    r_time,
    v_time,
    live_time,
    fit_time,
    stat_send,
    stat_recv,
    abs_send,
    abs_recv,
    fwd_send,
    fwd_recv,
    back_send,
    back_recv,
    rim_send,
    rim_recv,
    stat_sems,
    abs_sems,
    fwd_ssem,
    fwd_rsem,
    back_ssem,
    back_rsem,
    rim_ssem,
    rim_rsem,
):
    zones, cap = res_ref.shape
    tiles = cap // LANES
    devices = n_sky * n_tm
    sky = lax.axis_index("sky")
    tm = lax.axis_index("tm")
    me = sky * n_tm + tm

    def wrapped(value, size):
        return jnp.where(value >= size, value - size, value)

    lower = sky < n_sky // 2

    def far_first(number):
        down = n_sky - 1 - number
        down = jnp.where(down <= sky, down - 1, down)
        up = jnp.where(number >= sky, number + 1, number)
        peer = jnp.where(lower, down, up)
        if isinstance(number, int):
            return sky if number == n_sky - 1 else peer
        return jnp.where(number == n_sky - 1, sky, peer)

    def every_other(body, after=None):
        if devices <= 64:
            if n_tm & (n_tm - 1):
                tms = [wrapped(tm + at, n_tm) for at in range(n_tm)]
            else:
                tms = [tm ^ at for at in range(n_tm)]
            for number in range(n_sky):
                other = far_first(number)
                for at in reversed(range(n_tm)):
                    if number < n_sky - 1 or at:
                        body(other, tms[at])
                if after and number < n_sky - 1:
                    after(other)
            return

        @pl.loop(1, devices)
        def _(step):
            flat = lax.rem(me + step, devices)
            body(flat // n_tm, lax.rem(flat, n_tm))

        if after:
            each(n_sky - 1, lambda number, carry: (after(far_first(number)), carry)[1], 0)

    arriving = [
        pltpu.make_async_copy(source, target, in_sems.at[number])
        for number, (source, target) in enumerate(
            (
                (res_hbm, res_ref),
                (cnt_hbm, cnt_ref),
                (src_hbm, src_ref),
                (sp_hbm, sp_ref),
                (seg_hbm, seg_ref),
                (ap_hbm, ap_ref),
                (unit_hbm, unit_ref),
                (base_hbm, base_ref),
                (cp_hbm, cp_ref),
            )
        )
    ]
    for copy in arriving:
        copy.start()

    barrier = pltpu.get_barrier_semaphore()

    def greet(to_sky, to_tm):
        pl.semaphore_signal(
            barrier, inc=1, device_id={"sky": to_sky, "tm": to_tm}, device_id_type=MESH
        )

    every_other(greet)

    lane_row = lax.broadcasted_iota(jnp.int32, (1, cap), 1)

    def fold(row):
        total = row[:, :LANES]
        for at in range(1, tiles):
            total = total + row[:, at * LANES : (at + 1) * LANES]
        return total

    def live_of(zone):
        return (lane_row < cnt_ref[zone]).astype(F32)

    for copy in arriving[:2]:
        copy.wait()

    def first_stats(zone, carry):
        sums, lives = carry
        row = res_ref[pl.ds(zone, 1), :] * live_of(zone)
        r_src[zone] = row
        return sums + fold(jnp.abs(row)), lives + cnt_ref[zone]

    zero_row = jnp.zeros((1, LANES), F32)
    lane = lax.broadcasted_iota(jnp.int32, (1, LANES), 1)
    count_lane, live_lane = LANES - 1, LANES - 2
    sums, lives = each(zones, first_stats, (zero_row, jnp.int32(0)))
    sums = sums + jnp.where(lane < 2, pltpu.roll(sums, 2, 1), 0.0)
    sums = jnp.where(lane == live_lane, jnp.full((1, LANES), lives, jnp.int32).astype(F32), sums)

    def put_stats(zone, carry):
        count = jnp.full((1, LANES), cnt_ref[zone], jnp.int32).astype(F32)
        stat_send[zone] = jnp.where(lane == count_lane, count, sums)
        return carry

    each(zones, put_stats, 0)
    stat_recv[me] = stat_send[sky]
    for copy in arriving[2:]:
        copy.wait()

    store_products(sp_ref, src_prods, SRC_PARAMS)
    store_products(ap_ref, att_prods, ATT_PARAMS)
    for at in range(2 * ATT_PARAMS):
        att_twice[:, at, :] = ap_ref[at % ATT_PARAMS].astype(F32)
    for at in range(SPLINE):
        cal_rows[:, at, :] = cp_ref[at].astype(F32)

    def hot_rows(rows, labels):
        number = lax.broadcasted_iota(jnp.int32, (rows, cap), 0)
        return jnp.where(number == labels, 1.0, 0.0).astype(BF16)

    def tables(zone, carry):
        for labels_ref, hot_ref, side_ref, mask_ref in (
            (src_ref, src_hot, src_side, src_mask),
            (seg_ref, seg_hot, seg_side, seg_mask),
        ):
            labels = labels_ref[pl.ds(zone, 1), :]
            groups = hot_ref.shape[1]
            above = labels >= groups
            hot_ref[zone] = hot_rows(groups, jnp.where(above, labels - groups, labels))
            side = jnp.where(above, 1.0, 0.0)
            side_ref[zone] = side
            mask_ref[zone] = jnp.broadcast_to(side, (16, cap)).astype(BF16)
        hot = hot_rows(UNIT_ROWS, unit_ref[pl.ds(zone, 1), :])
        unit_hot[zone] = jnp.concatenate([hot, hot], axis=0)
        base = jnp.broadcast_to(base_ref[pl.ds(zone, 1), :], (8, cap))
        turned = []
        for part in range(SPLINE // 8):
            rows = cal_rows[zone, part * 8 : part * 8 + 8, :]
            for bit in (1, 2, 4):
                rows = jnp.where((base & bit) != 0, pltpu.roll(rows, bit, 0), rows)
            turned.append(rows)
        reach = lax.shift_right_arithmetic(
            lax.broadcasted_iota(jnp.int32, (8, cap), 0) - base, jnp.int32(3)
        )
        pieces = []
        for group in range(EXTENT // 8):
            piece = jnp.zeros((8, cap), F32)
            for part, rows in enumerate(turned):
                piece = jnp.where(reach == part - group, rows, piece)
            pieces.append(piece)
        spread = jnp.concatenate(pieces, axis=0)
        placed[zone] = spread.astype(BF16)
        square = spread * spread
        rim_part[zone] = jnp.concatenate([spread[:RIM], spread[EXTENT - RIM :]], axis=0)
        rim_square[zone] = jnp.concatenate([square[:RIM], square[EXTENT - RIM :]], axis=0)
        high = square.astype(BF16)
        sq_high[zone] = high
        sq_low[zone] = (square - high.astype(F32)).astype(BF16)
        return carry


    def lead_rows(zone, prods, order, row):
        number = lax.broadcasted_iota(jnp.int32, (8, cap), 0)
        return prods[zone, :8, :] * jnp.where(number < order, row, 1.0)

    def src_ready(zone, carry):
        src_lead[zone] = lead_rows(zone, src_prods, SRC_PARAMS, r_src[zone])
        return carry

    each(zones, src_ready, 0)

    steps_off = n_sky + n_tm - 2 - sky - tm
    early = jnp.minimum(steps_off, zones) if zones <= 16 else 0
    lax.fori_loop(0, early, tables, 0)
    pl.semaphore_wait(barrier, devices - 1)

    def send_stats(to_sky, to_tm):
        pltpu.make_async_remote_copy(
            src_ref=stat_send.at[to_sky],
            dst_ref=stat_recv.at[me],
            send_sem=stat_sems.at[0],
            recv_sem=stat_sems.at[1],
            device_id={"sky": to_sky, "tm": to_tm},
            device_id_type=MESH,
        ).start()

    every_other(send_stats)

    lax.fori_loop(early, zones, tables, 0)

    whole_stat = stat_recv.at[pl.ds(0, devices - 1)]
    pltpu.make_async_copy(whole_stat, whole_stat, stat_sems.at[1]).wait()
    stats = jnp.sum(stat_recv[...], axis=0)
    live_total = jnp.sum(jnp.where(lane == live_lane, stats, 0.0), axis=1, keepdims=True)
    abs_total = jnp.sum(jnp.where(lane < live_lane, stats, 0.0), axis=1, keepdims=True)

    def time_live(zone, carry):
        held = stat_recv[zone * n_tm + tm]
        count = jnp.sum(jnp.where(lane == count_lane, held, 0.0), axis=1, keepdims=True)
        live_time[zone] = (lane_row.astype(F32) < count).astype(F32)
        return carry

    src_total = jnp.zeros((SRC_PARAMS, SRC_DEV), F32)
    att_total = jnp.zeros((ATT_PARAMS, SEG_DEV), F32)

    chunk = min(cap, 256) if cap % 256 == 0 else cap
    parts = [slice(at, at + chunk) for at in range(0, cap, chunk)]

    def group_sums(zone, lead, prods, hot, mask, weights):
        tall = split_rows(jnp.concatenate([lead * weights, prods[zone, 8:, :] * weights], axis=0))
        above = jnp.concatenate(
            [tall[at : at + 16] * mask[zone] for at in range(0, tall.shape[0], 16)], axis=0
        )
        return dot_nt(jnp.concatenate([tall - above, above], axis=0), hot[zone])

    def group_totals(both, order):
        rows = both[0].shape[0] // 4
        halves = []
        for at in (0, 2 * rows):
            low, high = slice(at, at + rows), slice(at + rows, at + 2 * rows)
            halves.append((both[0][low] + both[0][high]) + (both[1][low] + both[1][high]))
        return jnp.concatenate(halves, axis=1)

    def padded_steps(step, order):
        groups = step.shape[1]
        tall = split_rows(jnp.concatenate([step, jnp.zeros((8 - order, groups), F32)], axis=0))
        return jnp.concatenate([tall[:, : groups // 2], tall[:, groups // 2 :]], axis=0)

    def att_steps(step):
        high = step.astype(BF16).astype(F32)
        tall = jnp.concatenate([high, step - high], axis=0)
        groups = step.shape[1] // 2
        return jnp.concatenate([tall[:, :groups], tall[:, groups:]], axis=0).astype(BF16)

    def att_fitted(zones_at, steps):
        picked = [[dot_nn(steps, seg_hot[zone, :, part]) for part in parts] for zone in zones_at]
        fits = []
        for zone, values_of in zip(zones_at, picked):
            fit = []
            for part, values in zip(parts, values_of):
                values = jnp.where(seg_side[zone, :, part] > 0.5, values[8:], values[:8])
                fit.append(jnp.sum(values * att_twice[zone, :, part], axis=0, keepdims=True))
            fits.append(jnp.concatenate(fit, axis=1) if len(fit) > 1 else fit[0])
        return fits

    def fitted(zones_at, steps, prods, hot, side):
        picked = [[dot_nn(steps, hot[zone, :, part]) for part in parts] for zone in zones_at]
        fits = []
        for zone, values_of in zip(zones_at, picked):
            fit = []
            for part, values in zip(parts, values_of):
                values = jnp.where(
                    side[zone, :, part] > 0.5, values[16:24] + values[24:], values[:8] + values[8:16]
                )
                fit.append(jnp.sum(values * prods[zone, :8, part], axis=0, keepdims=True))
            fits.append(jnp.concatenate(fit, axis=1) if len(fit) > 1 else fit[0])
        return fits

    def zone_copy(send, recv, ssem, rsem, peer):
        return pltpu.make_async_remote_copy(
            src_ref=send.at[peer],
            dst_ref=recv.at[sky],
            send_sem=ssem,
            recv_sem=rsem,
            device_id={"sky": peer, "tm": tm},
            device_id_type=MESH,
        )

    def rim_copy(it, way, kind):
        return pltpu.make_async_remote_copy(
            src_ref=rim_send.at[it, way, kind],
            dst_ref=rim_recv.at[it, way, kind],
            send_sem=rim_ssem.at[it, way, kind],
            recv_sem=rim_rsem.at[it, way, kind],
            device_id={"sky": sky, "tm": lax.rem(tm + (1, n_tm - 1)[way], n_tm)},
            device_id_type=MESH,
        )

    has_next, has_last = tm < n_tm - 1, tm > 0

    def to_rims(it, kind, act):
        for way, there in ((0, has_next), (1, has_last)):

            @pl.when(there)
            def _():
                act(rim_copy(it, way, kind))

    def from_rims(it, kind):
        for way, there in ((0, has_last), (1, has_next)):

            @pl.when(there)
            def _():
                rim_copy(it, way, kind).wait_recv()

    def send_rims(it, kind, rims):
        for way, rows in ((0, slice(RIM, 2 * RIM)), (1, slice(0, RIM))):
            rim_send[it, way, kind, :, :UNIT_ROWS] = rims[rows]
        to_rims(it, kind, lambda copy: copy.start())

    wide = 2 * UNIT_ROWS

    def unit_weights(zone, row):
        high = row.astype(BF16).astype(F32)
        tall = jnp.concatenate(
            [
                jnp.broadcast_to(high, (UNIT_ROWS, cap)),
                jnp.broadcast_to(row - high, (UNIT_ROWS, cap)),
            ],
            axis=0,
        ).astype(BF16)
        return unit_hot[zone] * tall

    for it in range(ITERS):
        bound = clip_factor * (abs_total / live_total)

        def src_sums(numbers, total):
            rows = [r_src[zone] for zone in numbers]
            weights = [
                live_of(zone) * bound / jnp.maximum(jnp.abs(row), bound)
                for zone, row in zip(numbers, rows)
            ]
            return in_turns(
                total,
                (group_sums(zone, src_lead[zone], src_prods, src_hot, src_mask, weight)
                for zone, weight in zip(numbers, weights)),
            )

        blank = jnp.zeros((4 * rows_of(SRC_PARAMS), SRC_DEV // 2), F32)
        both = in_groups(zones, 8, src_sums, (blank, blank))
        step_x = block_solve(group_totals(both, SRC_PARAMS), SRC_PARAMS)
        src_total = src_total + step_x
        steps_x = padded_steps(step_x, SRC_PARAMS)

        def src_out(numbers, carry):
            zones_at = [far_first(number) for number in numbers]
            fits = fitted(zones_at, steps_x, src_prods, src_hot, src_side)
            for zone, fit in zip(zones_at, fits):
                fwd_send[it, zone] = r_src[zone] - live_of(zone) * fit

            for number, zone in zip(numbers, zones_at):

                def send():
                    zone_copy(
                        fwd_send.at[it], fwd_recv.at[it], fwd_ssem.at[it], fwd_rsem.at[it, sky], zone
                    ).start()

                if isinstance(number, int):
                    if number < n_sky - 1:
                        send()
                else:
                    pl.when(number < n_sky - 1)(send)
            return carry

        in_groups(zones, 6, src_out, 0, first=2)
        fwd_recv[it, sky] = fwd_send[it, sky]
        if it == 0:
            each(zones, time_live, 0)

        def att_sums(numbers, total):
            zones_at = [far_first(n_sky - 1 - number) for number in numbers]
            for number, zone in zip(numbers, zones_at):

                def arrive():
                    zone_copy(
                        fwd_send.at[it], fwd_recv.at[it], fwd_ssem.at[it], fwd_rsem.at[it, zone], zone
                    ).wait_recv()

                if isinstance(number, int):
                    if number > 0:
                        arrive()
                else:
                    pl.when(number > 0)(arrive)
            rows = [fwd_recv[it, zone] for zone in zones_at]
            weights = [
                live_time[zone] * bound / jnp.maximum(jnp.abs(row), bound)
                for zone, row in zip(zones_at, rows)
            ]
            for zone, weight in zip(zones_at, weights):
                v_time[zone] = weight
            att_part, h_part = total
            att_part = in_turns(
                att_part,
                (
                    group_sums(
                        zone, lead_rows(zone, att_prods, ATT_PARAMS, row), att_prods, seg_hot, seg_mask, weight
                    )
                    for zone, weight, row in zip(zones_at, weights, rows)
                ),
            )
            h_part = in_turns(
                h_part,
                (
                    dot_nt(split_rows(rim_square[zone] * weight), unit_hot[zone, :UNIT_ROWS, :])
                    for zone, weight in zip(zones_at, weights)
                ),
            )
            return att_part, h_part

        rim_blank = (jnp.zeros((4 * RIM, UNIT_ROWS), F32),) * 2
        blank = jnp.zeros((4 * rows_of(ATT_PARAMS), SEG_DEV // 2), F32)
        both, h_rims = in_groups(zones, 2, att_sums, ((blank, blank), rim_blank))

        def rim_total(sums):
            return add_all(half[at : at + 2 * RIM] for half in sums for at in (0, 2 * RIM))

        h_rims = rim_total(h_rims)
        step_y = block_solve(group_totals(both, ATT_PARAMS), ATT_PARAMS)
        att_total = att_total + step_y
        steps_y = att_steps(step_y)

        send_rims(it, 1, h_rims)

        def rim_sums(numbers, total):
            fits = att_fitted(numbers, steps_y)
            rows = [
                fwd_recv[it, zone] - live_time[zone] * fit for zone, fit in zip(numbers, fits)
            ]
            for zone, row in zip(numbers, rows):
                r_time[zone] = row
            return in_turns(
                total,
                (
                    dot_nt(split_rows(rim_part[zone] * (v_time[zone] * row)), unit_hot[zone, :UNIT_ROWS, :])
                    for zone, row in zip(numbers, rows)
                ),
            )

        g_rims = in_groups(zones, 8, rim_sums, rim_blank)
        g_rims = rim_total(g_rims)

        def joined(g_part, h_part):
            g_part = g_part + pltpu.roll(g_part, UNIT_ROWS, 1)
            left_half = lax.broadcasted_iota(jnp.int32, g_part.shape, 1) < UNIT_ROWS
            return jnp.where(left_half, g_part, h_part)

        def coefs_of(knots):
            ratio = knots / (pltpu.roll(knots, UNIT_ROWS, 1) + ridge)
            left_half = lax.broadcasted_iota(jnp.int32, knots.shape, 1) < UNIT_ROWS
            ratio = jnp.where(left_half, ratio, 0.0)
            high = ratio.astype(BF16).astype(F32)
            return (high + pltpu.roll(ratio - high, UNIT_ROWS, 1)).astype(BF16)

        send_rims(it, 0, g_rims)
        inner = slice(RIM, EXTENT - RIM)

        def inner_sums(numbers, total):
            g_part, h_part = total
            for zone in numbers:
                weight = v_time[zone]
                tall = unit_weights(zone, weight)
                h_part = h_part + dot_nt(sq_high[zone, inner, :], tall) + dot_nt(sq_low[zone, inner, :], tall)
                g_part = g_part + dot_nt(placed[zone, inner, :], unit_weights(zone, weight * r_time[zone]))
            return g_part, h_part

        middle = jnp.zeros((EXTENT - 2 * RIM, wide), F32)
        middle, h_total = in_groups(zones, 8, inner_sums, (middle, middle))
        h_total = h_total + pltpu.roll(h_total, UNIT_ROWS, 1)
        inner_coefs = coefs_of(joined(middle, h_total))

        def inner_fit(zone, carry):
            picked = dot_nn(inner_coefs, unit_hot[zone])
            fit = picked * placed[zone, inner, :].astype(F32)
            fit_time[zone] = jnp.sum(fit.reshape(-1, 8, cap), axis=0)
            return carry

        each(zones, inner_fit, 0)

        for kind in (1, 0):
            from_rims(it, kind)
        lead = KNOT_DEV - (EXTENT - RIM)
        shared = SPLINE - 1
        from_last = jnp.where(tm > 0, rim_recv[it, 0], 0.0)[:, lead : lead + shared, :UNIT_ROWS]
        from_next = jnp.where(tm < n_tm - 1, rim_recv[it, 1], 0.0)[:, :shared, :UNIT_ROWS]

        def added(rims, at):
            blank = lambda rows: [jnp.zeros((rows, UNIT_ROWS), F32)] if rows else []
            return rims + jnp.concatenate(
                [from_last[at]]
                + blank(RIM - shared + lead)
                + [from_next[at]]
                + blank(RIM - lead - shared),
                axis=0,
            )

        rim_coefs = split_rows(added(g_rims, 0) / (added(h_rims, 1) + ridge))

        last = it == ITERS - 1

        def back_out(peer):
            zone_copy(
                back_send.at[it], back_recv.at[it], back_ssem.at[it], back_rsem.at[it], peer
            ).start()

        def cal_out(numbers, total):
            zones_at = [far_first(number) for number in numbers] if last else numbers
            picked = [dot_nn(rim_coefs, unit_hot[zone, :UNIT_ROWS, :]) for zone in zones_at]
            rows = []
            for zone, values in zip(zones_at, picked):
                fit = (values[: 2 * RIM] + values[2 * RIM :]) * rim_part[zone]
                fit = jnp.sum(fit.reshape(-1, 8, cap), axis=0) + fit_time[zone]
                fit = jnp.sum(fit, axis=0, keepdims=True)
                rows.append(r_time[zone] - live_time[zone] * fit)
            for zone, row in zip(zones_at, rows):
                back_send[it, zone] = row
            if not last:
                return total + add_all(fold(jnp.abs(row)) for row in rows)
            for number, zone in zip(numbers, zones_at):
                if isinstance(number, int):
                    if number < n_sky - 1:
                        back_out(zone)
                else:
                    pl.when(number < n_sky - 1)(functools.partial(back_out, zone))
            return total

        if last:
            in_groups(zones, 6, cal_out, zero_row, first=2)
            srcp_ref[...] = src_total
            attp_ref[...] = att_total
        else:
            abs_sum = in_groups(zones, 8, cal_out, zero_row)
            abs_send[it] = abs_sum
            abs_recv[it, me] = abs_sum

            def send_abs(to_sky, to_tm):
                pltpu.make_async_remote_copy(
                    src_ref=abs_send.at[it],
                    dst_ref=abs_recv.at[it, me],
                    send_sem=abs_sems.at[it, 0],
                    recv_sem=abs_sems.at[it, 1],
                    device_id={"sky": to_sky, "tm": to_tm},
                    device_id_type=MESH,
                ).start()

            every_other(send_abs)
            each(n_sky - 1, lambda number, carry: (back_out(far_first(number)), carry)[1], 0)

        back_recv[it, sky] = back_send[it, sky]

        whole = back_recv.at[it, pl.ds(0, n_sky - 1)]
        pltpu.make_async_copy(whole, whole, back_rsem.at[it]).wait()

        def put_back(zone, carry):
            if last:
                out_ref[pl.ds(zone, 1), :] = back_recv[it, zone]
            else:
                r_src[zone] = back_recv[it, zone]
            return carry

        each(zones, put_back, 0)

        if not last:
            each(zones, src_ready, 0)
            whole = abs_recv.at[it, pl.ds(0, devices - 1)]
            pltpu.make_async_copy(whole, whole, abs_sems.at[it, 1]).wait()
            abs_total = jnp.sum(jnp.sum(abs_recv[it], axis=0), axis=1, keepdims=True)

    pltpu.make_async_copy(whole_stat, whole_stat, stat_sems.at[0]).wait()
    for it in range(ITERS):
        if it < ITERS - 1:
            whole = abs_recv.at[it, pl.ds(0, devices - 1)]
            pltpu.make_async_copy(whole, whole, abs_sems.at[it, 0]).wait()

        for recv, ssem in ((fwd_recv, fwd_ssem), (back_recv, back_ssem)):
            whole = recv.at[it, pl.ds(0, n_sky - 1)]
            pltpu.make_async_copy(whole, whole, ssem.at[it]).wait()
        for kind in (1, 0):
            to_rims(it, kind, lambda copy: copy.wait_send())


def write_out(count, *refs):
    sems = refs[-1]
    copies = [
        pltpu.make_async_copy(refs[at], refs[count + at], sems.at[at]) for at in range(count)
    ]
    for copy in copies:
        copy.start()
    for copy in copies:
        copy.wait()


def shards(
    residual,
    counts,
    source_index,
    source_partials,
    segment_index,
    attitude_partials,
    unit_index,
    knot_base,
    calib_partials,
    n_sky,
    n_tm,
):
    zones, capacity = residual.shape[2:]
    cap = -(-capacity // LANES) * LANES
    devices = n_sky * n_tm

    def flat(value):
        value = value.reshape(value.shape[:-4] + (zones, capacity))
        if cap != capacity:
            value = jnp.pad(value, [(0, 0)] * (value.ndim - 1) + [(0, cap - capacity)])
        return value

    vmem = pl.BlockSpec(memory_space=pltpu.VMEM)
    row = lambda *lead: pltpu.VMEM(lead + (1, cap), F32)
    dma = pltpu.SemaphoreType.DMA
    result_bytes = 4 * (zones * cap + 8 * SRC_DEV + 8 * SEG_DEV)
    pinned = cap == capacity
    result = pltpu.VMEM if pinned else jax.ShapeDtypeStruct
    corrected, src_params, att_params = pl.pallas_call(
        functools.partial(kernel, n_sky, n_tm),
        out_shape=(
            result((zones, cap), F32),
            result((SRC_PARAMS, SRC_DEV), F32),
            result((ATT_PARAMS, SEG_DEV), F32),
        ),
        in_specs=[pl.BlockSpec(memory_space=pltpu.HBM)] * 9,
        out_specs=(vmem, vmem, vmem),
        scratch_shapes=[
            pltpu.VMEM((zones, cap), F32),
            pltpu.SMEM((zones,), jnp.int32),
            pltpu.VMEM((zones, cap), jnp.int32),
            pltpu.VMEM((SRC_PARAMS, zones, cap), BF16),
            pltpu.VMEM((zones, cap), jnp.int32),
            pltpu.VMEM((ATT_PARAMS, zones, cap), BF16),
            pltpu.VMEM((zones, cap), jnp.int32),
            pltpu.VMEM((zones, cap), jnp.int32),
            pltpu.VMEM((SPLINE, zones, cap), BF16),
            dma((9,)),
            pltpu.VMEM((zones, SRC_DEV // 2, cap), BF16),
            pltpu.VMEM((zones, SEG_DEV // 2, cap), BF16),
            row(zones),
            row(zones),
            pltpu.VMEM((zones, 16, cap), BF16),
            pltpu.VMEM((zones, 16, cap), BF16),
            pltpu.VMEM((zones, 8, cap), F32),
            pltpu.VMEM((zones, 2 * UNIT_ROWS, cap), BF16),
            pltpu.VMEM((zones, EXTENT, cap), BF16),
            pltpu.VMEM((zones, EXTENT, cap), BF16),
            pltpu.VMEM((zones, EXTENT, cap), BF16),
            pltpu.VMEM((zones, 2 * RIM, cap), F32),
            pltpu.VMEM((zones, 2 * RIM, cap), F32),
            pltpu.VMEM((zones, rows_of(SRC_PARAMS), cap), F32),
            pltpu.VMEM((zones, rows_of(ATT_PARAMS), cap), F32),
            pltpu.VMEM((zones, 2 * ATT_PARAMS, cap), F32),
            pltpu.VMEM((zones, SPLINE, cap), F32),
            row(zones),
            row(zones),
            row(zones),
            row(zones),
            pltpu.VMEM((zones, 8, cap), F32),
            pltpu.VMEM((n_sky, 1, LANES), F32),
            pltpu.VMEM((devices, 1, LANES), F32),
            pltpu.VMEM((ITERS, 1, LANES), F32),
            pltpu.VMEM((ITERS, devices, 1, LANES), F32),
            row(ITERS, zones),
            row(ITERS, zones),
            row(ITERS, zones),
            row(ITERS, zones),
            pltpu.VMEM((ITERS, 2, 2, RIM, LANES), F32),
            pltpu.VMEM((ITERS, 2, 2, RIM, LANES), F32),
            dma((2,)),
            dma((ITERS, 2)),
            dma((ITERS,)),
            dma((ITERS, n_sky)),
            dma((ITERS,)),
            dma((ITERS,)),
            dma((ITERS, 2, 2)),
            dma((ITERS, 2, 2)),
        ],
        compiler_params=pltpu.CompilerParams(
            collective_id=0, has_side_effects=True, vmem_limit_bytes=67010000
        ),
        name="astrometry",
    )(
        flat(residual),
        counts.reshape(zones),
        flat(source_index),
        flat(source_partials),
        flat(segment_index),
        flat(attitude_partials),
        flat(unit_index),
        flat(knot_base),
        flat(calib_partials),
    )
    results = (corrected, src_params, att_params)
    if pinned:
        results = [pltpu.with_memory_space_constraint(value, pltpu.VMEM) for value in results]
    corrected, src_params, att_params = pl.pallas_call(
        functools.partial(write_out, len(results)),
        out_shape=tuple(jax.ShapeDtypeStruct(value.shape, value.dtype) for value in results),
        in_specs=[vmem] * len(results),
        out_specs=tuple(pl.BlockSpec(memory_space=pltpu.HBM) for _ in results),
        scratch_shapes=[dma((len(results),))],
        name="write_out",
    )(*results)
    return corrected[:, :capacity].reshape(1, 1, zones, capacity), src_params, att_params


def solution(mesh):
    return jax.shard_map(
        functools.partial(shards, n_sky=mesh.shape["sky"], n_tm=mesh.shape["tm"]),
        mesh=mesh,
        in_specs=(
            P("sky", "tm", None, None),
            P("sky", "tm", None),
            P("sky", "tm", None, None),
            P(None, "sky", "tm", None, None),
            P("sky", "tm", None, None),
            P(None, "sky", "tm", None, None),
            P("sky", "tm", None, None),
            P("sky", "tm", None, None),
            P(None, "sky", "tm", None, None),
        ),
        out_specs=(P("sky", "tm", None, None), P(None, ("sky", "tm")), P(None, ("sky", "tm"))),
        check_vma=False,
    )
```
